512 devices in a mesh: ctx: 32 (over x_hi, y, core), batch: 16 (over z, x_lo).
Axes of the slice: x: 4 (x_hi: 2, x_lo: 2; x = x_hi * 2 + x_lo), y: 8, z: 8, core: 2. Of those that a mesh axis runs over, the one named last changes fastest.
Arguments:
- seq_in: bfloat16 [16, 4096, 512], P('batch', 'ctx'), may hold values from -6 to 6
- w_in: bfloat16 [512, 2048], replicated, may hold values from -0.25 to 0.25
- w_out: bfloat16 [512, 512], replicated, may hold values from -0.25 to 0.25
- pos_emb: bfloat16 [16, 4096, 512], P('batch', 'ctx'), may hold values from -0.29882812 to 0.29882812
- pos_ids: int32 [16, 4096], P('batch', 'ctx'), may hold values from 0 to 3999999, as said below
- neg_emb: bfloat16 [128, 512], P('batch'), may hold values from -0.29882812 to 0.29882812
- neg_ids: int32 [128], P('batch'), may hold values from 0 to 3999999
- neg_counts: int32 [128], P('batch'), may hold values from 1000 to 99999
Outputs:
- loss: float32 [16, 4096], P('batch', 'ctx')
- d_seq: bfloat16 [16, 4096, 512], P('batch', 'ctx')
- d_neg: float32 [128, 512], P('batch')
The draws below stay inside these ranges and needn't reach their ends.
Inputs may be any that keep to these rules, and one draw needn't show every extreme that they name: `pos_ids`: item ids; many positions name the item of one of the sampled negatives.
All inputs are finite; a program needn't handle non-finite values.
Results may differ from the reference program's by a relative error of at most 0.008.
Values may be sent and summed in bfloat16 or wider, within the bound.
A program may use at most 128 MiB of HBM per device.

```python
import math
import jax
import jax.numpy as jnp
from jax import lax

HEADS = 8
HEAD = 64
D = 512
SEQ_LEN = 4096
HISTORIES = 16
NEG = 128
ITEMS = 4000000


def item_pair(key):
    base = jax.random.fold_in(key, 7)
    negatives = jax.random.randint(jax.random.fold_in(base, 1), (NEG,), 0, ITEMS, dtype=jnp.int32)
    picked = jax.random.randint(jax.random.fold_in(base, 2), (HISTORIES, SEQ_LEN), 0, NEG, dtype=jnp.int32)
    fresh = jax.random.randint(jax.random.fold_in(base, 3), (HISTORIES, SEQ_LEN), 0, ITEMS, dtype=jnp.int32)
    coins = jax.random.randint(jax.random.fold_in(base, 4), (HISTORIES, SEQ_LEN), 0, 2, dtype=jnp.int32)
    positives = jnp.where(coins == 0, negatives[picked], fresh)
    return (negatives, positives)


def draw_neg_ids(key, part):
    return item_pair(key)[0]


def draw_pos_ids(key, part):
    return item_pair(key)[1]


def touch_ends(result, rng, least, largest):
    place = [jax.random.randint(jax.random.fold_in(rng, axis), (), 0, length) for axis, length in enumerate(result.shape)]
    widest = result.shape.index(max(result.shape))
    neighbour = place[:widest] + [(place[widest] + 1) % result.shape[widest]] + place[widest + 1:]
    return result.at[tuple(place)].set(least).at[tuple(neighbour)].set(largest)


def shard_levels(stream_key, dims, cuts, smallest, largest):
    gain, own = 1.0, jax.random.fold_in(stream_key, 6)
    for dim, parts in cuts:
        draws = jnp.exp(jax.random.uniform(jax.random.fold_in(own, dim), (parts,), jnp.float32, smallest / len(cuts), largest / len(cuts)))
        gain = gain * jnp.repeat(draws, dims[dim] // parts).reshape([-1 if axis == dim else 1 for axis in range(len(dims))])
    return gain


def gaussian(rng, extent, scale, bound, pieces=(), held_as=jnp.bfloat16):
    entries = scale * jax.random.normal(rng, extent, jnp.float32)
    if pieces:
        entries = entries * shard_levels(rng, extent, pieces, -0.22, 0.18)
    return jnp.clip(entries, -bound, bound).astype(held_as)


def setup_inputs(seed: int = 0) -> dict:
    arg_keys = jax.random.split(jax.random.key(seed), 9)
    return {
        "seq_in": gaussian(arg_keys[0], (HISTORIES, SEQ_LEN, D), 1.0, 6.0, ((0, 16), (1, 32))),
        "w_in": gaussian(arg_keys[1], (D, 4 * D), D ** -0.5, 0.25),
        "w_out": gaussian(arg_keys[2], (D, D), D ** -0.5, 0.25),
        "pos_emb": gaussian(arg_keys[3], (HISTORIES, SEQ_LEN, D), 0.05, 0.29882812, ((0, 16), (1, 32))),
        "pos_ids": draw_pos_ids(jax.random.fold_in(arg_keys[8], 71), 0),
        "neg_emb": gaussian(arg_keys[5], (NEG, D), 0.05, 0.29882812, ((0, 16),)),
        "neg_ids": draw_neg_ids(jax.random.fold_in(arg_keys[8], 71), 0),
        "neg_counts": touch_ends(jax.random.randint(arg_keys[7], (NEG,), 1000, 100000), jax.random.fold_in(arg_keys[7], 1), 1000, 99999).astype(jnp.int32),
    }


SOFTMAX_TEMPER = 0.05

def silu_slope(scores):
    sigma = jax.nn.sigmoid(scores)
    return sigma * (1.0 + scores * (1.0 - sigma))

def rounded(matrix):
    return lax.optimization_barrier(matrix.astype(jnp.bfloat16)).astype(jnp.float32)

def query_block(start, queries, keys, values, grads, score_scale):
    width = queries.shape[0]
    scores = jnp.einsum('ihe,jhe->hij', queries.astype(jnp.float32), keys.astype(jnp.float32)) * score_scale
    query_pos = start + lax.iota(jnp.int32, width)
    key_pos = lax.iota(jnp.int32, keys.shape[0])
    allowed = (key_pos[None, :] <= query_pos[:, None])[None]
    weights = rounded(jnp.where(allowed, jax.nn.silu(scores), 0.0))
    mixed = jnp.einsum('hij,jhe->ihe', weights, values.astype(jnp.float32))
    d_weights = jnp.einsum('ihe,jhe->hij', grads.astype(jnp.float32), values.astype(jnp.float32))
    d_scores = rounded(jnp.where(allowed, d_weights * silu_slope(scores) * score_scale, 0.0))
    d_queries = jnp.einsum('hij,jhe->ihe', d_scores, keys.astype(jnp.float32))
    return (mixed, d_queries)

def key_block(start, queries, keys, values, grads, score_scale):
    width = keys.shape[0]
    scores = jnp.einsum('ihe,jhe->hij', queries.astype(jnp.float32), keys.astype(jnp.float32)) * score_scale
    key_pos = start + lax.iota(jnp.int32, width)
    query_pos = lax.iota(jnp.int32, queries.shape[0])
    allowed = (key_pos[None, :] <= query_pos[:, None])[None]
    weights = rounded(jnp.where(allowed, jax.nn.silu(scores), 0.0))
    d_weights = jnp.einsum('ihe,jhe->hij', grads.astype(jnp.float32), values.astype(jnp.float32))
    d_scores = rounded(jnp.where(allowed, d_weights * silu_slope(scores) * score_scale, 0.0))
    d_keys = jnp.einsum('hij,ihe->jhe', d_scores, queries.astype(jnp.float32))
    d_values = jnp.einsum('hij,ihe->jhe', weights, grads.astype(jnp.float32))
    return (d_keys, d_values)

def attention_forward(queries, keys, values, score_scale, block_rows):
    length = queries.shape[0]
    starts = jnp.arange(length // block_rows, dtype=jnp.int32) * block_rows
    grads = jnp.zeros_like(queries)

    def one_block(start):
        rows = lax.dynamic_slice_in_dim(queries, start, block_rows, 0)
        grad_rows = lax.dynamic_slice_in_dim(grads, start, block_rows, 0)
        return query_block(start, rows, keys, values, grad_rows, score_scale)[0]
    return lax.map(one_block, starts).reshape(length, D)

def history_pass(seq_x, pos_x, pos_id, negative_rounded, log_sample_share, neg_ids, w_in, w_out):
    length = seq_x.shape[0]
    score_scale = HEAD ** (-0.5)
    block_rows = math.gcd(length, 512)
    starts = jnp.arange(length // block_rows, dtype=jnp.int32) * block_rows
    pre_act = jnp.dot(seq_x, w_in, preferred_element_type=jnp.float32)
    proj = jax.nn.silu(pre_act).astype(jnp.bfloat16)
    gate_u = proj[:, :D].astype(jnp.float32)
    values = proj[:, D:2 * D].reshape(length, HEADS, HEAD)
    queries = proj[:, 2 * D:3 * D].reshape(length, HEADS, HEAD)
    keys = proj[:, 3 * D:].reshape(length, HEADS, HEAD)
    mixed = attention_forward(queries, keys, values, score_scale, block_rows)
    centred = mixed - lax.optimization_barrier(jnp.mean(mixed, axis=1, keepdims=True))
    inv_std = lax.rsqrt(lax.optimization_barrier(jnp.mean(centred * centred, axis=1, keepdims=True)) + 1e-05)
    normed = centred * inv_std
    gated = (normed * gate_u).astype(jnp.bfloat16)
    outputs = seq_x.astype(jnp.float32) + jnp.dot(gated, w_out, preferred_element_type=jnp.float32)
    out_scale = lax.rsqrt(lax.optimization_barrier(jnp.sum(outputs * outputs, axis=1, keepdims=True)) + 1e-06)
    user_vector = outputs * out_scale
    user_rounded = user_vector.astype(jnp.bfloat16)
    pos_float = pos_x.astype(jnp.float32)
    positive_unit = pos_float * lax.rsqrt(lax.optimization_barrier(jnp.sum(pos_float * pos_float, axis=1, keepdims=True)) + 1e-06)
    positive_item = lax.optimization_barrier(jnp.sum(user_vector * positive_unit, axis=1)) / SOFTMAX_TEMPER
    score_logits = jnp.dot(user_rounded, negative_rounded.T, preferred_element_type=jnp.float32) / SOFTMAX_TEMPER - log_sample_share[None, :]
    allowed = pos_id[:, None] != neg_ids[None, :]
    terms = jnp.where(allowed, jnp.exp(score_logits), 0.0)
    pos_exp = jnp.exp(positive_item)
    denom = pos_exp + lax.optimization_barrier(jnp.sum(terms, axis=1))
    loss = jnp.log(denom) - positive_item
    positive_gradient = pos_exp / denom - 1.0
    probabilities = (terms / denom[:, None]).astype(jnp.bfloat16)
    user_gradient = positive_gradient[:, None] * positive_unit / SOFTMAX_TEMPER + jnp.dot(probabilities, negative_rounded, preferred_element_type=jnp.float32) / SOFTMAX_TEMPER
    unit_gradient = jnp.dot(probabilities.T, user_rounded, preferred_element_type=jnp.float32) / SOFTMAX_TEMPER
    d_outputs = out_scale * (user_gradient - user_vector * lax.optimization_barrier(jnp.sum(user_vector * user_gradient, axis=1, keepdims=True)))
    d_gated = jnp.dot(d_outputs.astype(jnp.bfloat16), w_out.T, preferred_element_type=jnp.float32)
    d_normed = d_gated * gate_u
    d_gate = d_gated * normed
    d_mixed = inv_std * (d_normed - lax.optimization_barrier(jnp.mean(d_normed, axis=1, keepdims=True)) - normed * lax.optimization_barrier(jnp.mean(d_normed * normed, axis=1, keepdims=True)))
    d_heads = d_mixed.astype(jnp.bfloat16).reshape(length, HEADS, HEAD)

    def query_grads(start):
        rows = lax.dynamic_slice_in_dim(queries, start, block_rows, 0)
        grad_rows = lax.dynamic_slice_in_dim(d_heads, start, block_rows, 0)
        return query_block(start, rows, keys, values, grad_rows, score_scale)[1]

    def key_grads(start):
        key_rows = lax.dynamic_slice_in_dim(keys, start, block_rows, 0)
        value_rows = lax.dynamic_slice_in_dim(values, start, block_rows, 0)
        return key_block(start, queries, key_rows, value_rows, d_heads, score_scale)
    d_queries = lax.map(query_grads, starts).reshape(length, D)
    d_keys, d_values = lax.map(key_grads, starts)
    d_proj = jnp.concatenate([d_gate, d_values.reshape(length, D), d_queries, d_keys.reshape(length, D)], axis=1)
    d_pre = (d_proj * silu_slope(pre_act)).astype(jnp.bfloat16)
    d_seq = (d_outputs + jnp.dot(d_pre, w_in.T, preferred_element_type=jnp.float32)).astype(jnp.bfloat16)
    return (loss, d_seq, unit_gradient)

def reference(seq_in, w_in, w_out, pos_emb, pos_ids, neg_emb, neg_ids, neg_counts):
    neg_float = neg_emb.astype(jnp.float32)
    neg_scale = lax.rsqrt(lax.optimization_barrier(jnp.sum(neg_float * neg_float, axis=1, keepdims=True)) + 1e-06)
    neg_unit = neg_float * neg_scale
    negative_rounded = neg_unit.astype(jnp.bfloat16)
    count_float = neg_counts.astype(jnp.float32)
    log_sample_share = jnp.log(neg_counts.shape[0] * count_float / jnp.sum(count_float))

    def per_history(packed):
        seq_x, pos_x, pos_id = packed
        return history_pass(seq_x, pos_x, pos_id, negative_rounded, log_sample_share, neg_ids, w_in, w_out)
    losses, d_seqs, d_units = lax.map(per_history, (seq_in, pos_emb, pos_ids))
    d_total = lax.optimization_barrier(jnp.sum(d_units, axis=0))
    d_neg = neg_scale * (d_total - neg_unit * lax.optimization_barrier(jnp.sum(neg_unit * d_total, axis=1, keepdims=True)))
    return (losses, d_seqs, d_neg)
```

```python
import jax
import jax.numpy as jnp
from jax import lax
from jax.experimental import pallas as pl
from jax.experimental.pallas import tpu as pltpu
from jax.sharding import PartitionSpec as P

MESH = pl.DeviceIdType.MESH
F32, BF16, I32 = jnp.float32, jnp.bfloat16, jnp.int32
HEAD = 64
ROWS = 128
TEMPER_INV = 20.0


def dot_nn(a, b):
    return lax.dot_general(a, b, (((1,), (0,)), ((), ())), preferred_element_type=F32)


def dot_nt(a, b):
    return lax.dot_general(a, b, (((1,), (1,)), ((), ())), preferred_element_type=F32)


def swap(v):
    return pltpu.roll(v, 64, 1)


def low(shape):
    return lax.broadcasted_iota(I32, shape, 1) < HEAD


def slope(v):
    g = jax.nn.sigmoid(v)
    return g * (1.0 + v * (1.0 - g))


def pack_rows(tile, which):
    top, bottom = tile[:64], tile[64:]
    if which == 0:
        return jnp.where(low(top.shape), top, swap(bottom))
    return jnp.where(low(top.shape), swap(top), bottom)


def unpack_pair(even, odd):
    top = jnp.where(low(even.shape), even, swap(odd))
    bottom = jnp.where(low(even.shape), swap(even), odd)
    return jnp.concatenate([top, bottom], axis=0)


def kernel(
    NY, NB,
    seq_ref, w_in_ref, w_out_ref, pos_ref, pid_ref, neg_ref, nid_ref, ncnt_ref,
    loss_ref, dseq_ref, dneg_ref,
    pre, skv, sq, kv, rq, qz, acc, smix, rmix, sdm, rdm, dmz, qdt, dq, dkv,
    sibo, sibx, sx, rx, sret, rret, sretq, rretq, dout, dpre, negs, nega, gsend, grecv, g1, g2, g3, g4, gfin,
    kv_s, kv_r, q_s, q_r, rel_s, rel_r, xf_s, xf_r, xr_s, xr_r, mix_s, mix_r, dm_s, dm_r,
    so_s, so_r, sx_s, sx_r, xx_s, xx_r, ret_s, ret_r, retq_s, retq_r,
    neg_s, neg_r, gb_s, gb_r, g1_s, g1_r, gc_s, gc_r, g4_s, g4_r,
):
    D = HEAD * NY
    T = NY // 2
    me = lax.axis_index("ctx")
    b = lax.axis_index("batch")
    c = lax.rem(me, 2)
    y = lax.rem(lax.div(me, 2), NY)
    x = lax.div(me, 2 * NY)

    def at(xx, yy, cc):
        return (xx * NY + yy) * 2 + cc

    def yo(d):
        return lax.rem(y + d, NY)

    def bo(d):
        return lax.rem(b + d, NB)

    sib = at(x, y, 1 - c)
    others = [at(x, yo(d), c) for d in range(1, NY)]
    across = [at(1 - x, yo(d), c) for d in range(NY)]

    def copy(src, dst, ss, rs, ctx=None, batch=None):
        where = {"ctx": ctx} if batch is None else {"batch": batch}
        return pltpu.make_async_remote_copy(
            src_ref=src, dst_ref=dst, send_sem=ss, recv_sem=rs, device_id=where, device_id_type=MESH
        )

    barrier = pltpu.get_barrier_semaphore()
    for p in [sib] + others + across:
        pl.semaphore_signal(barrier, inc=1, device_id={"ctx": p}, device_id_type=MESH)
    for d in range(1, NB):
        pl.semaphore_signal(barrier, inc=1, device_id={"batch": bo(d)}, device_id_type=MESH)

    xin = seq_ref[0]
    lane = lax.broadcasted_iota(I32, (ROWS, 128), 1)
    lo = lane < HEAD

    for j in range(NY // 2):
        cols = [slice(p * D + 128 * j, p * D + 128 * (j + 1)) for p in range(4)]
        tiles = []
        for p in (1, 2, 3):
            v = dot_nn(xin, w_in_ref[:, cols[p]])
            pre[:, cols[p]] = v
            tiles.append(jax.nn.silu(v))
        vt, qt, kt = tiles
        skv[2 * j] = jnp.where(lo, kt, swap(vt)).astype(BF16)
        skv[2 * j + 1] = jnp.where(lo, swap(kt), vt).astype(BF16)
        qt = qt * 0.0625
        sq[2 * j] = pack_rows(qt, 0).astype(BF16)
        sq[2 * j + 1] = pack_rows(qt, 1).astype(BF16)

    negs[:, :D] = neg_ref[...].astype(F32)
    meta_lane = lax.broadcasted_iota(I32, (8, 128), 1)
    meta_row = lax.broadcasted_iota(I32, (8, 128), 0)
    meta = jnp.zeros((8, 128), F32)
    for i in range(8):
        here = meta_lane == b * 8 + i
        meta = meta + jnp.where(
            jnp.logical_and(here, meta_row == 0), nid_ref[i].astype(F32),
            jnp.where(jnp.logical_and(here, meta_row == 1), ncnt_ref[i].astype(F32), 0.0),
        )
    negs[:, D:] = meta

    pl.semaphore_wait(barrier, 1 + (NY - 1) + NY + (NB - 1))

    def kv_copy(d):
        h = yo(d)
        return copy(skv.at[h], kv.at[me], kv_s.at[h], kv_r.at[y], ctx=at(x, h, c))

    def q_copy(d):
        h = yo(d)
        return copy(sq.at[h], rq.at[y], q_s.at[h], q_r.at[y], ctx=at(x, h, c))

    far_first = sorted(range(1, NY), key=lambda d: -min(d, NY - d))
    for d in far_first:
        kv_copy(d).start()
        q_copy(d).start()
    kv[me] = skv[y]
    rq[y] = sq[y]

    def relay(yy):
        r = at(x, yy, c)
        return copy(kv.at[r], kv.at[r], rel_s.at[yy], rel_r.at[yy], ctx=sib)

    def own_relay():
        return copy(skv.at[y], kv.at[me], rel_s.at[y], rel_r.at[y], ctx=sib)

    def forward(yy):
        r = at(0, yy, c)
        return copy(kv.at[r], kv.at[r], xf_s.at[yy], xf_r.at[yy], ctx=at(1, y, c))

    def own_forward():
        return copy(skv.at[y], kv.at[me], xf_s.at[y], xf_r.at[y], ctx=at(1, y, c))

    own_relay().start()

    @pl.when(x == 0)
    def _():
        own_forward().start()

    def neg_copy(d):
        return copy(negs, nega.at[b], neg_s.at[d], neg_r.at[b], batch=bo(d))

    for d in range(1, NB):
        neg_copy(d).start()
    nega[b] = negs[...]

    g_pre = dot_nn(xin, w_in_ref[:, :D])
    pre[:, :D] = g_pre

    near_first = far_first[::-1]
    for d in near_first:
        yy = yo(d)
        copy(skv.at[yy], kv.at[at(x, yy, c)], kv_s.at[yy], kv_r.at[yy], ctx=at(x, yy, c)).wait_recv()
        relay(yy).start()

        @pl.when(x == 0)
        def _():
            forward(yy).start()

    for d in near_first:
        yy = yo(d)
        copy(sq.at[yy], rq.at[yy], q_s.at[yy], q_r.at[yy], ctx=at(x, yy, c)).wait_recv()
    half = low((64, 128))
    for i in range(NY):
        v = rq[i].astype(F32)
        qz[i * 128 : i * 128 + 64] = jnp.where(half, v, 0.0).astype(BF16)
        qz[i * 128 + 64 : i * 128 + 128] = jnp.where(half, swap(v), 0.0).astype(BF16)
    acc[...] = jnp.zeros_like(acc)
    for d in range(NY):
        yy = yo(d)
        r = at(x, yy, 1 - c)
        copy(kv.at[r], kv.at[r], rel_s.at[yy], rel_r.at[yy], ctx=sib).wait_recv()

    def q_rows(k):
        return pl.ds(pl.multiple_of(k * 256, 256), 256)

    def keys_of(t):
        return kv[pl.ds(t * 4, 4)].reshape(512, 128)

    def allowed():
        i = lax.broadcasted_iota(I32, (256, 512), 0)
        j = lax.broadcasted_iota(I32, (256, 512), 1)
        return j <= i + jnp.where(i >= 128, 128, 0) + c * 128

    def fwd(k, t, diagonal):
        tile = keys_of(t)
        h = dot_nt(qz[q_rows(k), :], tile)
        w = h + h * jnp.tanh(h)
        if diagonal:
            w = jnp.where(allowed(), w, 0.0)
        acc[q_rows(k), :] += dot_nn(w.astype(BF16), tile)

    @pl.loop(0, T)
    def _(k):
        fwd(k, x * T + k, True)

        @pl.loop(0, k)
        def _(t):
            fwd(k, x * T + t, False)

    @pl.when(x == 1)
    def _():
        for d in range(NY):
            yy = yo(d)
            r = at(0, yy, c)
            copy(kv.at[r], kv.at[r], xf_s.at[yy], xf_r.at[yy], ctx=at(0, y, c)).wait_recv()
            copy(kv.at[r], kv.at[r], xr_s.at[yy], xr_r.at[yy], ctx=sib).start()
        for d in range(NY):
            yy = yo(d)
            r = at(0, yy, 1 - c)
            copy(kv.at[r], kv.at[r], xr_s.at[yy], xr_r.at[yy], ctx=sib).wait_recv()

        @pl.loop(0, T)
        def _(k):
            @pl.loop(0, T)
            def _(t):
                fwd(k, t, False)

    for i in range(NY):
        top = acc[i * 128 : i * 128 + 64]
        bottom = acc[i * 128 + 64 : i * 128 + 128]
        smix[i] = jnp.where(half, swap(top), bottom).astype(BF16)

    def mix_copy(d):
        yy = yo(d)
        return copy(smix.at[yy], rmix.at[y], mix_s.at[yy], mix_r.at[y], ctx=at(x, yy, c))

    for d in far_first:
        mix_copy(d).start()
    rmix[y] = smix[y]

    for d in range(1, NB):
        bb = bo(d)
        copy(negs, nega.at[bb], neg_s.at[d], neg_r.at[bb], batch=bb).wait_recv()
    NEG = 8 * NB
    neg_f = nega[:, :, :D].reshape(NEG, D)
    neg_b = (neg_f * lax.rsqrt(jnp.sum(neg_f * neg_f, axis=1, keepdims=True) + 1e-06)).astype(BF16)
    metas = nega[0, :, D:]
    for i in range(1, NB):
        metas = metas + nega[i, :, D:]
    ids = metas[0:1, :NEG]
    counts = metas[1:2, :NEG]
    log_share = jnp.log(NEG * counts / jnp.sum(counts, axis=1, keepdims=True))
    pid = jnp.transpose(jnp.broadcast_to(pid_ref[...].astype(F32), (NEG, ROWS)))
    same = pid == ids
    posf = pos_ref[0].astype(F32)
    pos_unit = posf * lax.rsqrt(jnp.sum(posf * posf, axis=1, keepdims=True) + 1e-06)
    gate_u = jax.nn.silu(pre[:, :D]).astype(BF16).astype(F32)

    for d in near_first:
        yy = yo(d)
        copy(smix.at[yy], rmix.at[yy], mix_s.at[yy], mix_r.at[yy], ctx=at(x, yy, c)).wait_recv()
    mixed = jnp.concatenate(
        [unpack_pair(rmix[2 * j].astype(F32), rmix[2 * j + 1].astype(F32)) for j in range(NY // 2)], axis=1
    )
    centred = mixed - jnp.mean(mixed, axis=1, keepdims=True)
    inv_std = lax.rsqrt(jnp.mean(centred * centred, axis=1, keepdims=True) + 1e-05)
    normed = centred * inv_std
    gated = (normed * gate_u).astype(BF16)
    outputs = xin.astype(F32) + dot_nn(gated, w_out_ref[...])
    out_scale = lax.rsqrt(jnp.sum(outputs * outputs, axis=1, keepdims=True) + 1e-06)
    user = outputs * out_scale
    user_b = user.astype(BF16)
    positive = jnp.sum(user * pos_unit, axis=1, keepdims=True) * TEMPER_INV
    logits = dot_nt(user_b, neg_b) * TEMPER_INV - log_share
    terms = jnp.where(same, 0.0, jnp.exp(logits))
    pos_exp = jnp.exp(positive)
    denom = pos_exp + jnp.sum(terms, axis=1, keepdims=True)
    loss = jnp.log(denom) - positive
    d_pos = pos_exp / denom - 1.0
    probs = terms / denom
    probs_b = probs.astype(BF16)
    d_user = (d_pos * TEMPER_INV) * pos_unit + dot_nn(probs_b, neg_b) * TEMPER_INV
    d_out = out_scale * (d_user - user * jnp.sum(user * d_user, axis=1, keepdims=True))
    dout[...] = d_out
    d_gated = dot_nt(d_out.astype(BF16), w_out_ref[...])
    d_normed = d_gated * gate_u
    d_gate = d_gated * normed
    d_mixed = inv_std * (
        d_normed
        - jnp.mean(d_normed, axis=1, keepdims=True)
        - normed * jnp.mean(d_normed * normed, axis=1, keepdims=True)
    )
    for j in range(NY // 2):
        tile = d_mixed[:, 128 * j : 128 * (j + 1)]
        sdm[2 * j] = pack_rows(tile, 0).astype(BF16)
        sdm[2 * j + 1] = pack_rows(tile, 1).astype(BF16)

    def dm_copy(d):
        yy = yo(d)
        return copy(sdm.at[yy], rdm.at[y], dm_s.at[yy], dm_r.at[y], ctx=at(x, yy, c))

    for d in far_first:
        dm_copy(d).start()
    rdm[y] = sdm[y]

    dpre[:, :D] = (d_gate * slope(pre[:, :D])).astype(BF16)
    loss_ref[...] = jnp.transpose(jnp.broadcast_to(loss, (ROWS, 128)))[0:1, :]
    grad = dot_nn(jnp.transpose(probs).astype(BF16), user_b) * TEMPER_INV
    gsend[...] = grad.reshape(NB, 8, D)

    def gb_copy(d):
        bb = bo(d)
        return copy(gsend.at[bb], grecv.at[b], gb_s.at[d], gb_r.at[b], batch=bb)

    for d in range(1, NB):
        gb_copy(d).start()
    grecv[b] = gsend[b]
    dq[...] = jnp.zeros_like(dq)
    dkv[...] = jnp.zeros_like(dkv)

    for d in near_first:
        yy = yo(d)
        copy(sdm.at[yy], rdm.at[yy], dm_s.at[yy], dm_r.at[yy], ctx=at(x, yy, c)).wait_recv()
    for i in range(NY):
        v = rdm[i].astype(F32)
        up = jnp.concatenate([jnp.where(half, 0.0, swap(v)), jnp.where(half, 0.0, v)], axis=0)
        dmz[i * 128 : i * 128 + 128] = up.astype(BF16)
        both = up + qz[i * 128 : i * 128 + 128].astype(F32)
        qdt[i // 2, :, 128 * (i % 2) : 128 * (i % 2) + 128] = jnp.transpose(both).astype(BF16)

    def bwd(k, t, diagonal):
        tile = keys_of(t)
        h = dot_nt(qz[q_rows(k), :], tile)
        dw = dot_nt(dmz[q_rows(k), :], tile)
        th = jnp.tanh(h)
        u = 1.0 + th
        w = h * u
        ds = dw * (u + w * (1.0 - th))
        if diagonal:
            ok = allowed()
            w = jnp.where(ok, w, 0.0)
            ds = jnp.where(ok, ds, 0.0)
        w = w.astype(BF16)
        ds = ds.astype(BF16)
        dq[q_rows(k), :] += dot_nn(ds, tile)
        dk = dot_nn(qdt[k, :64, :], ds)
        dv = dot_nn(qdt[k, 64:, :], w)
        for j in range(4):
            dkv[t * 4 + j, :64, :] += dk[:, 128 * j : 128 * (j + 1)]
            dkv[t * 4 + j, 64:, :] += dv[:, 128 * j : 128 * (j + 1)]

    def sib_own(yy):
        return copy(dkv.at[at(x, yy, 1 - c)], sibo.at[yy], so_s.at[yy], so_r.at[yy], ctx=sib)

    def sib_cross(yy):
        return copy(dkv.at[at(0, yy, 1 - c)], sibx.at[yy], sx_s.at[yy], sx_r.at[yy], ctx=sib)

    def cross(yy):
        return copy(sx.at[yy], rx.at[yy], xx_s.at[yy], xx_r.at[yy], ctx=at(1 - x, y, c))

    @pl.when(x == 1)
    def _():
        @pl.loop(0, T)
        def _(t):
            @pl.loop(0, T)
            def _(k):
                bwd(k, t, False)

        for i in range(NY):
            sib_cross(i).start()
        for i in range(NY):
            sib_cross(i).wait_recv()
            sx[i] = (dkv[at(0, i, c)] + sibx[i]).astype(BF16)
            cross(i).start()

    @pl.loop(0, T)
    def _(t):
        bwd(t, x * T + t, True)

        @pl.loop(t + 1, T)
        def _(k):
            bwd(k, x * T + t, False)

    for i in range(NY):
        sib_own(i).start()

    for i in range(NY):
        top = dq[i * 128 : i * 128 + 64] * 0.0625
        bottom = dq[i * 128 + 64 : i * 128 + 128] * 0.0625
        sretq[i] = jnp.where(half, top, swap(bottom)).astype(BF16)

    def retq_copy(d):
        yy = yo(d)
        return copy(sretq.at[yy], rretq.at[y], retq_s.at[yy], retq_r.at[y], ctx=at(x, yy, c))

    for d in far_first:
        retq_copy(d).start()
    rretq[y] = sretq[y]

    for d in range(1, NB):
        bb = bo(d)
        copy(gsend.at[bb], grecv.at[bb], gb_s.at[d], gb_r.at[bb], batch=bb).wait_recv()
    g1[...] = jnp.sum(grecv[...], axis=0)

    def g1_copy():
        return copy(g1, g2, g1_s.at[0], g1_r.at[0], ctx=sib)

    g1_copy().start()

    def ret_copy(d):
        yy = yo(d)
        return copy(sret.at[yy], rret.at[y], ret_s.at[yy], ret_r.at[y], ctx=at(x, yy, c))

    for d in far_first + [0]:
        yy = yo(d)
        sib_own(yy).wait_recv()
        total = dkv[at(x, yy, c)] + sibo[yy]

        @pl.when(x == 0)
        def _():
            copy(sx.at[yy], rx.at[yy], xx_s.at[yy], xx_r.at[yy], ctx=at(1, y, c)).wait_recv()
            sret[yy] = jnp.transpose(total + rx[yy].astype(F32)).astype(BF16)

        @pl.when(x == 1)
        def _():
            sret[yy] = jnp.transpose(total).astype(BF16)

        if d:
            ret_copy(d).start()
    rret[y] = sret[y]

    g1_copy().wait_recv()
    H = D // 2
    gsum = g1[...] + g2[...]
    g3[...] = jnp.where(c == 0, gsum[:, :H], gsum[:, H:])

    def gc_copy(d, xx):
        yy = yo(d)
        return copy(g3, g4.at[x * NY + y], gc_s.at[xx * NY + d], gc_r.at[x * NY + y], ctx=at(jnp.where(xx == 0, x, 1 - x), yy, c))

    peers = [(d, 0) for d in range(1, NY)] + [(d, 1) for d in range(NY)]
    for d, xx in peers:
        gc_copy(d, xx).start()
    g4[x * NY + y] = g3[...]

    for d in near_first:
        yy = yo(d)
        copy(sretq.at[yy], rretq.at[yy], retq_s.at[yy], retq_r.at[yy], ctx=at(x, yy, c)).wait_recv()
    for j in range(NY // 2):
        cols = slice(2 * D + 128 * j, 2 * D + 128 * (j + 1))
        d_q = unpack_pair(rretq[2 * j].astype(F32), rretq[2 * j + 1].astype(F32))
        dpre[:, cols] = (d_q * slope(pre[:, cols])).astype(BF16)

    for d, xx in peers:
        s = jnp.where(xx == 0, x, 1 - x) * NY + yo(d)
        copy(g3, g4.at[s], gc_s.at[xx * NY + d], gc_r.at[s], ctx=sib).wait_recv()
    gfin[c] = jnp.sum(g4[...], axis=0)

    def g4_copy():
        return copy(gfin.at[c], gfin.at[c], g4_s.at[0], g4_r.at[0], ctx=sib)

    g4_copy().start()

    for d in near_first:
        yy = yo(d)
        copy(sret.at[yy], rret.at[yy], ret_s.at[yy], ret_r.at[yy], ctx=at(x, yy, c)).wait_recv()
    for j in range(NY // 2):
        even, odd = rret[2 * j].astype(F32), rret[2 * j + 1].astype(F32)
        cols = slice(3 * D + 128 * j, 3 * D + 128 * (j + 1))
        dpre[:, cols] = (jnp.where(lo, even, swap(odd)) * slope(pre[:, cols])).astype(BF16)
        cols = slice(D + 128 * j, D + 128 * (j + 1))
        dpre[:, cols] = (jnp.where(lo, swap(even), odd) * slope(pre[:, cols])).astype(BF16)
    dseq_ref[0] = (dout[...] + dot_nt(dpre[...], w_in_ref[...])).astype(BF16)

    copy(gfin.at[1 - c], gfin.at[1 - c], g4_s.at[0], g4_r.at[0], ctx=sib).wait_recv()
    d_total = jnp.concatenate([gfin[0], gfin[1]], axis=1)
    nf = neg_ref[...].astype(F32)
    scale = lax.rsqrt(jnp.sum(nf * nf, axis=1, keepdims=True) + 1e-06)
    unit = nf * scale
    dneg_ref[...] = scale * (d_total - unit * jnp.sum(unit * d_total, axis=1, keepdims=True))

    for d in range(1, NY):
        kv_copy(d).wait_send()
        q_copy(d).wait_send()
        mix_copy(d).wait_send()
        dm_copy(d).wait_send()
        retq_copy(d).wait_send()
        ret_copy(d).wait_send()
    for i in range(NY):
        relay(i).wait_send()
        sib_own(i).wait_send()
    for d in range(1, NB):
        neg_copy(d).wait_send()
        gb_copy(d).wait_send()
    for d, xx in peers:
        gc_copy(d, xx).wait_send()
    g1_copy().wait_send()
    g4_copy().wait_send()

    @pl.when(x == 0)
    def _():
        for i in range(NY):
            forward(i).wait_send()

    @pl.when(x == 1)
    def _():
        for i in range(NY):
            r = at(0, i, c)
            copy(kv.at[r], kv.at[r], xr_s.at[i], xr_r.at[i], ctx=sib).wait_send()
            sib_cross(i).wait_send()
            cross(i).wait_send()


def solution(mesh):
    NY = mesh.shape["ctx"] // 4
    NB = mesh.shape["batch"]
    D = HEAD * NY
    V, S = pltpu.VMEM, pltpu.SemaphoreType.DMA

    def body(*refs):
        kernel(NY, NB, *refs)

    def shards(seq_in, w_in, w_out, pos_emb, pos_ids, neg_emb, neg_ids, neg_counts):
        vm = pl.BlockSpec(memory_space=pltpu.VMEM)
        sm = pl.BlockSpec(memory_space=pltpu.SMEM)
        return pl.pallas_call(
            body,
            out_shape=(
                jax.ShapeDtypeStruct((1, ROWS), F32),
                jax.ShapeDtypeStruct((1, ROWS, D), BF16),
                jax.ShapeDtypeStruct((8, D), F32),
            ),
            in_specs=[vm] * 6 + [sm] * 2,
            out_specs=(vm, vm, vm),
            scratch_shapes=[
                V((ROWS, 4 * D), F32),
                V((NY, 128, 128), BF16),
                V((NY, 64, 128), BF16),
                V((4 * NY, 128, 128), BF16),
                V((NY, 64, 128), BF16),
                V((NY * 128, 128), BF16),
                V((NY * 128, 128), F32),
                V((NY, 64, 128), BF16),
                V((NY, 64, 128), BF16),
                V((NY, 64, 128), BF16),
                V((NY, 64, 128), BF16),
                V((NY * 128, 128), BF16),
                V((NY // 2, 128, 256), BF16),
                V((NY * 128, 128), F32),
                V((4 * NY, 128, 128), F32),
                V((NY, 128, 128), F32),
                V((NY, 128, 128), F32),
                V((NY, 128, 128), BF16),
                V((NY, 128, 128), BF16),
                V((NY, 128, 128), BF16),
                V((NY, 128, 128), BF16),
                V((NY, 64, 128), BF16),
                V((NY, 64, 128), BF16),
                V((ROWS, D), F32),
                V((ROWS, 4 * D), BF16),
                V((8, D + 128), F32),
                V((NB, 8, D + 128), F32),
                V((NB, 8, D), F32),
                V((NB, 8, D), F32),
                V((8, D), F32),
                V((8, D), F32),
                V((8, D // 2), F32),
                V((2 * NY, 8, D // 2), F32),
                V((2, 8, D // 2), F32),
            ]
            + [S((NY,))] * 24
            + [S((NB,))] * 4
            + [S((1,))] * 2
            + [S((2 * NY,))] * 2
            + [S((1,))] * 2,
            compiler_params=pltpu.CompilerParams(
                collective_id=0, has_side_effects=True, vmem_limit_bytes=48 << 20
            ),
        )(seq_in, w_in, w_out, pos_emb, pos_ids, neg_emb, neg_ids, neg_counts)

    in_specs = (
        P("batch", "ctx", None), P(), P(), P("batch", "ctx", None), P("batch", "ctx"),
        P("batch", None), P("batch"), P("batch"),
    )
    out_specs = (P("batch", "ctx"), P("batch", "ctx", None), P("batch", None))
    return jax.shard_map(shards, mesh=mesh, in_specs=in_specs, out_specs=out_specs, check_vma=False)
```

```python
import jax
import jax.numpy as jnp
from jax import lax
from jax.experimental import pallas as pl
from jax.experimental.pallas import tpu as pltpu
from jax.sharding import PartitionSpec as P

MESH = pl.DeviceIdType.MESH
F32, BF16, I32 = jnp.float32, jnp.bfloat16, jnp.int32
HEAD = 64
ROWS = 128
TEMPER_INV = 20.0


def dot_nn(a, b):
    return lax.dot_general(a, b, (((1,), (0,)), ((), ())), preferred_element_type=F32)


def dot_nt(a, b):
    return lax.dot_general(a, b, (((1,), (1,)), ((), ())), preferred_element_type=F32)


def swap(v):
    return pltpu.roll(v, 64, 1)


def low(shape):
    return lax.broadcasted_iota(I32, shape, 1) < HEAD


def slope(v):
    g = jax.nn.sigmoid(v)
    return g * (1.0 + v * (1.0 - g))


def pack_rows(tile, which):
    top, bottom = tile[:64], tile[64:]
    if which == 0:
        return jnp.where(low(top.shape), top, swap(bottom))
    return jnp.where(low(top.shape), swap(top), bottom)


def unpack_pair(even, odd):
    top = jnp.where(low(even.shape), even, swap(odd))
    bottom = jnp.where(low(even.shape), swap(even), odd)
    return jnp.concatenate([top, bottom], axis=0)


def kernel(
    NY, NB,
    seq_hbm, w_in_hbm, w_out_hbm, pos_hbm, pid_hbm, neg_hbm, nid_hbm, ncnt_hbm,
    loss_ref, dseq_ref, dneg_ref,
    seq_ref, w_in_ref, w_out_ref, pos_ref, pid_ref, neg_ref, nid_ref, ncnt_ref, in_s,
    pre, skv, sq, kv, rq, qz, acc, smix, rmix, sdm, rdm, dmz, qdt, dq, dkv,
    sibo, sibx, sx, rx, sret, rret, sretq, rretq, dout, dpre, negs, nega, gsend, grecv, g1, g2, g3, g4, gfin,
    kv_s, kv_r, q_s, q_r, rel_s, rel_r, xf_s, xf_r, xr_s, xr_r, mix_s, mix_r, dm_s, dm_r,
    so_s, so_r, sx_s, sx_r, xx_s, xx_r, ret_s, ret_r, retq_s, retq_r,
    neg_s, neg_r, gb_s, gb_r, g1_s, g1_r, gc_s, gc_r, g4_s, g4_r,
):
    D = HEAD * NY
    T = NY // 2
    me = lax.axis_index("ctx")
    b = lax.axis_index("batch")
    c = lax.rem(me, 2)
    y = lax.rem(lax.div(me, 2), NY)
    x = lax.div(me, 2 * NY)

    def at(xx, yy, cc):
        return (xx * NY + yy) * 2 + cc

    def yo(d):
        return lax.rem(y + d, NY)

    def bo(d):
        return lax.rem(b + d, NB)

    sib = at(x, y, 1 - c)
    others = [at(x, yo(d), c) for d in range(1, NY)]
    across = [at(1 - x, yo(d), c) for d in range(NY)]

    def copy(src, dst, ss, rs, ctx=None, batch=None):
        where = {"ctx": ctx} if batch is None else {"batch": batch}
        return pltpu.make_async_remote_copy(
            src_ref=src, dst_ref=dst, send_sem=ss, recv_sem=rs, device_id=where, device_id_type=MESH
        )


    loads = [
        pltpu.make_async_copy(src, dst, in_s.at[i])
        for i, (src, dst) in enumerate(
            [
                (seq_hbm, seq_ref),
                (w_in_hbm.at[:, D:], w_in_ref.at[:, D:]),
                (w_in_hbm.at[:, :D], w_in_ref.at[:, :D]),
                (neg_hbm, neg_ref),
                (nid_hbm, nid_ref),
                (ncnt_hbm, ncnt_ref),
                (pos_hbm, pos_ref),
                (pid_hbm, pid_ref),
                (w_out_hbm, w_out_ref),
            ]
        )
    ]
    for load in loads:
        load.start()
    barrier = pltpu.get_barrier_semaphore()
    for p in [sib] + others + across:
        pl.semaphore_signal(barrier, inc=1, device_id={"ctx": p}, device_id_type=MESH)
    for d in range(1, NB):
        pl.semaphore_signal(barrier, inc=1, device_id={"batch": bo(d)}, device_id_type=MESH)

    loads[0].wait()
    loads[1].wait()
    xin = seq_ref[0]
    lane = lax.broadcasted_iota(I32, (ROWS, 128), 1)
    lo = lane < HEAD

    for j in range(NY // 2):
        cols = [slice(p * D + 128 * j, p * D + 128 * (j + 1)) for p in range(4)]
        tiles = []
        for p in (1, 2, 3):
            v = dot_nn(xin, w_in_ref[:, cols[p]])
            pre[:, cols[p]] = v
            tiles.append(jax.nn.silu(v))
        vt, qt, kt = tiles
        skv[2 * j] = jnp.where(lo, kt, swap(vt)).astype(BF16)
        skv[2 * j + 1] = jnp.where(lo, swap(kt), vt).astype(BF16)
        qt = qt * 0.0625
        sq[2 * j] = pack_rows(qt, 0).astype(BF16)
        sq[2 * j + 1] = pack_rows(qt, 1).astype(BF16)

    for load in loads[2:]:
        load.wait()
    negs[:, :D] = neg_ref[...].astype(F32)
    meta_lane = lax.broadcasted_iota(I32, (8, 128), 1)
    meta_row = lax.broadcasted_iota(I32, (8, 128), 0)
    meta = jnp.zeros((8, 128), F32)
    for i in range(8):
        here = meta_lane == b * 8 + i
        meta = meta + jnp.where(
            jnp.logical_and(here, meta_row == 0), nid_ref[i].astype(F32),
            jnp.where(jnp.logical_and(here, meta_row == 1), ncnt_ref[i].astype(F32), 0.0),
        )
    negs[:, D:] = meta

    pl.semaphore_wait(barrier, 1 + (NY - 1) + NY + (NB - 1))

    def kv_copy(d):
        h = yo(d)
        return copy(skv.at[h], kv.at[me], kv_s.at[h], kv_r.at[y], ctx=at(x, h, c))

    def q_copy(d):
        h = yo(d)
        return copy(sq.at[h], rq.at[y], q_s.at[h], q_r.at[y], ctx=at(x, h, c))

    far_first = sorted(range(1, NY), key=lambda d: -min(d, NY - d))
    for d in far_first:
        kv_copy(d).start()
        q_copy(d).start()
    kv[me] = skv[y]
    rq[y] = sq[y]

    def relay(yy):
        r = at(x, yy, c)
        return copy(kv.at[r], kv.at[r], rel_s.at[yy], rel_r.at[yy], ctx=sib)

    def own_relay():
        return copy(skv.at[y], kv.at[me], rel_s.at[y], rel_r.at[y], ctx=sib)

    def forward(yy):
        r = at(0, yy, c)
        return copy(kv.at[r], kv.at[r], xf_s.at[yy], xf_r.at[yy], ctx=at(1, y, c))

    def own_forward():
        return copy(skv.at[y], kv.at[me], xf_s.at[y], xf_r.at[y], ctx=at(1, y, c))

    own_relay().start()

    @pl.when(x == 0)
    def _():
        own_forward().start()

    def neg_copy(d):
        return copy(negs, nega.at[b], neg_s.at[d], neg_r.at[b], batch=bo(d))

    for d in range(1, NB):
        neg_copy(d).start()
    nega[b] = negs[...]

    g_pre = dot_nn(xin, w_in_ref[:, :D])
    pre[:, :D] = g_pre

    near_first = far_first[::-1]
    for d in near_first:
        yy = yo(d)
        copy(skv.at[yy], kv.at[at(x, yy, c)], kv_s.at[yy], kv_r.at[yy], ctx=at(x, yy, c)).wait_recv()
        relay(yy).start()

        @pl.when(x == 0)
        def _():
            forward(yy).start()

    for d in near_first:
        yy = yo(d)
        copy(sq.at[yy], rq.at[yy], q_s.at[yy], q_r.at[yy], ctx=at(x, yy, c)).wait_recv()
    half = low((64, 128))
    for i in range(NY):
        v = rq[i].astype(F32)
        qz[i * 128 : i * 128 + 64] = jnp.where(half, v, 0.0).astype(BF16)
        qz[i * 128 + 64 : i * 128 + 128] = jnp.where(half, swap(v), 0.0).astype(BF16)
    for d in range(NY):
        yy = yo(d)
        r = at(x, yy, 1 - c)
        copy(kv.at[r], kv.at[r], rel_s.at[yy], rel_r.at[yy], ctx=sib).wait_recv()

    def keys_of(t):
        return kv[pl.ds(t * 4, 4)].reshape(512, 128)

    def allowed():
        i = lax.broadcasted_iota(I32, (256, 512), 0)
        j = lax.broadcasted_iota(I32, (256, 512), 1)
        return j <= i + jnp.where(i >= 128, 128, 0) + c * 128

    def weighted(q, tile, diagonal):
        h = dot_nt(q, tile)
        w = h + h * jnp.tanh(h)
        if diagonal:
            last = jnp.where(allowed(), w[:, -512:], 0.0)
            w = last if w.shape[1] == 512 else jnp.concatenate([w[:, :-512], last], axis=1)
        return dot_nn(w.astype(BF16), tile)

    def mix_copy(i):
        return copy(smix.at[i], rmix.at[y], mix_s.at[i], mix_r.at[y], ctx=at(x, i, c))

    def send_mixed(k, rows):
        for e in range(2):
            i = 2 * k + e
            top, bottom = rows[e * 128 : e * 128 + 64], rows[e * 128 + 64 : e * 128 + 128]
            smix[i] = jnp.where(half, swap(top), bottom).astype(BF16)

            @pl.when(y == i)
            def _():
                rmix[y] = smix[i]

            @pl.when(y != i)
            def _():
                mix_copy(i).start()

    def cross_in(yy):
        r = at(0, yy, c)
        return copy(kv.at[r], kv.at[r], xf_s.at[yy], xf_r.at[yy], ctx=at(1 - x, y, c))

    def cross_relay(yy, cc):
        r = at(0, yy, cc)
        return copy(kv.at[r], kv.at[r], xr_s.at[yy], xr_r.at[yy], ctx=sib)

    def take_cross(ds):
        @pl.when(x == 1)
        def _():
            for d in ds:
                cross_in(yo(d)).wait_recv()
                cross_relay(yo(d), c).start()

    order = [0] + near_first
    take_cross(order[: NY // 2])
    for k in range(T):
        if k == T - 1:
            take_cross(order[NY // 2 :])
        tile = kv[pl.ds(x * 2 * NY, 4 * (k + 1))].reshape(512 * (k + 1), 128)
        rows = weighted(qz[256 * k : 256 * (k + 1)], tile, True)

        @pl.when(x == 0)
        def _():
            send_mixed(k, rows)

        @pl.when(x == 1)
        def _():
            acc[256 * k : 256 * (k + 1)] = rows


    @pl.when(x == 1)
    def _():
        for d in order:
            cross_relay(yo(d), 1 - c).wait_recv()
        tile = kv[: 2 * NY].reshape(512 * T, 128)
        for k in range(T):
            rows = slice(256 * k, 256 * (k + 1))
            send_mixed(k, acc[rows] + weighted(qz[rows], tile, False))

    for d in range(1, NB):
        bb = bo(d)
        copy(negs, nega.at[bb], neg_s.at[d], neg_r.at[bb], batch=bb).wait_recv()
    NEG = 8 * NB
    neg_f = nega[:, :, :D].reshape(NEG, D)
    neg_b = (neg_f * lax.rsqrt(jnp.sum(neg_f * neg_f, axis=1, keepdims=True) + 1e-06)).astype(BF16)
    metas = nega[0, :, D:]
    for i in range(1, NB):
        metas = metas + nega[i, :, D:]
    ids = metas[0:1, :NEG]
    counts = metas[1:2, :NEG]
    log_share = jnp.log(NEG * counts / jnp.sum(counts, axis=1, keepdims=True))
    pid = jnp.transpose(jnp.broadcast_to(pid_ref[...].astype(F32), (NEG, ROWS)))
    same = pid == ids
    posf = pos_ref[0].astype(F32)
    pos_unit = posf * lax.rsqrt(jnp.sum(posf * posf, axis=1, keepdims=True) + 1e-06)
    gate_u = jax.nn.silu(pre[:, :D]).astype(BF16).astype(F32)

    for d in near_first:
        yy = yo(d)
        copy(smix.at[yy], rmix.at[yy], mix_s.at[yy], mix_r.at[yy], ctx=at(x, yy, c)).wait_recv()
    mixed = jnp.concatenate(
        [unpack_pair(rmix[2 * j].astype(F32), rmix[2 * j + 1].astype(F32)) for j in range(NY // 2)], axis=1
    )
    centred = mixed - jnp.mean(mixed, axis=1, keepdims=True)
    inv_std = lax.rsqrt(jnp.mean(centred * centred, axis=1, keepdims=True) + 1e-05)
    normed = centred * inv_std
    gated = (normed * gate_u).astype(BF16)
    outputs = xin.astype(F32) + dot_nn(gated, w_out_ref[...])
    out_scale = lax.rsqrt(jnp.sum(outputs * outputs, axis=1, keepdims=True) + 1e-06)
    user = outputs * out_scale
    user_b = user.astype(BF16)
    positive = jnp.sum(user * pos_unit, axis=1, keepdims=True) * TEMPER_INV
    logits = dot_nt(user_b, neg_b) * TEMPER_INV - log_share
    terms = jnp.where(same, 0.0, jnp.exp(logits))
    pos_exp = jnp.exp(positive)
    denom = pos_exp + jnp.sum(terms, axis=1, keepdims=True)
    loss = jnp.log(denom) - positive
    d_pos = pos_exp / denom - 1.0
    probs = terms / denom
    probs_b = probs.astype(BF16)
    d_user = (d_pos * TEMPER_INV) * pos_unit + dot_nn(probs_b, neg_b) * TEMPER_INV
    d_out = out_scale * (d_user - user * jnp.sum(user * d_user, axis=1, keepdims=True))
    d_gated = dot_nt(d_out.astype(BF16), w_out_ref[...])
    d_normed = d_gated * gate_u
    d_gate = d_gated * normed
    d_mixed = inv_std * (
        d_normed
        - jnp.mean(d_normed, axis=1, keepdims=True)
        - normed * jnp.mean(d_normed * normed, axis=1, keepdims=True)
    )
    for j in range(NY // 2):
        tile = d_mixed[:, 128 * j : 128 * (j + 1)]
        sdm[2 * j] = pack_rows(tile, 0).astype(BF16)
        sdm[2 * j + 1] = pack_rows(tile, 1).astype(BF16)

    def dm_copy(d):
        yy = yo(d)
        return copy(sdm.at[yy], rdm.at[y], dm_s.at[yy], dm_r.at[y], ctx=at(x, yy, c))

    for d in far_first:
        dm_copy(d).start()
    rdm[y] = sdm[y]

    d_pre = (d_gate * slope(pre[:, :D])).astype(BF16)
    dout[...] = d_out + dot_nt(d_pre, w_in_ref[:, :D])
    loss_ref[...] = jnp.transpose(jnp.broadcast_to(loss, (ROWS, 128)))[0:1, :]
    grad = dot_nn(jnp.transpose(probs).astype(BF16), user_b) * TEMPER_INV
    gsend[...] = grad.reshape(NB, 8, D)

    def gb_copy(d):
        bb = bo(d)
        return copy(gsend.at[bb], grecv.at[b], gb_s.at[d], gb_r.at[b], batch=bb)

    for d in range(1, NB):
        gb_copy(d).start()
    grecv[b] = gsend[b]
    dq[...] = jnp.zeros_like(dq)

    for d in near_first:
        yy = yo(d)
        copy(sdm.at[yy], rdm.at[yy], dm_s.at[yy], dm_r.at[yy], ctx=at(x, yy, c)).wait_recv()
    for i in range(NY):
        v = rdm[i].astype(F32)
        up = jnp.concatenate([jnp.where(half, 0.0, swap(v)), jnp.where(half, 0.0, v)], axis=0)
        dmz[i * 128 : i * 128 + 128] = up.astype(BF16)
        both = up + qz[i * 128 : i * 128 + 128].astype(F32)
        qdt[:, i * 128 : i * 128 + 128] = jnp.transpose(both).astype(BF16)

    def g1_copy():
        return copy(g1, g2, g1_s.at[0], g1_r.at[0], ctx=sib)

    def gc_copy(d, xx):
        there = x if xx == 0 else 1 - x
        return copy(
            g3, g4.at[x * NY + y], gc_s.at[xx * NY + d], gc_r.at[x * NY + y], ctx=at(there, yo(d), c)
        )

    def g4_copy():
        return copy(gfin.at[c], gfin.at[c], g4_s.at[0], g4_r.at[0], ctx=sib)

    peers = [(d, 0) for d in range(1, NY)] + [(d, 1) for d in range(NY)]
    H = D // 2

    def g_histories():
        for d in range(1, NB):
            bb = bo(d)
            copy(gsend.at[bb], grecv.at[bb], gb_s.at[d], gb_r.at[bb], batch=bb).wait_recv()
        g1[...] = jnp.sum(grecv[...], axis=0)
        g1_copy().start()

    def g_pair():
        g1_copy().wait_recv()
        gsum = g1[...] + g2[...]
        g3[...] = jnp.where(c == 0, gsum[:, :H], gsum[:, H:])
        for d, xx in peers:
            gc_copy(d, xx).start()
        g4[x * NY + y] = g3[...]

    def g_chips():
        for d, xx in peers:
            s = (x if xx == 0 else 1 - x) * NY + yo(d)
            copy(g3, g4.at[s], gc_s.at[xx * NY + d], gc_r.at[s], ctx=sib).wait_recv()
        gfin[c] = jnp.sum(g4[...], axis=0)
        g4_copy().start()

    def bwd(k0, t, diagonal):
        rows = slice(256 * k0, 256 * T)
        tile = keys_of(t)
        h = dot_nt(qz[rows], tile)
        dw = dot_nt(dmz[rows], tile)
        th = jnp.tanh(h)
        u = 1.0 + th
        w = h * u
        ds = dw * (u + w * (1.0 - th))
        if diagonal:
            ok = allowed()

            def masked(v):
                first = jnp.where(ok, v[:256], 0.0)
                return first if v.shape[0] == 256 else jnp.concatenate([first, v[256:]], axis=0)

            w, ds = masked(w), masked(ds)
        w = w.astype(BF16)
        ds = ds.astype(BF16)
        dq[rows] += dot_nn(ds, tile)
        dk = dot_nn(qdt[:64, rows], ds)
        dv = dot_nn(qdt[64:, rows], w)
        for j in range(4):
            dkv[t * 4 + j, :64, :] = dk[:, 128 * j : 128 * (j + 1)]
            dkv[t * 4 + j, 64:, :] = dv[:, 128 * j : 128 * (j + 1)]

    def sib_own(yy):
        return copy(dkv.at[at(x, yy, 1 - c)], sibo.at[yy], so_s.at[yy], so_r.at[yy], ctx=sib)

    def sib_cross(yy):
        return copy(dkv.at[at(0, yy, 1 - c)], sibx.at[yy], sx_s.at[yy], sx_r.at[yy], ctx=sib)

    def cross(yy):
        return copy(sx.at[yy], rx.at[yy], xx_s.at[yy], xx_r.at[yy], ctx=at(1 - x, y, c))

    def cross_sums(t):
        for e in range(2):
            i = 2 * t + e
            sib_cross(i).wait_recv()
            sx[i] = (dkv[at(0, i, c)] + sibx[i]).astype(BF16)
            cross(i).start()

    def retq_copy(i):
        return copy(sretq.at[i], rretq.at[y], retq_s.at[i], retq_r.at[y], ctx=at(x, i, c))

    def ret_copy(i):
        return copy(sret.at[i], rret.at[y], ret_s.at[i], ret_r.at[y], ctx=at(x, i, c))

    def send_dq(k):
        for i in (2 * k, 2 * k + 1):
            top = dq[i * 128 : i * 128 + 64] * 0.0625
            bottom = dq[i * 128 + 64 : i * 128 + 128] * 0.0625
            sretq[i] = jnp.where(half, top, swap(bottom)).astype(BF16)

            @pl.when(y == i)
            def _():
                rretq[y] = sretq[i]

            @pl.when(y != i)
            def _():
                retq_copy(i).start()

    def send_dkv(t, crossed):
        for i in (2 * t, 2 * t + 1):
            sib_own(i).wait_recv()
            total = dkv[at(x, i, c)] + sibo[i]
            if crossed:
                cross(i).wait_recv()
                total = total + rx[i].astype(F32)
            sret[i] = jnp.transpose(total).astype(BF16)

            @pl.when(y == i)
            def _():
                rret[y] = sret[i]

            @pl.when(y != i)
            def _():
                ret_copy(i).start()


    @pl.when(x == 1)
    def _():
        @pl.loop(0, T)
        def _(t):
            bwd(0, t, False)
            for e in range(2):
                sib_cross(2 * t + e).start()

            @pl.when(t > 0)
            def _():
                cross_sums(t - 1)

    steps = [T - 1] + list(range(T - 1))
    for n, t in enumerate(steps):
        bwd(t, x * T + t, True)
        for i in (2 * t, 2 * t + 1):
            sib_own(i).start()
        if n == 0:

            @pl.when(x == 1)
            def _():
                cross_sums(T - 1)

            g_histories()
        else:
            send_dq(t)

            @pl.when(x == 1)
            def _():
                send_dkv(steps[n - 1], False)
        if n == 1 or T == 1:
            g_pair()
    send_dq(T - 1)


    @pl.when(x == 1)
    def _():
        send_dkv(steps[-1], False)

    @pl.when(x == 0)
    def _():
        for t in range(T):
            send_dkv(t, True)

    g_chips()

    for d in near_first:
        yy = yo(d)
        copy(sretq.at[yy], rretq.at[yy], retq_s.at[yy], retq_r.at[yy], ctx=at(x, yy, c)).wait_recv()
    for j in range(NY // 2):
        cols = slice(2 * D + 128 * j, 2 * D + 128 * (j + 1))
        d_q = unpack_pair(rretq[2 * j].astype(F32), rretq[2 * j + 1].astype(F32))
        dpre[:, cols] = (d_q * slope(pre[:, cols])).astype(BF16)
    dout[...] += dot_nt(dpre[:, 2 * D : 3 * D], w_in_ref[:, 2 * D : 3 * D])

    copy(gfin.at[1 - c], gfin.at[1 - c], g4_s.at[0], g4_r.at[0], ctx=sib).wait_recv()
    d_total = jnp.concatenate([gfin[0], gfin[1]], axis=1)
    nf = neg_ref[...].astype(F32)
    scale = lax.rsqrt(jnp.sum(nf * nf, axis=1, keepdims=True) + 1e-06)
    unit = nf * scale
    dneg_ref[...] = scale * (d_total - unit * jnp.sum(unit * d_total, axis=1, keepdims=True))

    for d in near_first:
        yy = yo(d)
        copy(sret.at[yy], rret.at[yy], ret_s.at[yy], ret_r.at[yy], ctx=at(x, yy, c)).wait_recv()
    for j in range(NY // 2):
        even, odd = rret[2 * j].astype(F32), rret[2 * j + 1].astype(F32)
        cols = slice(3 * D + 128 * j, 3 * D + 128 * (j + 1))
        dpre[:, cols] = (jnp.where(lo, even, swap(odd)) * slope(pre[:, cols])).astype(BF16)
        cols = slice(D + 128 * j, D + 128 * (j + 1))
        dpre[:, cols] = (jnp.where(lo, swap(even), odd) * slope(pre[:, cols])).astype(BF16)
    d_seq = dout[...] + dot_nt(dpre[:, D : 2 * D], w_in_ref[:, D : 2 * D])
    dseq_ref[0] = (d_seq + dot_nt(dpre[:, 3 * D :], w_in_ref[:, 3 * D :])).astype(BF16)

    for d in range(1, NY):
        kv_copy(d).wait_send()
        q_copy(d).wait_send()
        mix_copy(yo(d)).wait_send()
        dm_copy(d).wait_send()
        retq_copy(yo(d)).wait_send()
        ret_copy(yo(d)).wait_send()
    for i in range(NY):
        relay(i).wait_send()
        sib_own(i).wait_send()
    for d in range(1, NB):
        neg_copy(d).wait_send()
        gb_copy(d).wait_send()
    for d, xx in peers:
        gc_copy(d, xx).wait_send()
    g1_copy().wait_send()
    g4_copy().wait_send()

    @pl.when(x == 0)
    def _():
        for i in range(NY):
            forward(i).wait_send()

    @pl.when(x == 1)
    def _():
        for i in range(NY):
            cross_relay(i, c).wait_send()
            sib_cross(i).wait_send()
            cross(i).wait_send()


def solution(mesh):
    NY = mesh.shape["ctx"] // 4
    NB = mesh.shape["batch"]
    D = HEAD * NY
    V, S = pltpu.VMEM, pltpu.SemaphoreType.DMA

    def body(*refs):
        kernel(NY, NB, *refs)

    def shards(seq_in, w_in, w_out, pos_emb, pos_ids, neg_emb, neg_ids, neg_counts):
        vm = pl.BlockSpec(memory_space=pltpu.VMEM)
        return pl.pallas_call(
            body,
            out_shape=(
                jax.ShapeDtypeStruct((1, ROWS), F32),
                jax.ShapeDtypeStruct((1, ROWS, D), BF16),
                jax.ShapeDtypeStruct((8, D), F32),
            ),
            in_specs=[pl.BlockSpec(memory_space=pltpu.HBM)] * 8,
            out_specs=(vm, vm, vm),
            scratch_shapes=[
                V((1, ROWS, D), BF16),
                V((D, 4 * D), BF16),
                V((D, D), BF16),
                V((1, ROWS, D), BF16),
                V((1, ROWS), I32),
                V((8, D), BF16),
                pltpu.SMEM((8,), I32),
                pltpu.SMEM((8,), I32),
                S((9,)),
                V((ROWS, 4 * D), F32),
                V((NY, 128, 128), BF16),
                V((NY, 64, 128), BF16),
                V((4 * NY, 128, 128), BF16),
                V((NY, 64, 128), BF16),
                V((NY * 128, 128), BF16),
                V((NY * 128, 128), F32),
                V((NY, 64, 128), BF16),
                V((NY, 64, 128), BF16),
                V((NY, 64, 128), BF16),
                V((NY, 64, 128), BF16),
                V((NY * 128, 128), BF16),
                V((128, NY * 128), BF16),
                V((NY * 128, 128), F32),
                V((4 * NY, 128, 128), F32),
                V((NY, 128, 128), F32),
                V((NY, 128, 128), F32),
                V((NY, 128, 128), BF16),
                V((NY, 128, 128), BF16),
                V((NY, 128, 128), BF16),
                V((NY, 128, 128), BF16),
                V((NY, 64, 128), BF16),
                V((NY, 64, 128), BF16),
                V((ROWS, D), F32),
                V((ROWS, 4 * D), BF16),
                V((8, D + 128), F32),
                V((NB, 8, D + 128), F32),
                V((NB, 8, D), F32),
                V((NB, 8, D), F32),
                V((8, D), F32),
                V((8, D), F32),
                V((8, D // 2), F32),
                V((2 * NY, 8, D // 2), F32),
                V((2, 8, D // 2), F32),
            ]
            + [S((NY,))] * 24
            + [S((NB,))] * 4
            + [S((1,))] * 2
            + [S((2 * NY,))] * 2
            + [S((1,))] * 2,
            compiler_params=pltpu.CompilerParams(
                collective_id=0, has_side_effects=True, vmem_limit_bytes=60 << 20
            ),
        )(seq_in, w_in, w_out, pos_emb, pos_ids, neg_emb, neg_ids, neg_counts)

    in_specs = (
        P("batch", "ctx", None), P(), P(), P("batch", "ctx", None), P("batch", "ctx"),
        P("batch", None), P("batch"), P("batch"),
    )
    out_specs = (P("batch", "ctx"), P("batch", "ctx", None), P("batch", None))
    return jax.shard_map(shards, mesh=mesh, in_specs=in_specs, out_specs=out_specs, check_vma=False)
```

```python
import jax
import jax.numpy as jnp
from jax import lax
from jax.experimental import pallas as pl
from jax.experimental.pallas import tpu as pltpu
from jax.sharding import PartitionSpec as P

MESH = pl.DeviceIdType.MESH
F32, BF16, I32 = jnp.float32, jnp.bfloat16, jnp.int32
HEAD = 64
ROWS = 128
TEMPER_INV = 20.0


def dot_nn(a, b):
    return lax.dot_general(a, b, (((1,), (0,)), ((), ())), preferred_element_type=F32)


def dot_nt(a, b):
    return lax.dot_general(a, b, (((1,), (1,)), ((), ())), preferred_element_type=F32)


def swap(v):
    return pltpu.roll(v, 64, 1)


def low(shape):
    return lax.broadcasted_iota(I32, shape, 1) < HEAD


def slope(v):
    g = jax.nn.sigmoid(v)
    return g * (1.0 + v * (1.0 - g))


def pack_rows(tile, which):
    top, bottom = tile[:64], tile[64:]
    if which == 0:
        return jnp.where(low(top.shape), top, swap(bottom))
    return jnp.where(low(top.shape), swap(top), bottom)


def unpack_pair(even, odd):
    top = jnp.where(low(even.shape), even, swap(odd))
    bottom = jnp.where(low(even.shape), swap(even), odd)
    return jnp.concatenate([top, bottom], axis=0)


def kernel(
    NY, NB,
    seq_hbm, w_in_hbm, w_out_hbm, pos_hbm, pid_hbm, neg_hbm, nid_hbm, ncnt_hbm,
    loss_ref, dseq_ref, dneg_ref,
    seq_ref, w_in_ref, w_out_ref, pos_ref, pid_ref, neg_ref, nid_ref, ncnt_ref, in_s,
    pre, skv, sq, kv, rq, qz, acc, smix, rmix, sdm, rdm, dmz, qdt, dq, dkv,
    sibo, sibx, sx, rx, sxq, rxq, smx, rmx, sret, rret, sretq, rretq, dout, dpre, negs, nega, gsend, grecv, g1, g2, g3, g4, gfin,
    kv_s, kv_r, q_s, q_r, rel_s, rel_r, xf_s, xf_r, xr_s, xr_r, mix_s, mix_r, dm_s, dm_r,
    qf_s, qf_r, mx_s, mx_r, df_s, df_r, xq_s, xq_r, so_s, so_r, sx_s, sx_r, xx_s, xx_r, ret_s, ret_r, retq_s, retq_r,
    neg_s, neg_r, gb_s, gb_r, g1_s, g1_r, gc_s, gc_r, g4_s, g4_r, hello,
):
    D = HEAD * NY
    T = NY // 2
    me = lax.axis_index("ctx")
    b = lax.axis_index("batch")
    c = lax.rem(me, 2)
    y = lax.rem(lax.div(me, 2), NY)
    x = lax.div(me, 2 * NY)

    def at(xx, yy, cc):
        return (xx * NY + yy) * 2 + cc

    def yo(d):
        return lax.rem(y + d, NY)

    def bo(d):
        return lax.rem(b + d, NB)

    sib = at(x, y, 1 - c)
    others = [at(x, yo(d), c) for d in range(1, NY)]
    across = [at(1 - x, yo(d), c) for d in range(NY)]

    def copy(src, dst, ss, rs, ctx=None, batch=None):
        where = {"ctx": ctx} if batch is None else {"batch": batch}
        return pltpu.make_async_remote_copy(
            src_ref=src, dst_ref=dst, send_sem=ss, recv_sem=rs, device_id=where, device_id_type=MESH
        )


    loads = [
        pltpu.make_async_copy(src, dst, in_s.at[i])
        for i, (src, dst) in enumerate(
            [
                (seq_hbm, seq_ref),
                (w_in_hbm.at[:, D:], w_in_ref.at[:, D:]),
                (w_in_hbm.at[:, :D], w_in_ref.at[:, :D]),
                (neg_hbm, neg_ref),
                (nid_hbm, nid_ref),
                (ncnt_hbm, ncnt_ref),
                (pos_hbm, pos_ref),
                (pid_hbm, pid_ref),
                (w_out_hbm, w_out_ref),
            ]
        )
    ]
    for load in loads:
        load.start()
    barrier = pltpu.get_barrier_semaphore()
    for p in [sib] + others + across:
        pl.semaphore_signal(barrier, inc=1, device_id={"ctx": p}, device_id_type=MESH)
    for d in range(1, NB):

        @pl.when(bo(d) > b)
        def _():
            pl.semaphore_signal(barrier, inc=1, device_id={"batch": bo(d)}, device_id_type=MESH)


    loads[0].wait()
    loads[1].wait()
    xin = seq_ref[0]
    lane = lax.broadcasted_iota(I32, (ROWS, 128), 1)
    lo = lane < HEAD

    for j in range(NY // 2):
        cols = [slice(p * D + 128 * j, p * D + 128 * (j + 1)) for p in range(4)]
        tiles = []
        for p in (1, 2, 3):
            v = dot_nn(xin, w_in_ref[:, cols[p]])
            pre[:, cols[p]] = v
            tiles.append(jax.nn.silu(v))
        vt, qt, kt = tiles
        skv[2 * j] = jnp.where(lo, kt, swap(vt)).astype(BF16)
        skv[2 * j + 1] = jnp.where(lo, swap(kt), vt).astype(BF16)
        qt = qt * 0.0625
        sq[2 * j] = pack_rows(qt, 0).astype(BF16)
        sq[2 * j + 1] = pack_rows(qt, 1).astype(BF16)

    for load in loads[2:]:
        load.wait()
    negs[:, :D] = neg_ref[...].astype(F32)
    meta_lane = lax.broadcasted_iota(I32, (8, 128), 1)
    meta_row = lax.broadcasted_iota(I32, (8, 128), 0)
    meta = jnp.zeros((8, 128), F32)
    for i in range(8):
        here = meta_lane == b * 8 + i
        meta = meta + jnp.where(
            jnp.logical_and(here, meta_row == 0), nid_ref[i].astype(F32),
            jnp.where(jnp.logical_and(here, meta_row == 1), ncnt_ref[i].astype(F32), 0.0),
        )
    negs[:, D:] = meta

    pl.semaphore_wait(barrier, 1 + (NY - 1) + NY + b)

    def kv_copy(d):
        h = yo(d)
        return copy(skv.at[h], kv.at[me], kv_s.at[h], kv_r.at[y], ctx=at(x, h, c))

    def q_copy(d):
        h = yo(d)
        return copy(sq.at[h], rq.at[y], q_s.at[h], q_r.at[y], ctx=at(x, h, c))

    far_first = sorted(range(1, NY), key=lambda d: -min(d, NY - d))
    for d in far_first:
        kv_copy(d).start()
        q_copy(d).start()
    kv[me] = skv[y]
    rq[y] = sq[y]

    def relay(yy):
        r = at(x, yy, c)
        return copy(kv.at[r], kv.at[r], rel_s.at[yy], rel_r.at[yy], ctx=sib)

    def own_relay():
        return copy(skv.at[y], kv.at[me], rel_s.at[y], rel_r.at[y], ctx=sib)

    E = NY // 2

    def forward(yy):
        r = at(0, yy, c)
        return copy(kv.at[r], kv.at[r], xf_s.at[yy], xf_r.at[yy], ctx=at(1 - x, y, c))

    def q_forward(i):
        return copy(rq.at[i], rq.at[NY + i], qf_s.at[i], qf_r.at[i], ctx=at(1 - x, y, c))

    own_relay().start()

    @pl.when(jnp.logical_and(x == 0, y >= E))
    def _():
        copy(skv.at[y], kv.at[me], xf_s.at[y], xf_r.at[y], ctx=at(1 - x, y, c)).start()

    @pl.when(x == 1)
    def _():
        copy(sq.at[y], rq.at[NY + y], qf_s.at[y], qf_r.at[y], ctx=at(1 - x, y, c)).start()

    def neg_copy(d):
        return copy(negs, nega.at[b], neg_s.at[d], neg_r.at[b], batch=bo(d))

    for d in range(1, NB):

        @pl.when(bo(d) < b)
        def _():
            pl.semaphore_signal(hello, inc=1, device_id={"batch": bo(d)}, device_id_type=MESH)
            neg_copy(d).start()

    nega[b] = negs[...]

    g_pre = dot_nn(xin, w_in_ref[:, :D])
    pre[:, :D] = g_pre

    near_first = far_first[::-1]
    for d in near_first:
        yy = yo(d)
        copy(skv.at[yy], kv.at[at(x, yy, c)], kv_s.at[yy], kv_r.at[yy], ctx=at(x, yy, c)).wait_recv()
        relay(yy).start()

        @pl.when(jnp.logical_and(x == 0, yy >= E))
        def _():
            forward(yy).start()

        copy(sq.at[yy], rq.at[yy], q_s.at[yy], q_r.at[yy], ctx=at(x, yy, c)).wait_recv()

        @pl.when(x == 1)
        def _():
            q_forward(yy).start()

    half = low((64, 128))

    @pl.when(b < NB - 1)
    def _():
        pl.semaphore_wait(hello, NB - 1 - b)

    for d in range(1, NB):

        @pl.when(bo(d) > b)
        def _():
            neg_copy(d).start()


    def take_q(i):
        v = rq[i].astype(F32)
        qz[i * 128 : i * 128 + 64] = jnp.where(half, v, 0.0).astype(BF16)
        qz[i * 128 + 64 : i * 128 + 128] = jnp.where(half, swap(v), 0.0).astype(BF16)

    for i in range(NY):
        take_q(i)
    for d in range(NY):
        yy = yo(d)
        r = at(x, yy, 1 - c)
        copy(kv.at[r], kv.at[r], rel_s.at[yy], rel_r.at[yy], ctx=sib).wait_recv()

    def keys_of(t):
        return kv[pl.ds(t * 4, 4)].reshape(512, 128)

    def allowed():
        i = lax.broadcasted_iota(I32, (256, 512), 0)
        j = lax.broadcasted_iota(I32, (256, 512), 1)
        return j <= i + jnp.where(i >= 128, 128, 0) + c * 128

    def weighted(q, tile, diagonal):
        h = dot_nt(q, tile)
        w = h + h * jnp.tanh(h)
        if diagonal:
            last = jnp.where(allowed(), w[:, -512:], 0.0)
            w = last if w.shape[1] == 512 else jnp.concatenate([w[:, :-512], last], axis=1)
        return dot_nn(w.astype(BF16), tile)

    def mix_copy(i):
        return copy(smix.at[i], rmix.at[y], mix_s.at[i], mix_r.at[y], ctx=at(x, i, c))

    def pack_mixed(rows, e):
        top, bottom = rows[e * 128 : e * 128 + 64], rows[e * 128 + 64 : e * 128 + 128]
        return jnp.where(half, swap(top), bottom)

    def send_mixed(i, packed):
        smix[i] = packed.astype(BF16)

        @pl.when(y == i)
        def _():
            rmix[y] = smix[i]

        @pl.when(y != i)
        def _():
            mix_copy(i).start()

    def mix_cross(i):
        return copy(smx.at[i], rmx.at[i], mx_s.at[i], mx_r.at[i], ctx=at(1 - x, y, c))

    def cross_in(yy):
        r = at(0, yy, c)
        return copy(kv.at[r], kv.at[r], xf_s.at[yy], xf_r.at[yy], ctx=at(1 - x, y, c))

    def cross_relay(yy, cc):
        r = at(0, yy, cc)
        return copy(kv.at[r], kv.at[r], xr_s.at[yy], xr_r.at[yy], ctx=sib)

    for k in range(T):
        if k == T - 1:

            @pl.when(x == 1)
            def _():
                for i in range(E, NY):
                    cross_in(i).wait_recv()
                    cross_relay(i, c).start()

        tile = kv[pl.ds(x * 2 * NY, 4 * (k + 1))].reshape(512 * (k + 1), 128)
        rows = weighted(qz[256 * k : 256 * (k + 1)], tile, True)

        @pl.when(x == 0)
        def _():
            for e in range(2):
                send_mixed(2 * k + e, pack_mixed(rows, e))

        @pl.when(x == 1)
        def _():
            acc[256 * k : 256 * (k + 1)] = rows

    W = 128 * T

    @pl.when(x == 0)
    def _():
        for i in range(NY):
            q_forward(i).wait_recv()
            take_q(NY + i)
        tile = kv[:NY].reshape(128 * NY, 128)
        for n in range(2):
            rows = weighted(qz[256 * T + W * n : 256 * T + W * (n + 1)], tile, False)
            for e in range(T):
                smx[n * T + e] = pack_mixed(rows, e).astype(BF16)
                mix_cross(n * T + e).start()

    @pl.when(x == 1)
    def _():
        for i in range(E, NY):
            cross_relay(i, 1 - c).wait_recv()
        tile = kv[NY : 2 * NY].reshape(128 * NY, 128)
        for n in range(2):
            piece = slice(W * n, W * (n + 1))
            acc[piece] += weighted(qz[piece], tile, False)
        for i in range(NY):
            mix_cross(i).wait_recv()
            send_mixed(i, pack_mixed(acc[i * 128 : (i + 1) * 128], 0) + rmx[i].astype(F32))

    for d in range(1, NB):
        bb = bo(d)
        copy(negs, nega.at[bb], neg_s.at[d], neg_r.at[bb], batch=bb).wait_recv()
    NEG = 8 * NB
    neg_f = nega[:, :, :D].reshape(NEG, D)
    neg_b = (neg_f * lax.rsqrt(jnp.sum(neg_f * neg_f, axis=1, keepdims=True) + 1e-06)).astype(BF16)
    metas = nega[0, :, D:]
    for i in range(1, NB):
        metas = metas + nega[i, :, D:]
    ids = metas[0:1, :NEG]
    counts = metas[1:2, :NEG]
    log_share = jnp.log(NEG * counts / jnp.sum(counts, axis=1, keepdims=True))
    pid = jnp.transpose(jnp.broadcast_to(pid_ref[...].astype(F32), (NEG, ROWS)))
    same = pid == ids
    posf = pos_ref[0].astype(F32)
    pos_unit = posf * lax.rsqrt(jnp.sum(posf * posf, axis=1, keepdims=True) + 1e-06)
    gate_u = jax.nn.silu(pre[:, :D]).astype(BF16).astype(F32)

    for d in near_first:
        yy = yo(d)
        copy(smix.at[yy], rmix.at[yy], mix_s.at[yy], mix_r.at[yy], ctx=at(x, yy, c)).wait_recv()
    mixed = jnp.concatenate(
        [unpack_pair(rmix[2 * j].astype(F32), rmix[2 * j + 1].astype(F32)) for j in range(NY // 2)], axis=1
    )
    centred = mixed - jnp.mean(mixed, axis=1, keepdims=True)
    inv_std = lax.rsqrt(jnp.mean(centred * centred, axis=1, keepdims=True) + 1e-05)
    normed = centred * inv_std
    gated = (normed * gate_u).astype(BF16)
    outputs = xin.astype(F32) + dot_nn(gated, w_out_ref[...])
    out_scale = lax.rsqrt(jnp.sum(outputs * outputs, axis=1, keepdims=True) + 1e-06)
    user = outputs * out_scale
    user_b = user.astype(BF16)
    positive = jnp.sum(user * pos_unit, axis=1, keepdims=True) * TEMPER_INV
    logits = dot_nt(user_b, neg_b) * TEMPER_INV - log_share
    terms = jnp.where(same, 0.0, jnp.exp(logits))
    pos_exp = jnp.exp(positive)
    denom = pos_exp + jnp.sum(terms, axis=1, keepdims=True)
    loss = jnp.log(denom) - positive
    d_pos = pos_exp / denom - 1.0
    probs = terms / denom
    probs_b = probs.astype(BF16)
    d_user = (d_pos * TEMPER_INV) * pos_unit + dot_nn(probs_b, neg_b) * TEMPER_INV
    d_out = out_scale * (d_user - user * jnp.sum(user * d_user, axis=1, keepdims=True))
    d_gated = dot_nt(d_out.astype(BF16), w_out_ref[...])
    d_normed = d_gated * gate_u
    d_gate = d_gated * normed
    d_mixed = inv_std * (
        d_normed
        - jnp.mean(d_normed, axis=1, keepdims=True)
        - normed * jnp.mean(d_normed * normed, axis=1, keepdims=True)
    )
    for j in range(NY // 2):
        tile = d_mixed[:, 128 * j : 128 * (j + 1)]
        sdm[2 * j] = pack_rows(tile, 0).astype(BF16)
        sdm[2 * j + 1] = pack_rows(tile, 1).astype(BF16)

    def dm_copy(d):
        yy = yo(d)
        return copy(sdm.at[yy], rdm.at[y], dm_s.at[yy], dm_r.at[y], ctx=at(x, yy, c))

    for d in far_first:
        dm_copy(d).start()
    rdm[y] = sdm[y]

    d_pre = (d_gate * slope(pre[:, :D])).astype(BF16)
    dout[...] = d_out + dot_nt(d_pre, w_in_ref[:, :D])
    loss_ref[...] = jnp.transpose(jnp.broadcast_to(loss, (ROWS, 128)))[0:1, :]
    grad = dot_nn(jnp.transpose(probs).astype(BF16), user_b) * TEMPER_INV
    for j in range(D // 256):
        pair = [grad[:, 256 * j + 128 * e : 256 * j + 128 * (e + 1)].reshape(NB, 8, 128) for e in range(2)]
        gsend[:, 16 * j : 16 * (j + 1), :] = jnp.concatenate(pair, axis=1).astype(BF16)

    def gb_copy(d):
        bb = bo(d)
        return copy(gsend.at[bb], grecv.at[b], gb_s.at[d], gb_r.at[b], batch=bb)

    for d in range(1, NB):
        gb_copy(d).start()
    grecv[b] = gsend[b]
    dq[...] = jnp.zeros_like(dq)

    def dm_forward(i):
        return copy(rdm.at[i], rdm.at[NY + i], df_s.at[i], df_r.at[i], ctx=at(1 - x, y, c))

    def pass_dm(i):
        @pl.when(x == 1)
        def _():
            dm_forward(i).start()

    pass_dm(y)
    for d in near_first:
        yy = yo(d)
        copy(sdm.at[yy], rdm.at[yy], dm_s.at[yy], dm_r.at[yy], ctx=at(x, yy, c)).wait_recv()
        pass_dm(yy)

    def take_dm(i):
        v = rdm[i].astype(F32)
        up = jnp.concatenate([jnp.where(half, 0.0, swap(v)), jnp.where(half, 0.0, v)], axis=0)
        dmz[i * 128 : i * 128 + 128] = up.astype(BF16)
        both = up + qz[i * 128 : i * 128 + 128].astype(F32)
        qdt[:, i * 128 : i * 128 + 128] = jnp.transpose(both).astype(BF16)

    for i in range(NY):
        take_dm(i)

    def g1_copy():
        return copy(g1, g2, g1_s.at[0], g1_r.at[0], ctx=sib)

    def gc_copy(d, xx):
        there = x if xx == 0 else 1 - x
        return copy(
            g3, g4.at[x * NY + y], gc_s.at[xx * NY + d], gc_r.at[x * NY + y], ctx=at(there, yo(d), c)
        )

    def g4_copy():
        return copy(gfin.at[c], gfin.at[c], g4_s.at[0], g4_r.at[0], ctx=sib)

    peers = [(d, 0) for d in range(1, NY)] + [(d, 1) for d in range(NY)]
    H = D // 32

    def g_histories():
        for d in range(1, NB):
            bb = bo(d)
            copy(gsend.at[bb], grecv.at[bb], gb_s.at[d], gb_r.at[bb], batch=bb).wait_recv()
        g1[...] = jnp.sum(grecv[...].astype(F32), axis=0)
        g1_copy().start()

    def g_pair():
        g1_copy().wait_recv()
        gsum = g1[...] + g2[...]
        g3[...] = jnp.where(c == 0, gsum[:H], gsum[H:]).astype(BF16)
        for d, xx in peers:
            gc_copy(d, xx).start()
        g4[x * NY + y] = g3[...]

    def g_chips():
        for d, xx in peers:
            s = (x if xx == 0 else 1 - x) * NY + yo(d)
            copy(g3, g4.at[s], gc_s.at[xx * NY + d], gc_r.at[s], ctx=sib).wait_recv()
        gfin[c] = jnp.sum(g4[...].astype(F32), axis=0)
        g4_copy().start()

    def bwd(rows, block, blocks, diagonal, more):
        tile = kv[pl.ds(block, blocks)].reshape(128 * blocks, 128)
        h = dot_nt(qz[rows], tile)
        dw = dot_nt(dmz[rows], tile)
        th = jnp.tanh(h)
        u = 1.0 + th
        w = h * u
        ds = dw * (u + w * (1.0 - th))
        if diagonal:
            ok = allowed()

            def masked(v):
                first = jnp.where(ok, v[:256], 0.0)
                return first if v.shape[0] == 256 else jnp.concatenate([first, v[256:]], axis=0)

            w, ds = masked(w), masked(ds)
        w = w.astype(BF16)
        ds = ds.astype(BF16)
        dq[rows] += dot_nn(ds, tile)
        dk = dot_nn(qdt[:64, rows], ds)
        dv = dot_nn(qdt[64:, rows], w)
        for j in range(blocks):
            one = slice(128 * j, 128 * (j + 1))
            if more:
                dkv[block + j, :64, :] += dk[:, one]
                dkv[block + j, 64:, :] += dv[:, one]
            else:
                dkv[block + j, :64, :] = dk[:, one]
                dkv[block + j, 64:, :] = dv[:, one]

    def sib_own(yy):
        return copy(dkv.at[at(x, yy, 1 - c)], sibo.at[yy], so_s.at[yy], so_r.at[yy], ctx=sib)

    def sib_cross(yy):
        return copy(dkv.at[at(0, yy, 1 - c)], sibx.at[yy], sx_s.at[yy], sx_r.at[yy], ctx=sib)

    def cross(yy):
        return copy(sx.at[yy], rx.at[yy], xx_s.at[yy], xx_r.at[yy], ctx=at(1 - x, y, c))

    def cross_sums(t):
        for e in range(2):
            i = 2 * t + e
            sib_cross(i).wait_recv()
            sx[i] = (dkv[at(0, i, c)] + sibx[i]).astype(BF16)
            cross(i).start()

    def retq_copy(i):
        return copy(sretq.at[i], rretq.at[y], retq_s.at[i], retq_r.at[y], ctx=at(x, i, c))

    def ret_copy(i):
        return copy(sret.at[i], rret.at[y], ret_s.at[i], ret_r.at[y], ctx=at(x, i, c))

    def pack_dq(i):
        top = dq[i * 128 : i * 128 + 64] * 0.0625
        bottom = dq[i * 128 + 64 : i * 128 + 128] * 0.0625
        return jnp.where(half, top, swap(bottom))

    def send_dq(k, crossed):
        for i in (2 * k, 2 * k + 1):
            mine = pack_dq(i)
            if crossed:
                dq_cross(i).wait_recv()
                mine = mine + rxq[i].astype(F32)
            sretq[i] = mine.astype(BF16)

            @pl.when(y == i)
            def _():
                rretq[y] = sretq[i]

            @pl.when(y != i)
            def _():
                retq_copy(i).start()

    def dq_cross(i):
        return copy(sxq.at[i], rxq.at[i], xq_s.at[i], xq_r.at[i], ctx=at(1 - x, y, c))

    def send_dkv(t, crossed):
        for i in (2 * t, 2 * t + 1):
            sib_own(i).wait_recv()
            total = dkv[at(x, i, c)] + sibo[i]
            if crossed:
                cross(i).wait_recv()
                total = total + rx[i].astype(F32)
            sret[i] = jnp.transpose(total).astype(BF16)

            @pl.when(y == i)
            def _():
                rret[y] = sret[i]

            @pl.when(y != i)
            def _():
                ret_copy(i).start()


    HALF = T // 2
    every = slice(0, 256 * T)

    @pl.when(x == 1)
    def _():
        for t in range(HALF, T):
            bwd(every, 4 * t, 4, False, False)
            for e in range(2):
                sib_cross(2 * t + e).start()
            if t > HALF:
                cross_sums(t - 1)

    for t in range(T):
        bwd(slice(256 * t, 256 * T), (x * T + t) * 4, 4, True, False)

        @pl.when(jnp.logical_or(x == 1, t >= HALF))
        def _():
            for e in range(2):
                sib_own(2 * t + e).start()

        @pl.when(x == 1)
        def _():
            if t == 0:
                cross_sums(T - 1)
            else:
                send_dkv(t - 1, False)

        @pl.when(x == 0)
        def _():
            send_dq(t, False)

    g_histories()


    @pl.when(x == 0)
    def _():
        for i in range(NY):
            dm_forward(i).wait_recv()
            take_dm(NY + i)
        for n in range(2):
            bwd(slice(256 * T + 128 * T * n, 256 * T + 128 * T * (n + 1)), 0, 4 * HALF, False, True)
            for e in range(T):
                i = n * T + e
                sxq[i] = pack_dq(NY + i).astype(BF16)
                dq_cross(i).start()
        for i in range(2 * HALF):
            sib_own(i).start()


    @pl.when(x == 1)
    def _():
        send_dkv(T - 1, False)

    g_pair()

    @pl.when(x == 1)
    def _():
        for k in range(T):
            send_dq(k, True)

    @pl.when(x == 0)
    def _():
        for t in list(range(HALF, T)) + list(range(HALF)):
            send_dkv(t, t >= HALF)

    def finish_dq():
        for d in near_first:
            yy = yo(d)
            copy(sretq.at[yy], rretq.at[yy], retq_s.at[yy], retq_r.at[yy], ctx=at(x, yy, c)).wait_recv()
        for j in range(NY // 2):
            cols = slice(2 * D + 128 * j, 2 * D + 128 * (j + 1))
            d_q = unpack_pair(rretq[2 * j].astype(F32), rretq[2 * j + 1].astype(F32))
            dpre[:, cols] = (d_q * slope(pre[:, cols])).astype(BF16)
        dout[...] += dot_nt(dpre[:, 2 * D : 3 * D], w_in_ref[:, 2 * D : 3 * D])


    @pl.when(x == 0)
    def _():
        finish_dq()

    for d in near_first:
        yy = yo(d)
        copy(sret.at[yy], rret.at[yy], ret_s.at[yy], ret_r.at[yy], ctx=at(x, yy, c)).wait_recv()
    for j in range(NY // 2):
        even, odd = rret[2 * j].astype(F32), rret[2 * j + 1].astype(F32)
        cols = slice(3 * D + 128 * j, 3 * D + 128 * (j + 1))
        dpre[:, cols] = (jnp.where(lo, even, swap(odd)) * slope(pre[:, cols])).astype(BF16)
        cols = slice(D + 128 * j, D + 128 * (j + 1))
        dpre[:, cols] = (jnp.where(lo, swap(even), odd) * slope(pre[:, cols])).astype(BF16)
    dout[...] += dot_nt(dpre[:, D : 2 * D], w_in_ref[:, D : 2 * D]) + dot_nt(dpre[:, 3 * D :], w_in_ref[:, 3 * D :])
    g_chips()

    @pl.when(x == 1)
    def _():
        finish_dq()

    dseq_ref[0] = dout[...].astype(BF16)

    copy(gfin.at[1 - c], gfin.at[1 - c], g4_s.at[0], g4_r.at[0], ctx=sib).wait_recv()
    d_total = jnp.concatenate([gfin[e // (H // 8), 8 * (e % (H // 8)) : 8 * (e % (H // 8)) + 8] for e in range(D // 128)], axis=1)
    nf = neg_ref[...].astype(F32)
    scale = lax.rsqrt(jnp.sum(nf * nf, axis=1, keepdims=True) + 1e-06)
    unit = nf * scale
    dneg_ref[...] = scale * (d_total - unit * jnp.sum(unit * d_total, axis=1, keepdims=True))

    for d in range(1, NY):
        kv_copy(d).wait_send()
        q_copy(d).wait_send()
        mix_copy(yo(d)).wait_send()
        dm_copy(d).wait_send()
        retq_copy(yo(d)).wait_send()
        ret_copy(yo(d)).wait_send()
    for i in range(NY):
        relay(i).wait_send()
        sib_own(i).wait_send()
    for d in range(1, NB):
        neg_copy(d).wait_send()
        gb_copy(d).wait_send()
    for d, xx in peers:
        gc_copy(d, xx).wait_send()
    g1_copy().wait_send()
    g4_copy().wait_send()

    @pl.when(x == 0)
    def _():
        for i in range(NY):
            mix_cross(i).wait_send()
            dq_cross(i).wait_send()
        for i in range(E, NY):
            forward(i).wait_send()

    @pl.when(x == 1)
    def _():
        for i in range(NY):
            q_forward(i).wait_send()
            dm_forward(i).wait_send()
        for i in range(2 * HALF, NY):
            sib_cross(i).wait_send()
            cross(i).wait_send()
            cross_relay(i, c).wait_send()


def solution(mesh):
    NY = mesh.shape["ctx"] // 4
    NB = mesh.shape["batch"]
    D = HEAD * NY
    V, S = pltpu.VMEM, pltpu.SemaphoreType.DMA

    def body(*refs):
        kernel(NY, NB, *refs)

    def shards(seq_in, w_in, w_out, pos_emb, pos_ids, neg_emb, neg_ids, neg_counts):
        vm = pl.BlockSpec(memory_space=pltpu.VMEM)
        return pl.pallas_call(
            body,
            out_shape=(
                jax.ShapeDtypeStruct((1, ROWS), F32),
                jax.ShapeDtypeStruct((1, ROWS, D), BF16),
                jax.ShapeDtypeStruct((8, D), F32),
            ),
            in_specs=[pl.BlockSpec(memory_space=pltpu.HBM)] * 8,
            out_specs=(vm, vm, vm),
            scratch_shapes=[
                V((1, ROWS, D), BF16),
                V((D, 4 * D), BF16),
                V((D, D), BF16),
                V((1, ROWS, D), BF16),
                V((1, ROWS), I32),
                V((8, D), BF16),
                pltpu.SMEM((8,), I32),
                pltpu.SMEM((8,), I32),
                S((9,)),
                V((ROWS, 4 * D), F32),
                V((NY, 128, 128), BF16),
                V((NY, 64, 128), BF16),
                V((4 * NY, 128, 128), BF16),
                V((2 * NY, 64, 128), BF16),
                V((NY * 256, 128), BF16),
                V((NY * 128, 128), F32),
                V((NY, 64, 128), BF16),
                V((NY, 64, 128), BF16),
                V((NY, 64, 128), BF16),
                V((2 * NY, 64, 128), BF16),
                V((NY * 256, 128), BF16),
                V((128, NY * 256), BF16),
                V((NY * 256, 128), F32),
                V((4 * NY, 128, 128), F32),
                V((NY, 128, 128), F32),
                V((NY, 128, 128), F32),
                V((NY, 128, 128), BF16),
                V((NY, 128, 128), BF16),
                V((NY, 64, 128), BF16),
                V((NY, 64, 128), BF16),
                V((NY, 64, 128), BF16),
                V((NY, 64, 128), BF16),
                V((NY, 128, 128), BF16),
                V((NY, 128, 128), BF16),
                V((NY, 64, 128), BF16),
                V((NY, 64, 128), BF16),
                V((ROWS, D), F32),
                V((ROWS, 4 * D), BF16),
                V((8, D + 128), F32),
                V((NB, 8, D + 128), F32),
                V((NB, D // 16, 128), BF16),
                V((NB, D // 16, 128), BF16),
                V((D // 16, 128), F32),
                V((D // 16, 128), F32),
                V((D // 32, 128), BF16),
                V((2 * NY, D // 32, 128), BF16),
                V((2, D // 32, 128), F32),
            ]
            + [S((NY,))] * 32
            + [S((NB,))] * 4
            + [S((1,))] * 2
            + [S((2 * NY,))] * 2
            + [S((1,))] * 2
            + [pltpu.SemaphoreType.REGULAR],
            compiler_params=pltpu.CompilerParams(
                collective_id=0, has_side_effects=True, vmem_limit_bytes=60 << 20
            ),
        )(seq_in, w_in, w_out, pos_emb, pos_ids, neg_emb, neg_ids, neg_counts)

    in_specs = (
        P("batch", "ctx", None), P(), P(), P("batch", "ctx", None), P("batch", "ctx"),
        P("batch", None), P("batch"), P("batch"),
    )
    out_specs = (P("batch", "ctx"), P("batch", "ctx", None), P("batch", None))
    return jax.shard_map(shards, mesh=mesh, in_specs=in_specs, out_specs=out_specs, check_vma=False)
```

```python
import jax
import jax.numpy as jnp
from jax import lax
from jax.experimental import pallas as pl
from jax.experimental.pallas import tpu as pltpu
from jax.sharding import PartitionSpec as P

MESH = pl.DeviceIdType.MESH
F32, BF16, I32 = jnp.float32, jnp.bfloat16, jnp.int32
HEAD = 64
ROWS = 128
TEMPER_INV = 20.0


def dot_nn(a, b):
    return lax.dot_general(a, b, (((1,), (0,)), ((), ())), preferred_element_type=F32)


def dot_nt(a, b):
    return lax.dot_general(a, b, (((1,), (1,)), ((), ())), preferred_element_type=F32)


def swap(v):
    return pltpu.roll(v, 64, 1)


def low(shape):
    return lax.broadcasted_iota(I32, shape, 1) < HEAD


def slope(v):
    g = jax.nn.sigmoid(v)
    return g * (1.0 + v * (1.0 - g))


def pack_rows(tile, which):
    top, bottom = tile[:64], tile[64:]
    if which == 0:
        return jnp.where(low(top.shape), top, swap(bottom))
    return jnp.where(low(top.shape), swap(top), bottom)


def unpack_pair(even, odd):
    top = jnp.where(low(even.shape), even, swap(odd))
    bottom = jnp.where(low(even.shape), swap(even), odd)
    return jnp.concatenate([top, bottom], axis=0)


def kernel(
    NY, NB,
    seq_hbm, w_in_hbm, w_out_hbm, pos_hbm, pid_hbm, neg_hbm, nid_hbm, ncnt_hbm,
    loss_ref, dseq_ref, dneg_ref,
    seq_ref, w_in_ref, w_out_ref, pos_ref, pid_ref, neg_ref, nid_ref, ncnt_ref, in_s,
    pre, skv, sq, kv, rq, qz, acc, smix, rmix, sdm, rdm, dmz, qdt, dq, dkv,
    sibo, sibx, sx, rx, sxq, rxq, smx, rmx, sret, rret, sretq, rretq, dout, dpre, negs, nega, gsend, grecv, g1, g2, g3, g3x, gsum, g4, gfin,
    kv_s, kv_r, q_s, q_r, rel_s, rel_r, xf_s, xf_r, xr_s, xr_r, mix_s, mix_r, dm_s, dm_r,
    qf_s, qf_r, mx_s, mx_r, df_s, df_r, xq_s, xq_r, so_s, so_r, sx_s, sx_r, xx_s, xx_r, ret_s, ret_r, retq_s, retq_r,
    neg_s, neg_r, gb_s, gb_r, g1_s, g1_r, gc_s, gc_r, g4_s, g4_r, gx_s, gx_r, hello,
):
    D = HEAD * NY
    T = NY // 2
    me = lax.axis_index("ctx")
    b = lax.axis_index("batch")
    c = lax.rem(me, 2)
    y = lax.rem(lax.div(me, 2), NY)
    x = lax.div(me, 2 * NY)

    def at(xx, yy, cc):
        return (xx * NY + yy) * 2 + cc

    def yo(d):
        return lax.rem(y + d, NY)

    def bo(d):
        return lax.rem(b + d, NB)

    sib = at(x, y, 1 - c)
    others = [at(x, yo(d), c) for d in range(1, NY)]
    across = at(1 - x, y, c)

    def copy(src, dst, ss, rs, ctx=None, batch=None):
        where = {"ctx": ctx} if batch is None else {"batch": batch}
        return pltpu.make_async_remote_copy(
            src_ref=src, dst_ref=dst, send_sem=ss, recv_sem=rs, device_id=where, device_id_type=MESH
        )


    loads = [
        pltpu.make_async_copy(src, dst, in_s.at[i])
        for i, (src, dst) in enumerate(
            [
                (seq_hbm, seq_ref),
                *[
                    (w_in_hbm.at[pl.ds(r * D // 4, D // 4), D:], w_in_ref.at[pl.ds(r * D // 4, D // 4), D:])
                    for r in range(4)
                ],
                (w_in_hbm.at[:, :D], w_in_ref.at[:, :D]),
                (neg_hbm, neg_ref),
                (nid_hbm, nid_ref),
                (ncnt_hbm, ncnt_ref),
                (pos_hbm, pos_ref),
                (pid_hbm, pid_ref),
                (w_out_hbm, w_out_ref),
            ]
        )
    ]
    for load in loads:
        load.start()
    barrier = pltpu.get_barrier_semaphore()
    for p in [sib, across] + others:
        pl.semaphore_signal(barrier, inc=1, device_id={"ctx": p}, device_id_type=MESH)
    for d in range(1, NB):

        @pl.when(bo(d) > b)
        def _():
            pl.semaphore_signal(barrier, inc=1, device_id={"batch": bo(d)}, device_id_type=MESH)


    for load in loads[:5]:
        load.wait()
    xin = seq_ref[0]
    lane = lax.broadcasted_iota(I32, (ROWS, 128), 1)
    lo = lane < HEAD

    for j in range(NY // 2):
        cols = [slice(p * D + 128 * j, p * D + 128 * (j + 1)) for p in range(4)]
        tiles = []
        for p in (1, 2, 3):
            v = dot_nn(xin, w_in_ref[:, cols[p]])
            pre[:, cols[p]] = v
            tiles.append(jax.nn.silu(v))
        vt, qt, kt = tiles
        skv[2 * j] = jnp.where(lo, kt, swap(vt)).astype(BF16)
        skv[2 * j + 1] = jnp.where(lo, swap(kt), vt).astype(BF16)
        qt = qt * 0.0625
        sq[2 * j] = pack_rows(qt, 0).astype(BF16)
        sq[2 * j + 1] = pack_rows(qt, 1).astype(BF16)

    for load in loads[5:]:
        load.wait()
    negs[:, :D] = neg_ref[...].astype(F32)
    meta_lane = lax.broadcasted_iota(I32, (8, 128), 1)
    meta_row = lax.broadcasted_iota(I32, (8, 128), 0)
    meta = jnp.zeros((8, 128), F32)
    for i in range(8):
        here = meta_lane == b * 8 + i
        meta = meta + jnp.where(
            jnp.logical_and(here, meta_row == 0), nid_ref[i].astype(F32),
            jnp.where(jnp.logical_and(here, meta_row == 1), ncnt_ref[i].astype(F32), 0.0),
        )
    negs[:, D:] = meta

    pl.semaphore_wait(barrier, 2 + (NY - 1) + b)

    def kv_copy(d):
        h = yo(d)
        return copy(skv.at[h], kv.at[me], kv_s.at[h], kv_r.at[y], ctx=at(x, h, c))

    def q_copy(d):
        h = yo(d)
        return copy(sq.at[h], rq.at[y], q_s.at[h], q_r.at[y], ctx=at(x, h, c))

    far_first = sorted(range(1, NY), key=lambda d: -min(d, NY - d))
    @pl.when(x == 0)
    def _():
        for d in far_first:
            kv_copy(d).start()
        for d in far_first:
            q_copy(d).start()

    @pl.when(x == 1)
    def _():
        for d in far_first:
            q_copy(d).start()
        for d in far_first:
            kv_copy(d).start()

    kv[me] = skv[y]
    rq[y] = sq[y]

    def relay(yy):
        r = at(x, yy, c)
        return copy(kv.at[r], kv.at[r], rel_s.at[yy], rel_r.at[yy], ctx=sib)

    def own_relay():
        return copy(skv.at[y], kv.at[me], rel_s.at[y], rel_r.at[y], ctx=sib)

    E = NY // 2

    def forward(yy):
        r = at(0, yy, c)
        return copy(kv.at[r], kv.at[r], xf_s.at[yy], xf_r.at[yy], ctx=at(1 - x, y, c))

    def q_forward(i):
        return copy(rq.at[i], rq.at[NY + i], qf_s.at[i], qf_r.at[i], ctx=at(1 - x, y, c))

    own_relay().start()

    @pl.when(jnp.logical_and(x == 0, y >= E))
    def _():
        copy(skv.at[y], kv.at[me], xf_s.at[y], xf_r.at[y], ctx=at(1 - x, y, c)).start()

    @pl.when(x == 1)
    def _():
        copy(sq.at[y], rq.at[NY + y], qf_s.at[y], qf_r.at[y], ctx=at(1 - x, y, c)).start()

    def neg_copy(d):
        return copy(negs, nega.at[b], neg_s.at[d], neg_r.at[b], batch=bo(d))

    for d in range(1, NB):

        @pl.when(bo(d) < b)
        def _():
            pl.semaphore_signal(hello, inc=1, device_id={"batch": bo(d)}, device_id_type=MESH)
            neg_copy(d).start()

    nega[b] = negs[...]

    g_pre = dot_nn(xin, w_in_ref[:, :D])
    pre[:, :D] = g_pre

    near_first = far_first[::-1]
    half = low((64, 128))

    def take_q(i):
        v = rq[i].astype(F32)
        qz[i * 128 : i * 128 + 64] = jnp.where(half, v, 0.0).astype(BF16)
        qz[i * 128 + 64 : i * 128 + 128] = jnp.where(half, swap(v), 0.0).astype(BF16)

    def take_own_q():
        for d in near_first:
            yy = yo(d)
            copy(sq.at[yy], rq.at[yy], q_s.at[yy], q_r.at[yy], ctx=at(x, yy, c)).wait_recv()

            @pl.when(x == 1)
            def _():
                q_forward(yy).start()

        for i in range(NY):
            take_q(i)

    def weighted(q, tile):
        h = dot_nt(q, tile)
        return h + h * jnp.tanh(h)

    def pack_mixed(rows, e):
        top, bottom = rows[e * 128 : e * 128 + 64], rows[e * 128 + 64 : e * 128 + 128]
        return jnp.where(half, swap(top), bottom)

    def mix_cross(i):
        return copy(smx.at[i], rmx.at[i], mx_s.at[i], mx_r.at[i], ctx=at(1 - x, y, c))

    W = 128 * T

    def meet_higher():
        @pl.when(b < NB - 1)
        def _():
            pl.semaphore_wait(hello, NB - 1 - b)

        for d in range(1, NB):

            @pl.when(bo(d) > b)
            def _():
                neg_copy(d).start()

    @pl.when(x == 1)
    def _():
        take_own_q()

    for d in near_first:
        yy = yo(d)
        copy(skv.at[yy], kv.at[at(x, yy, c)], kv_s.at[yy], kv_r.at[yy], ctx=at(x, yy, c)).wait_recv()
        relay(yy).start()

        @pl.when(jnp.logical_and(x == 0, yy >= E))
        def _():
            forward(yy).start()


    @pl.when(x == 1)
    def _():
        meet_higher()

    for d in range(NY):
        yy = yo(d)
        r = at(x, yy, 1 - c)
        copy(kv.at[r], kv.at[r], rel_s.at[yy], rel_r.at[yy], ctx=sib).wait_recv()


    @pl.when(x == 0)
    def _():
        for i in range(NY):
            q_forward(i).wait_recv()
            take_q(NY + i)
        tile = kv[:NY].reshape(128 * NY, 128)
        for n in range(2):
            w = weighted(qz[256 * T + W * n : 256 * T + W * (n + 1)], tile)
            rows = dot_nn(w.astype(BF16), tile)
            for e in range(T):
                smx[n * T + e] = pack_mixed(rows, e).astype(BF16)
                mix_cross(n * T + e).start()
        meet_higher()
        take_own_q()

    def keys_of(t):
        return kv[pl.ds(t * 4, 4)].reshape(512, 128)

    def allowed(rows, keys):
        i = lax.broadcasted_iota(I32, (rows, keys), 0)
        j = lax.broadcasted_iota(I32, (rows, keys), 1)
        return j <= i + lax.shift_right_logical(i, 7) * 128 + c * 128

    def rows_of(q, tile, diagonal):
        w = weighted(q, tile)
        if diagonal:
            last = jnp.where(allowed(256, 512), w[:, -512:], 0.0)
            w = last if w.shape[1] == 512 else jnp.concatenate([w[:, :-512], last], axis=1)
        return dot_nn(w.astype(BF16), tile)

    def mix_copy(i):
        return copy(smix.at[i], rmix.at[y], mix_s.at[i], mix_r.at[y], ctx=at(x, i, c))

    def send_mixed(i, packed):
        smix[i] = packed.astype(BF16)

        @pl.when(y == i)
        def _():
            rmix[y] = smix[i]

        @pl.when(y != i)
        def _():
            mix_copy(i).start()

    def cross_in(yy):
        r = at(0, yy, c)
        return copy(kv.at[r], kv.at[r], xf_s.at[yy], xf_r.at[yy], ctx=at(1 - x, y, c))

    def cross_relay(yy, cc):
        r = at(0, yy, cc)
        return copy(kv.at[r], kv.at[r], xr_s.at[yy], xr_r.at[yy], ctx=sib)

    for k in range(T):
        if k == T - 1:

            @pl.when(x == 1)
            def _():
                for i in range(E, NY):
                    cross_in(i).wait_recv()
                    cross_relay(i, c).start()

        tile = kv[pl.ds(x * 2 * NY, 4 * (k + 1))].reshape(512 * (k + 1), 128)
        rows = rows_of(qz[256 * k : 256 * (k + 1)], tile, True)

        @pl.when(x == 0)
        def _():
            for e in range(2):
                send_mixed(2 * k + e, pack_mixed(rows, e))

        @pl.when(x == 1)
        def _():
            acc[256 * k : 256 * (k + 1)] = rows

    @pl.when(x == 1)
    def _():
        for i in range(E, NY):
            cross_relay(i, 1 - c).wait_recv()
        tile = kv[NY : 2 * NY].reshape(128 * NY, 128)
        for n in range(2):
            piece = slice(W * n, W * (n + 1))
            acc[piece] += rows_of(qz[piece], tile, False)
        for i in range(NY):
            mix_cross(i).wait_recv()
            send_mixed(i, pack_mixed(acc[i * 128 : (i + 1) * 128], 0) + rmx[i].astype(F32))

    for d in range(1, NB):
        bb = bo(d)
        copy(negs, nega.at[bb], neg_s.at[d], neg_r.at[bb], batch=bb).wait_recv()
    NEG = 8 * NB
    neg_f = nega[:, :, :D].reshape(NEG, D)
    neg_b = (neg_f * lax.rsqrt(jnp.sum(neg_f * neg_f, axis=1, keepdims=True) + 1e-06)).astype(BF16)
    metas = nega[0, :, D:]
    for i in range(1, NB):
        metas = metas + nega[i, :, D:]
    ids = metas[0:1, :NEG]
    counts = metas[1:2, :NEG]
    log_share = jnp.log(NEG * counts / jnp.sum(counts, axis=1, keepdims=True))
    pid = jnp.transpose(jnp.broadcast_to(pid_ref[...].astype(F32), (NEG, ROWS)))
    same = pid == ids
    posf = pos_ref[0].astype(F32)
    pos_unit = posf * lax.rsqrt(jnp.sum(posf * posf, axis=1, keepdims=True) + 1e-06)
    gate_u = jax.nn.silu(pre[:, :D]).astype(BF16).astype(F32)

    for d in near_first:
        yy = yo(d)
        copy(smix.at[yy], rmix.at[yy], mix_s.at[yy], mix_r.at[yy], ctx=at(x, yy, c)).wait_recv()
    mixed = jnp.concatenate(
        [unpack_pair(rmix[2 * j].astype(F32), rmix[2 * j + 1].astype(F32)) for j in range(NY // 2)], axis=1
    )
    centred = mixed - jnp.mean(mixed, axis=1, keepdims=True)
    inv_std = lax.rsqrt(jnp.mean(centred * centred, axis=1, keepdims=True) + 1e-05)
    normed = centred * inv_std
    gated = (normed * gate_u).astype(BF16)
    outputs = xin.astype(F32) + dot_nn(gated, w_out_ref[...])
    out_scale = lax.rsqrt(jnp.sum(outputs * outputs, axis=1, keepdims=True) + 1e-06)
    user = outputs * out_scale
    user_b = user.astype(BF16)
    positive = jnp.sum(user * pos_unit, axis=1, keepdims=True) * TEMPER_INV
    logits = dot_nt(user_b, neg_b) * TEMPER_INV - log_share
    terms = jnp.where(same, 0.0, jnp.exp(logits))
    pos_exp = jnp.exp(positive)
    denom = pos_exp + jnp.sum(terms, axis=1, keepdims=True)
    loss = jnp.log(denom) - positive
    d_pos = pos_exp / denom - 1.0
    probs = terms / denom
    probs_b = probs.astype(BF16)
    d_user = (d_pos * TEMPER_INV) * pos_unit + dot_nn(probs_b, neg_b) * TEMPER_INV
    d_out = out_scale * (d_user - user * jnp.sum(user * d_user, axis=1, keepdims=True))
    d_gated = dot_nt(d_out.astype(BF16), w_out_ref[...])
    d_normed = d_gated * gate_u
    d_gate = d_gated * normed
    d_mixed = inv_std * (
        d_normed
        - jnp.mean(d_normed, axis=1, keepdims=True)
        - normed * jnp.mean(d_normed * normed, axis=1, keepdims=True)
    )
    for j in range(NY // 2):
        tile = d_mixed[:, 128 * j : 128 * (j + 1)]
        sdm[2 * j] = pack_rows(tile, 0).astype(BF16)
        sdm[2 * j + 1] = pack_rows(tile, 1).astype(BF16)

    def dm_copy(d):
        yy = yo(d)
        return copy(sdm.at[yy], rdm.at[y], dm_s.at[yy], dm_r.at[y], ctx=at(x, yy, c))

    for d in far_first:
        dm_copy(d).start()
    rdm[y] = sdm[y]

    d_pre = (d_gate * slope(pre[:, :D])).astype(BF16)
    dout[...] = d_out + dot_nt(d_pre, w_in_ref[:, :D])
    loss_ref[...] = jnp.transpose(jnp.broadcast_to(loss, (ROWS, 128)))[0:1, :]
    grad = dot_nn(jnp.transpose(probs).astype(BF16), user_b) * TEMPER_INV
    for j in range(D // 256):
        pair = [grad[:, 256 * j + 128 * e : 256 * j + 128 * (e + 1)].reshape(NB, 8, 128) for e in range(2)]
        gsend[:, 16 * j : 16 * (j + 1), :] = jnp.concatenate(pair, axis=1).astype(BF16)

    def gb_copy(d):
        bb = bo(d)
        return copy(gsend.at[bb], grecv.at[b], gb_s.at[d], gb_r.at[b], batch=bb)

    for d in range(1, NB):
        gb_copy(d).start()
    grecv[b] = gsend[b]
    dq[...] = jnp.zeros_like(dq)

    def dm_forward(i):
        return copy(rdm.at[i], rdm.at[NY + i], df_s.at[i], df_r.at[i], ctx=at(1 - x, y, c))

    def pass_dm(i):
        @pl.when(x == 1)
        def _():
            dm_forward(i).start()

    pass_dm(y)
    for d in near_first:
        yy = yo(d)
        copy(sdm.at[yy], rdm.at[yy], dm_s.at[yy], dm_r.at[yy], ctx=at(x, yy, c)).wait_recv()
        pass_dm(yy)

    def take_dm(i):
        v = rdm[i].astype(F32)
        up = jnp.concatenate([jnp.where(half, 0.0, swap(v)), jnp.where(half, 0.0, v)], axis=0)
        dmz[i * 128 : i * 128 + 128] = up.astype(BF16)
        both = up + qz[i * 128 : i * 128 + 128].astype(F32)
        qdt[:, i * 128 : i * 128 + 128] = jnp.transpose(both).astype(BF16)

    for i in range(NY):
        take_dm(i)

    def g1_copy():
        return copy(g1, g2, g1_s.at[0], g1_r.at[0], ctx=sib)

    def gx_copy():
        return copy(g3, g3x, gx_s.at[0], gx_r.at[0], ctx=across)

    def gc_copy(d):
        return copy(gsum, g4.at[y], gc_s.at[d], gc_r.at[y], ctx=at(x, yo(d), c))

    def g4_copy():
        return copy(gfin.at[c], gfin.at[c], g4_s.at[0], g4_r.at[0], ctx=sib)

    H = D // 32

    def g_histories():
        for d in range(1, NB):
            bb = bo(d)
            copy(gsend.at[bb], grecv.at[bb], gb_s.at[d], gb_r.at[bb], batch=bb).wait_recv()
        g1[...] = jnp.sum(grecv[...].astype(F32), axis=0)
        g1_copy().start()

    def g_pair():
        g1_copy().wait_recv()
        total = g1[...] + g2[...]
        g3[...] = jnp.where(c == 0, total[:H], total[H:])
        gx_copy().start()

    def g_across():
        gx_copy().wait_recv()
        gsum[...] = (g3[...] + g3x[...]).astype(BF16)
        for d in range(1, NY):
            gc_copy(d).start()
        g4[y] = gsum[...]

    def g_chips():
        for d in range(1, NY):
            copy(gsum, g4.at[yo(d)], gc_s.at[d], gc_r.at[yo(d)], ctx=sib).wait_recv()
        gfin[c] = jnp.sum(g4[...].astype(F32), axis=0)
        g4_copy().start()

    def bwd(rows, block, blocks, diagonal, more):
        tile = kv[pl.ds(block, blocks)].reshape(128 * blocks, 128)
        h = dot_nt(qz[rows], tile)
        dw = dot_nt(dmz[rows], tile)
        th = jnp.tanh(h)
        u = 1.0 + th
        w = h * u
        ds = dw * (u + w * (1.0 - th))
        if diagonal:
            lead = 64 * blocks
            ok = allowed(lead, 128 * blocks)

            def masked(v):
                first = jnp.where(ok, v[:lead], 0.0)
                return first if v.shape[0] == lead else jnp.concatenate([first, v[lead:]], axis=0)

            w, ds = masked(w), masked(ds)
        w = w.astype(BF16)
        ds = ds.astype(BF16)
        dq[rows] += dot_nn(ds, tile)
        dk = dot_nn(qdt[:64, rows], ds)
        dv = dot_nn(qdt[64:, rows], w)
        for j in range(blocks):
            one = slice(128 * j, 128 * (j + 1))
            if more:
                dkv[block + j, :64, :] += dk[:, one]
                dkv[block + j, 64:, :] += dv[:, one]
            else:
                dkv[block + j, :64, :] = dk[:, one]
                dkv[block + j, 64:, :] = dv[:, one]

    def sib_own(yy):
        return copy(dkv.at[at(x, yy, 1 - c)], sibo.at[yy], so_s.at[yy], so_r.at[yy], ctx=sib)

    def sib_cross(yy):
        return copy(dkv.at[at(0, yy, 1 - c)], sibx.at[yy], sx_s.at[yy], sx_r.at[yy], ctx=sib)

    def cross(yy):
        return copy(sx.at[yy], rx.at[yy], xx_s.at[yy], xx_r.at[yy], ctx=at(1 - x, y, c))

    def cross_sums(t):
        for e in range(2):
            i = 2 * t + e
            sib_cross(i).wait_recv()
            sx[i] = (dkv[at(0, i, c)] + sibx[i]).astype(BF16)
            cross(i).start()

    def retq_copy(i):
        return copy(sretq.at[i], rretq.at[y], retq_s.at[i], retq_r.at[y], ctx=at(x, i, c))

    def ret_copy(i):
        return copy(sret.at[i], rret.at[y], ret_s.at[i], ret_r.at[y], ctx=at(x, i, c))

    def pack_dq(i):
        top = dq[i * 128 : i * 128 + 64] * 0.0625
        bottom = dq[i * 128 + 64 : i * 128 + 128] * 0.0625
        return jnp.where(half, top, swap(bottom))

    def send_dq(k, crossed):
        for i in (2 * k, 2 * k + 1):
            mine = pack_dq(i)
            if crossed:
                dq_cross(i).wait_recv()
                mine = mine + rxq[i].astype(F32)
            sretq[i] = mine.astype(BF16)

            @pl.when(y == i)
            def _():
                rretq[y] = sretq[i]

            @pl.when(y != i)
            def _():
                retq_copy(i).start()

    def dq_cross(i):
        return copy(sxq.at[i], rxq.at[i], xq_s.at[i], xq_r.at[i], ctx=at(1 - x, y, c))

    def send_dkv(t, crossed):
        for i in (2 * t, 2 * t + 1):
            sib_own(i).wait_recv()
            total = dkv[at(x, i, c)] + sibo[i]
            if crossed:
                cross(i).wait_recv()
                total = total + rx[i].astype(F32)
            sret[i] = jnp.transpose(total).astype(BF16)

            @pl.when(y == i)
            def _():
                rret[y] = sret[i]

            @pl.when(y != i)
            def _():
                ret_copy(i).start()


    HALF = T // 2
    every = slice(0, 256 * T)

    def own_step(t, tiles):
        bwd(slice(256 * t, 256 * T), (x * T + t) * 4, 4 * tiles, True, False)

        @pl.when(jnp.logical_or(x == 1, t >= HALF))
        def _():
            for i in range(2 * t, 2 * (t + tiles)):
                sib_own(i).start()

        @pl.when(x == 0)
        def _():
            for k in range(t, t + tiles):
                send_dq(k, False)

    if T == 2:
        steps = [(0, 1), (1, 1)]
    else:
        steps = [(t, 1) for t in range(T - 2)] + [(T - 2, 2)]
    own_step(*steps[0])


    @pl.when(x == 1)
    def _():
        for t in range(HALF, T):
            bwd(every, 4 * t, 4, False, False)
            for e in range(2):
                sib_cross(2 * t + e).start()
            if t > HALF:
                cross_sums(t - 1)
            else:
                send_dkv(0, False)

    for n, (t, tiles) in list(enumerate(steps))[1:]:
        own_step(t, tiles)

        @pl.when(x == 1)
        def _():
            if n == 1:
                cross_sums(T - 1)
            for k in range(steps[n - 1][0], t):
                if k:
                    send_dkv(k, False)

    g_histories()


    @pl.when(x == 0)
    def _():
        for i in range(NY):
            dm_forward(i).wait_recv()
            take_dm(NY + i)
        for n in range(2):
            bwd(slice(256 * T + 128 * T * n, 256 * T + 128 * T * (n + 1)), 0, 4 * HALF, False, True)
            for e in range(T):
                i = n * T + e
                sxq[i] = pack_dq(NY + i).astype(BF16)
                dq_cross(i).start()
        for i in range(2 * HALF):
            sib_own(i).start()


    @pl.when(x == 1)
    def _():
        for k in range(steps[-1][0], T):
            send_dkv(k, False)

    g_pair()

    @pl.when(x == 1)
    def _():
        for k in range(T):
            send_dq(k, True)

    @pl.when(x == 0)
    def _():
        for t in list(range(HALF, T)) + list(range(HALF)):
            send_dkv(t, t >= HALF)

    g_across()

    def finish_dq():
        for d in near_first:
            yy = yo(d)
            copy(sretq.at[yy], rretq.at[yy], retq_s.at[yy], retq_r.at[yy], ctx=at(x, yy, c)).wait_recv()
        for j in range(NY // 2):
            cols = slice(2 * D + 128 * j, 2 * D + 128 * (j + 1))
            d_q = unpack_pair(rretq[2 * j].astype(F32), rretq[2 * j + 1].astype(F32))
            dpre[:, cols] = (d_q * slope(pre[:, cols])).astype(BF16)
        dout[...] += dot_nt(dpre[:, 2 * D : 3 * D], w_in_ref[:, 2 * D : 3 * D])


    @pl.when(x == 0)
    def _():
        finish_dq()

    for d in near_first:
        yy = yo(d)
        copy(sret.at[yy], rret.at[yy], ret_s.at[yy], ret_r.at[yy], ctx=at(x, yy, c)).wait_recv()
    for j in range(NY // 2):
        even, odd = rret[2 * j].astype(F32), rret[2 * j + 1].astype(F32)
        cols = slice(3 * D + 128 * j, 3 * D + 128 * (j + 1))
        dpre[:, cols] = (jnp.where(lo, even, swap(odd)) * slope(pre[:, cols])).astype(BF16)
        cols = slice(D + 128 * j, D + 128 * (j + 1))
        dpre[:, cols] = (jnp.where(lo, swap(even), odd) * slope(pre[:, cols])).astype(BF16)
    dout[...] += dot_nt(dpre[:, D : 2 * D], w_in_ref[:, D : 2 * D]) + dot_nt(dpre[:, 3 * D :], w_in_ref[:, 3 * D :])
    g_chips()

    @pl.when(x == 1)
    def _():
        finish_dq()

    dseq_ref[0] = dout[...].astype(BF16)

    copy(gfin.at[1 - c], gfin.at[1 - c], g4_s.at[0], g4_r.at[0], ctx=sib).wait_recv()
    d_total = jnp.concatenate([gfin[e // (H // 8), 8 * (e % (H // 8)) : 8 * (e % (H // 8)) + 8] for e in range(D // 128)], axis=1)
    nf = neg_ref[...].astype(F32)
    scale = lax.rsqrt(jnp.sum(nf * nf, axis=1, keepdims=True) + 1e-06)
    unit = nf * scale
    dneg_ref[...] = scale * (d_total - unit * jnp.sum(unit * d_total, axis=1, keepdims=True))

    for d in range(1, NY):
        kv_copy(d).wait_send()
        q_copy(d).wait_send()
        mix_copy(yo(d)).wait_send()
        dm_copy(d).wait_send()
        retq_copy(yo(d)).wait_send()
        ret_copy(yo(d)).wait_send()
    for i in range(NY):
        relay(i).wait_send()
        sib_own(i).wait_send()
    for d in range(1, NB):
        neg_copy(d).wait_send()
        gb_copy(d).wait_send()
    for d in range(1, NY):
        gc_copy(d).wait_send()
    gx_copy().wait_send()
    g1_copy().wait_send()
    g4_copy().wait_send()

    @pl.when(x == 0)
    def _():
        for i in range(NY):
            mix_cross(i).wait_send()
            dq_cross(i).wait_send()
        for i in range(E, NY):
            forward(i).wait_send()

    @pl.when(x == 1)
    def _():
        for i in range(NY):
            q_forward(i).wait_send()
            dm_forward(i).wait_send()
        for i in range(2 * HALF, NY):
            sib_cross(i).wait_send()
            cross(i).wait_send()
            cross_relay(i, c).wait_send()


def solution(mesh):
    NY = mesh.shape["ctx"] // 4
    NB = mesh.shape["batch"]
    D = HEAD * NY
    V, S = pltpu.VMEM, pltpu.SemaphoreType.DMA

    def body(*refs):
        kernel(NY, NB, *refs)

    def shards(seq_in, w_in, w_out, pos_emb, pos_ids, neg_emb, neg_ids, neg_counts):
        vm = pl.BlockSpec(memory_space=pltpu.VMEM)
        return pl.pallas_call(
            body,
            out_shape=(
                jax.ShapeDtypeStruct((1, ROWS), F32),
                jax.ShapeDtypeStruct((1, ROWS, D), BF16),
                jax.ShapeDtypeStruct((8, D), F32),
            ),
            in_specs=[pl.BlockSpec(memory_space=pltpu.HBM)] * 8,
            out_specs=(vm, vm, vm),
            scratch_shapes=[
                V((1, ROWS, D), BF16),
                V((D, 4 * D), BF16),
                V((D, D), BF16),
                V((1, ROWS, D), BF16),
                V((1, ROWS), I32),
                V((8, D), BF16),
                pltpu.SMEM((8,), I32),
                pltpu.SMEM((8,), I32),
                S((12,)),
                V((ROWS, 4 * D), F32),
                V((NY, 128, 128), BF16),
                V((NY, 64, 128), BF16),
                V((4 * NY, 128, 128), BF16),
                V((2 * NY, 64, 128), BF16),
                V((NY * 256, 128), BF16),
                V((NY * 128, 128), F32),
                V((NY, 64, 128), BF16),
                V((NY, 64, 128), BF16),
                V((NY, 64, 128), BF16),
                V((2 * NY, 64, 128), BF16),
                V((NY * 256, 128), BF16),
                V((128, NY * 256), BF16),
                V((NY * 256, 128), F32),
                V((4 * NY, 128, 128), F32),
                V((NY, 128, 128), F32),
                V((NY, 128, 128), F32),
                V((NY, 128, 128), BF16),
                V((NY, 128, 128), BF16),
                V((NY, 64, 128), BF16),
                V((NY, 64, 128), BF16),
                V((NY, 64, 128), BF16),
                V((NY, 64, 128), BF16),
                V((NY, 128, 128), BF16),
                V((NY, 128, 128), BF16),
                V((NY, 64, 128), BF16),
                V((NY, 64, 128), BF16),
                V((ROWS, D), F32),
                V((ROWS, 4 * D), BF16),
                V((8, D + 128), F32),
                V((NB, 8, D + 128), F32),
                V((NB, D // 16, 128), BF16),
                V((NB, D // 16, 128), BF16),
                V((D // 16, 128), F32),
                V((D // 16, 128), F32),
                V((D // 32, 128), F32),
                V((D // 32, 128), F32),
                V((D // 32, 128), BF16),
                V((NY, D // 32, 128), BF16),
                V((2, D // 32, 128), F32),
            ]
            + [S((NY,))] * 32
            + [S((NB,))] * 4
            + [S((1,))] * 2
            + [S((NY,))] * 2
            + [S((1,))] * 4
            + [pltpu.SemaphoreType.REGULAR],
            compiler_params=pltpu.CompilerParams(
                collective_id=0, has_side_effects=True, vmem_limit_bytes=60 << 20
            ),
        )(seq_in, w_in, w_out, pos_emb, pos_ids, neg_emb, neg_ids, neg_counts)

    in_specs = (
        P("batch", "ctx", None), P(), P(), P("batch", "ctx", None), P("batch", "ctx"),
        P("batch", None), P("batch"), P("batch"),
    )
    out_specs = (P("batch", "ctx"), P("batch", "ctx", None), P("batch", None))
    return jax.shard_map(shards, mesh=mesh, in_specs=in_specs, out_specs=out_specs, check_vma=False)
```

```python
import jax
import jax.numpy as jnp
from jax import lax
from jax.experimental import pallas as pl
from jax.experimental.pallas import tpu as pltpu
from jax.sharding import PartitionSpec as P

MESH = pl.DeviceIdType.MESH
F32, BF16, I32 = jnp.float32, jnp.bfloat16, jnp.int32
HEAD = 64
ROWS = 128
TEMPER_INV = 20.0


def dot_nn(a, b):
    return lax.dot_general(a, b, (((1,), (0,)), ((), ())), preferred_element_type=F32)


def dot_nt(a, b):
    return lax.dot_general(a, b, (((1,), (1,)), ((), ())), preferred_element_type=F32)


def swap(v):
    return pltpu.roll(v, 64, 1)


def low(shape):
    return lax.broadcasted_iota(I32, shape, 1) < HEAD


def slope(v):
    g = jax.nn.sigmoid(v)
    return g * (1.0 + v * (1.0 - g))


def pack_rows(tile, which):
    top, bottom = tile[:64], tile[64:]
    if which == 0:
        return jnp.where(low(top.shape), top, swap(bottom))
    return jnp.where(low(top.shape), swap(top), bottom)


def unpack_pair(even, odd):
    top = jnp.where(low(even.shape), even, swap(odd))
    bottom = jnp.where(low(even.shape), swap(even), odd)
    return jnp.concatenate([top, bottom], axis=0)


def kernel(
    NY, NB,
    seq_hbm, w_in_hbm, w_out_hbm, pos_hbm, pid_hbm, neg_hbm, nid_hbm, ncnt_hbm,
    loss_ref, dseq_ref, dneg_ref,
    seq_ref, w_in_ref, w_out_ref, pos_ref, pid_ref, neg_ref, nid_ref, ncnt_ref, in_s,
    pre, skv, sq, kv, rq, qz, acc, smix, rmix, sdm, rdm, dmz, qdt, dq, dkv,
    sibo, sibx, sx, rx, sxq, rxq, smx, rmx, sret, rret, sretq, rretq, dout, dpre, negs, nega, gsend, grecv, g1, g2, g3, g3x, gsum, g4, gfin,
    kv_s, kv_r, q_s, q_r, rel_s, rel_r, xf_s, xf_r, xr_s, xr_r, mix_s, mix_r, dm_s, dm_r,
    qf_s, qf_r, mx_s, mx_r, df_s, df_r, xq_s, xq_r, so_s, so_r, sx_s, sx_r, xx_s, xx_r, ret_s, ret_r, retq_s, retq_r,
    neg_s, neg_r, gb_s, gb_r, g1_s, g1_r, gc_s, gc_r, g4_s, g4_r, gx_s, gx_r, hello,
):
    D = HEAD * NY
    T = NY // 2
    me = lax.axis_index("ctx")
    b = lax.axis_index("batch")
    c = lax.rem(me, 2)
    y = lax.rem(lax.div(me, 2), NY)
    x = lax.div(me, 2 * NY)

    def at(xx, yy, cc):
        return (xx * NY + yy) * 2 + cc

    def yo(d):
        return lax.rem(y + d, NY)

    def bo(d):
        return lax.rem(b + d, NB)

    sib = at(x, y, 1 - c)
    others = [at(x, yo(d), c) for d in range(1, NY)]
    across = at(1 - x, y, c)

    def copy(src, dst, ss, rs, ctx=None, batch=None):
        where = {"ctx": ctx} if batch is None else {"batch": batch}
        return pltpu.make_async_remote_copy(
            src_ref=src, dst_ref=dst, send_sem=ss, recv_sem=rs, device_id=where, device_id_type=MESH
        )


    loads = [
        pltpu.make_async_copy(src, dst, in_s.at[i])
        for i, (src, dst) in enumerate(
            [
                (seq_hbm, seq_ref),
                *[
                    (w_in_hbm.at[pl.ds(r * D // 4, D // 4), D:], w_in_ref.at[pl.ds(r * D // 4, D // 4), D:])
                    for r in range(4)
                ],
                (w_in_hbm.at[:, :D], w_in_ref.at[:, :D]),
                (neg_hbm, neg_ref),
                (nid_hbm, nid_ref),
                (ncnt_hbm, ncnt_ref),
                (pos_hbm, pos_ref),
                (pid_hbm, pid_ref),
                (w_out_hbm, w_out_ref),
            ]
        )
    ]
    for load in loads:
        load.start()
    barrier = pltpu.get_barrier_semaphore()
    for p in [sib, across] + others:
        pl.semaphore_signal(barrier, inc=1, device_id={"ctx": p}, device_id_type=MESH)
    for d in range(1, NB):

        @pl.when(bo(d) > b)
        def _():
            pl.semaphore_signal(barrier, inc=1, device_id={"batch": bo(d)}, device_id_type=MESH)


    for load in loads[:5]:
        load.wait()
    xin = seq_ref[0]
    lane = lax.broadcasted_iota(I32, (ROWS, 128), 1)
    lo = lane < HEAD

    for j in range(NY // 2):
        cols = [slice(p * D + 128 * j, p * D + 128 * (j + 1)) for p in range(4)]
        tiles = []
        for p in (1, 2, 3):
            v = dot_nn(xin, w_in_ref[:, cols[p]])
            pre[:, cols[p]] = v
            tiles.append(jax.nn.silu(v))
        vt, qt, kt = tiles
        skv[2 * j] = jnp.where(lo, kt, swap(vt)).astype(BF16)
        skv[2 * j + 1] = jnp.where(lo, swap(kt), vt).astype(BF16)
        qt = qt * 0.0625
        sq[2 * j] = pack_rows(qt, 0).astype(BF16)
        sq[2 * j + 1] = pack_rows(qt, 1).astype(BF16)

    for load in loads[5:]:
        load.wait()
    negs[:, :D] = neg_ref[...].astype(F32)
    meta_lane = lax.broadcasted_iota(I32, (8, 128), 1)
    meta_row = lax.broadcasted_iota(I32, (8, 128), 0)
    meta = jnp.zeros((8, 128), F32)
    for i in range(8):
        here = meta_lane == b * 8 + i
        meta = meta + jnp.where(
            jnp.logical_and(here, meta_row == 0), nid_ref[i].astype(F32),
            jnp.where(jnp.logical_and(here, meta_row == 1), ncnt_ref[i].astype(F32), 0.0),
        )
    negs[:, D:] = meta

    pl.semaphore_wait(barrier, 2 + (NY - 1) + b)

    def kv_copy(d):
        h = yo(d)
        return copy(skv.at[h], kv.at[me], kv_s.at[h], kv_r.at[y], ctx=at(x, h, c))

    def q_copy(d):
        h = yo(d)
        return copy(sq.at[h], rq.at[y], q_s.at[h], q_r.at[y], ctx=at(x, h, c))

    far_first = sorted(range(1, NY), key=lambda d: -min(d, NY - d))
    @pl.when(x == 0)
    def _():
        for d in far_first:
            kv_copy(d).start()
        for d in far_first:
            q_copy(d).start()

    @pl.when(x == 1)
    def _():
        for d in far_first:
            q_copy(d).start()
        for d in far_first:
            kv_copy(d).start()

    kv[me] = skv[y]
    rq[y] = sq[y]

    def relay(yy):
        r = at(x, yy, c)
        return copy(kv.at[r], kv.at[r], rel_s.at[yy], rel_r.at[yy], ctx=sib)

    def own_relay():
        return copy(skv.at[y], kv.at[me], rel_s.at[y], rel_r.at[y], ctx=sib)

    E = NY // 2

    def forward(yy):
        r = at(0, yy, c)
        return copy(kv.at[r], kv.at[r], xf_s.at[yy], xf_r.at[yy], ctx=at(1 - x, y, c))

    def q_forward(i):
        return copy(rq.at[i], rq.at[NY + i], qf_s.at[i], qf_r.at[i], ctx=at(1 - x, y, c))

    own_relay().start()

    @pl.when(jnp.logical_and(x == 0, y >= E))
    def _():
        copy(skv.at[y], kv.at[me], xf_s.at[y], xf_r.at[y], ctx=at(1 - x, y, c)).start()

    @pl.when(x == 1)
    def _():
        copy(sq.at[y], rq.at[NY + y], qf_s.at[y], qf_r.at[y], ctx=at(1 - x, y, c)).start()

    def neg_copy(d):
        return copy(negs, nega.at[b], neg_s.at[d], neg_r.at[b], batch=bo(d))

    for d in range(1, NB):

        @pl.when(bo(d) < b)
        def _():
            pl.semaphore_signal(hello, inc=1, device_id={"batch": bo(d)}, device_id_type=MESH)
            neg_copy(d).start()

    nega[b] = negs[...]

    g_pre = dot_nn(xin, w_in_ref[:, :D])
    pre[:, :D] = g_pre

    near_first = far_first[::-1]
    half = low((64, 128))

    def take_q(i):
        v = rq[i].astype(F32)
        qz[i * 128 : i * 128 + 64] = jnp.where(half, v, 0.0).astype(BF16)
        qz[i * 128 + 64 : i * 128 + 128] = jnp.where(half, swap(v), 0.0).astype(BF16)

    def take_own_q():
        for d in near_first:
            yy = yo(d)
            copy(sq.at[yy], rq.at[yy], q_s.at[yy], q_r.at[yy], ctx=at(x, yy, c)).wait_recv()

            @pl.when(x == 1)
            def _():
                q_forward(yy).start()

        for i in range(NY):
            take_q(i)

    def weighted(q, tile):
        h = dot_nt(q, tile)
        return h + h * jnp.tanh(h)

    def pack_mixed(rows, e):
        top, bottom = rows[e * 128 : e * 128 + 64], rows[e * 128 + 64 : e * 128 + 128]
        return jnp.where(half, swap(top), bottom)

    def mix_cross(i):
        return copy(smx.at[i], rmx.at[i], mx_s.at[i], mx_r.at[i], ctx=at(1 - x, y, c))

    W = 128 * T

    def meet_higher():
        @pl.when(b < NB - 1)
        def _():
            pl.semaphore_wait(hello, NB - 1 - b)

        for d in range(1, NB):

            @pl.when(bo(d) > b)
            def _():
                neg_copy(d).start()

    @pl.when(x == 1)
    def _():
        take_own_q()

    for d in near_first:
        yy = yo(d)
        copy(skv.at[yy], kv.at[at(x, yy, c)], kv_s.at[yy], kv_r.at[yy], ctx=at(x, yy, c)).wait_recv()
        relay(yy).start()

        @pl.when(jnp.logical_and(x == 0, yy >= E))
        def _():
            forward(yy).start()


    @pl.when(x == 1)
    def _():
        meet_higher()

    for d in range(NY):
        yy = yo(d)
        r = at(x, yy, 1 - c)
        copy(kv.at[r], kv.at[r], rel_s.at[yy], rel_r.at[yy], ctx=sib).wait_recv()


    @pl.when(x == 0)
    def _():
        for i in range(NY):
            q_forward(i).wait_recv()
            take_q(NY + i)
        tile = kv[:NY].reshape(128 * NY, 128)
        for n in range(2):
            w = weighted(qz[256 * T + W * n : 256 * T + W * (n + 1)], tile)
            rows = dot_nn(w.astype(BF16), tile)
            for e in range(T):
                smx[n * T + e] = pack_mixed(rows, e).astype(BF16)
                mix_cross(n * T + e).start()
        meet_higher()
        take_own_q()

    def keys_of(t):
        return kv[pl.ds(t * 4, 4)].reshape(512, 128)

    def allowed(rows, keys):
        i = lax.broadcasted_iota(I32, (rows, keys), 0)
        j = lax.broadcasted_iota(I32, (rows, keys), 1)
        return j <= i + lax.shift_right_logical(i, 7) * 128 + c * 128

    def rows_of(q, tile, diagonal):
        w = weighted(q, tile)
        if diagonal:
            last = jnp.where(allowed(256, 512), w[:, -512:], 0.0)
            w = last if w.shape[1] == 512 else jnp.concatenate([w[:, :-512], last], axis=1)
        return dot_nn(w.astype(BF16), tile)

    def mix_copy(i):
        return copy(smix.at[i], rmix.at[y], mix_s.at[i], mix_r.at[y], ctx=at(x, i, c))

    def send_mixed(i, packed):
        smix[i] = packed.astype(BF16)

        @pl.when(y == i)
        def _():
            rmix[y] = smix[i]

        @pl.when(y != i)
        def _():
            mix_copy(i).start()

    def cross_in(yy):
        r = at(0, yy, c)
        return copy(kv.at[r], kv.at[r], xf_s.at[yy], xf_r.at[yy], ctx=at(1 - x, y, c))

    def cross_relay(yy, cc):
        r = at(0, yy, cc)
        return copy(kv.at[r], kv.at[r], xr_s.at[yy], xr_r.at[yy], ctx=sib)

    for k in range(T):
        if k == T - 1:

            @pl.when(x == 1)
            def _():
                for i in range(E, NY):
                    cross_in(i).wait_recv()
                    cross_relay(i, c).start()

        tile = kv[pl.ds(x * 2 * NY, 4 * (k + 1))].reshape(512 * (k + 1), 128)
        rows = rows_of(qz[256 * k : 256 * (k + 1)], tile, True)

        @pl.when(x == 0)
        def _():
            for e in range(2):
                send_mixed(2 * k + e, pack_mixed(rows, e))

        @pl.when(x == 1)
        def _():
            acc[256 * k : 256 * (k + 1)] = rows

    @pl.when(x == 1)
    def _():
        for i in range(E, NY):
            cross_relay(i, 1 - c).wait_recv()
        tile = kv[NY : 2 * NY].reshape(128 * NY, 128)
        for n in range(2):
            piece = slice(W * n, W * (n + 1))
            acc[piece] += rows_of(qz[piece], tile, False)
        for i in range(NY):
            mix_cross(i).wait_recv()
            send_mixed(i, pack_mixed(acc[i * 128 : (i + 1) * 128], 0) + rmx[i].astype(F32))

    for d in range(1, NB):
        bb = bo(d)
        copy(negs, nega.at[bb], neg_s.at[d], neg_r.at[bb], batch=bb).wait_recv()
    NEG = 8 * NB
    neg_f = nega[:, :, :D].reshape(NEG, D)
    neg_b = (neg_f * lax.rsqrt(jnp.sum(neg_f * neg_f, axis=1, keepdims=True) + 1e-06)).astype(BF16)
    metas = nega[0, :, D:]
    for i in range(1, NB):
        metas = metas + nega[i, :, D:]
    ids = metas[0:1, :NEG]
    counts = metas[1:2, :NEG]
    log_share = jnp.log(NEG * counts / jnp.sum(counts, axis=1, keepdims=True))
    pid = jnp.transpose(jnp.broadcast_to(pid_ref[...].astype(F32), (NEG, ROWS)))
    same = pid == ids
    posf = pos_ref[0].astype(F32)
    pos_unit = posf * lax.rsqrt(jnp.sum(posf * posf, axis=1, keepdims=True) + 1e-06)
    gate_u = jax.nn.silu(pre[:, :D]).astype(BF16).astype(F32)

    for d in near_first:
        yy = yo(d)
        copy(smix.at[yy], rmix.at[yy], mix_s.at[yy], mix_r.at[yy], ctx=at(x, yy, c)).wait_recv()
    mixed = jnp.concatenate(
        [unpack_pair(rmix[2 * j].astype(F32), rmix[2 * j + 1].astype(F32)) for j in range(NY // 2)], axis=1
    )
    centred = mixed - jnp.mean(mixed, axis=1, keepdims=True)
    inv_std = lax.rsqrt(jnp.mean(centred * centred, axis=1, keepdims=True) + 1e-05)
    normed = centred * inv_std
    gated = (normed * gate_u).astype(BF16)
    outputs = xin.astype(F32) + dot_nn(gated, w_out_ref[...])
    out_scale = lax.rsqrt(jnp.sum(outputs * outputs, axis=1, keepdims=True) + 1e-06)
    user = outputs * out_scale
    user_b = user.astype(BF16)
    positive = jnp.sum(user * pos_unit, axis=1, keepdims=True) * TEMPER_INV
    logits = dot_nt(user_b, neg_b) * TEMPER_INV - log_share
    terms = jnp.where(same, 0.0, jnp.exp(logits))
    pos_exp = jnp.exp(positive)
    denom = pos_exp + jnp.sum(terms, axis=1, keepdims=True)
    loss = jnp.log(denom) - positive
    d_pos = pos_exp / denom - 1.0
    probs = terms / denom
    probs_b = probs.astype(BF16)
    d_user = (d_pos * TEMPER_INV) * pos_unit + dot_nn(probs_b, neg_b) * TEMPER_INV
    d_out = out_scale * (d_user - user * jnp.sum(user * d_user, axis=1, keepdims=True))
    d_gated = dot_nt(d_out.astype(BF16), w_out_ref[...])
    d_normed = d_gated * gate_u
    d_gate = d_gated * normed
    d_mixed = inv_std * (
        d_normed
        - jnp.mean(d_normed, axis=1, keepdims=True)
        - normed * jnp.mean(d_normed * normed, axis=1, keepdims=True)
    )
    for j in range(NY // 2):
        tile = d_mixed[:, 128 * j : 128 * (j + 1)]
        sdm[2 * j] = pack_rows(tile, 0).astype(BF16)
        sdm[2 * j + 1] = pack_rows(tile, 1).astype(BF16)

    def dm_copy(d):
        yy = yo(d)
        return copy(sdm.at[yy], rdm.at[y], dm_s.at[yy], dm_r.at[y], ctx=at(x, yy, c))

    for d in far_first:
        dm_copy(d).start()
    rdm[y] = sdm[y]

    d_pre = (d_gate * slope(pre[:, :D])).astype(BF16)
    dout[...] = d_out + dot_nt(d_pre, w_in_ref[:, :D])
    loss_ref[...] = jnp.transpose(jnp.broadcast_to(loss, (ROWS, 128)))[0:1, :]
    grad = dot_nn(jnp.transpose(probs).astype(BF16), user_b) * TEMPER_INV
    for j in range(D // 256):
        pair = [grad[:, 256 * j + 128 * e : 256 * j + 128 * (e + 1)].reshape(NB, 8, 128) for e in range(2)]
        gsend[:, 16 * j : 16 * (j + 1), :] = jnp.concatenate(pair, axis=1).astype(BF16)

    def gb_copy(d):
        bb = bo(d)
        return copy(gsend.at[bb], grecv.at[b], gb_s.at[d], gb_r.at[b], batch=bb)

    for d in range(1, NB):
        gb_copy(d).start()
    grecv[b] = gsend[b]
    dq[...] = jnp.zeros_like(dq)

    def dm_forward(i):
        return copy(rdm.at[i], rdm.at[NY + i], df_s.at[i], df_r.at[i], ctx=at(1 - x, y, c))

    def pass_dm(i):
        @pl.when(x == 1)
        def _():
            dm_forward(i).start()

    pass_dm(y)
    for d in near_first:
        yy = yo(d)
        copy(sdm.at[yy], rdm.at[yy], dm_s.at[yy], dm_r.at[yy], ctx=at(x, yy, c)).wait_recv()
        pass_dm(yy)

    def take_dm(i):
        v = rdm[i].astype(F32)
        up = jnp.concatenate([jnp.where(half, 0.0, swap(v)), jnp.where(half, 0.0, v)], axis=0)
        dmz[i * 128 : i * 128 + 128] = up.astype(BF16)
        both = up + qz[i * 128 : i * 128 + 128].astype(F32)
        qdt[:, i * 128 : i * 128 + 128] = jnp.transpose(both).astype(BF16)

    for i in range(NY):
        take_dm(i)

    def g1_copy():
        return copy(g1, g2, g1_s.at[0], g1_r.at[0], ctx=sib)

    def gx_copy():
        return copy(g3, g3x, gx_s.at[0], gx_r.at[0], ctx=across)

    def gc_copy(d):
        return copy(gsum, g4.at[y], gc_s.at[d], gc_r.at[y], ctx=at(x, yo(d), c))

    def g4_copy():
        return copy(gfin.at[c], gfin.at[c], g4_s.at[0], g4_r.at[0], ctx=sib)

    H = D // 32

    def g_histories():
        for d in range(1, NB):
            bb = bo(d)
            copy(gsend.at[bb], grecv.at[bb], gb_s.at[d], gb_r.at[bb], batch=bb).wait_recv()
        g1[...] = jnp.sum(grecv[...].astype(F32), axis=0)
        g1_copy().start()

    def g_pair():
        g1_copy().wait_recv()
        total = g1[...] + g2[...]
        g3[...] = jnp.where(c == 0, total[:H], total[H:])
        gx_copy().start()

    def g_across():
        gx_copy().wait_recv()
        gsum[...] = (g3[...] + g3x[...]).astype(BF16)
        for d in range(1, NY):
            gc_copy(d).start()
        g4[y] = gsum[...]

    def g_chips():
        for d in range(1, NY):
            copy(gsum, g4.at[yo(d)], gc_s.at[d], gc_r.at[yo(d)], ctx=sib).wait_recv()
        gfin[c] = jnp.sum(g4[...].astype(F32), axis=0)
        g4_copy().start()

    def bwd(rows, block, blocks, diagonal, more):
        tile = kv[pl.ds(block, blocks)].reshape(128 * blocks, 128)
        h = dot_nt(qz[rows], tile)
        dw = dot_nt(dmz[rows], tile)
        th = jnp.tanh(h)
        u = 1.0 + th
        w = h * u
        ds = dw * (u + w * (1.0 - th))
        if diagonal:
            lead = 64 * blocks
            ok = allowed(lead, 128 * blocks)

            def masked(v):
                first = jnp.where(ok, v[:lead], 0.0)
                return first if v.shape[0] == lead else jnp.concatenate([first, v[lead:]], axis=0)

            w, ds = masked(w), masked(ds)
        w = w.astype(BF16)
        ds = ds.astype(BF16)
        dq[rows] += dot_nn(ds, tile)
        dk = dot_nn(qdt[:64, rows], ds)
        dv = dot_nn(qdt[64:, rows], w)
        for j in range(blocks):
            one = slice(128 * j, 128 * (j + 1))
            if more:
                dkv[block + j, :64, :] += dk[:, one]
                dkv[block + j, 64:, :] += dv[:, one]
            else:
                dkv[block + j, :64, :] = dk[:, one]
                dkv[block + j, 64:, :] = dv[:, one]

    def sib_own(yy):
        return copy(dkv.at[at(x, yy, 1 - c)], sibo.at[yy], so_s.at[yy], so_r.at[yy], ctx=sib)

    def sib_cross(yy):
        return copy(dkv.at[at(0, yy, 1 - c)], sibx.at[yy], sx_s.at[yy], sx_r.at[yy], ctx=sib)

    def cross(yy):
        return copy(sx.at[yy], rx.at[yy], xx_s.at[yy], xx_r.at[yy], ctx=at(1 - x, y, c))

    def cross_sums(t):
        for e in range(2):
            i = 2 * t + e
            sib_cross(i).wait_recv()
            sx[i] = (dkv[at(0, i, c)] + sibx[i]).astype(BF16)
            cross(i).start()

    def retq_copy(i):
        return copy(sretq.at[i], rretq.at[y], retq_s.at[i], retq_r.at[y], ctx=at(x, i, c))

    def ret_copy(i):
        return copy(sret.at[i], rret.at[y], ret_s.at[i], ret_r.at[y], ctx=at(x, i, c))

    def pack_dq(i):
        top = dq[i * 128 : i * 128 + 64] * 0.0625
        bottom = dq[i * 128 + 64 : i * 128 + 128] * 0.0625
        return jnp.where(half, top, swap(bottom))

    def send_dq(k, crossed):
        for i in (2 * k, 2 * k + 1):
            mine = pack_dq(i)
            if crossed:
                dq_cross(i).wait_recv()
                mine = mine + rxq[i].astype(F32)
            sretq[i] = mine.astype(BF16)

            @pl.when(y == i)
            def _():
                rretq[y] = sretq[i]

            @pl.when(y != i)
            def _():
                retq_copy(i).start()

    def dq_cross(i):
        return copy(sxq.at[i], rxq.at[i], xq_s.at[i], xq_r.at[i], ctx=at(1 - x, y, c))

    def send_dkv(t, crossed):
        for i in (2 * t, 2 * t + 1):
            sib_own(i).wait_recv()
            total = dkv[at(x, i, c)] + sibo[i]
            if crossed:
                cross(i).wait_recv()
                total = total + rx[i].astype(F32)
            sret[i] = jnp.transpose(total).astype(BF16)

            @pl.when(y == i)
            def _():
                rret[y] = sret[i]

            @pl.when(y != i)
            def _():
                ret_copy(i).start()


    HALF = T // 2
    every = slice(0, 256 * T)

    def own_step(t, tiles):
        bwd(slice(256 * t, 256 * T), (x * T + t) * 4, 4 * tiles, True, False)

        @pl.when(jnp.logical_or(x == 1, t >= HALF))
        def _():
            for i in range(2 * t, 2 * (t + tiles)):
                sib_own(i).start()

        @pl.when(x == 0)
        def _():
            for k in range(t, t + tiles):
                send_dq(k, False)

    if T == 2:
        steps = [(0, 1), (1, 1)]
    else:
        steps = [(t, 1) for t in range(T - 2)] + [(T - 2, 2)]
    own_step(*steps[0])

    def cross_step(t):
        bwd(every, 4 * t, 4, False, False)
        for e in range(2):
            sib_cross(2 * t + e).start()


    @pl.when(x == 1)
    def _():
        cross_step(HALF)
        send_dkv(0, False)
        if T == 2:
            cross_sums(HALF)

    own_step(*steps[1])


    @pl.when(x == 1)
    def _():
        if T > 2:
            g_histories()
            cross_sums(HALF)
            cross_step(T - 1)
            send_dkv(1, False)
        else:
            g_histories()
        g_pair()

    if T > 2:
        own_step(*steps[2])


    @pl.when(x == 1)
    def _():
        if T > 2:
            cross_sums(T - 1)
        g_across()

    @pl.when(x == 0)
    def _():
        g_histories()


    @pl.when(x == 0)
    def _():
        for i in range(NY):
            dm_forward(i).wait_recv()
            take_dm(NY + i)
        for n in range(2):
            bwd(slice(256 * T + 128 * T * n, 256 * T + 128 * T * (n + 1)), 0, 4 * HALF, False, True)
            for e in range(T):
                i = n * T + e
                sxq[i] = pack_dq(NY + i).astype(BF16)
                dq_cross(i).start()
            if n == 0:
                g_pair()
        for i in range(2 * HALF):
            sib_own(i).start()


    @pl.when(x == 1)
    def _():
        for k in range(steps[-1][0], T):
            send_dkv(k, False)
        for k in range(T):
            send_dq(k, True)

    @pl.when(x == 0)
    def _():
        send_dkv(HALF, True)
        g_across()
        send_dkv(0, False)
        for t in range(1, HALF):
            send_dkv(t, False)
        for t in range(HALF + 1, T):
            send_dkv(t, True)

    def finish_dq():
        for d in near_first:
            yy = yo(d)
            copy(sretq.at[yy], rretq.at[yy], retq_s.at[yy], retq_r.at[yy], ctx=at(x, yy, c)).wait_recv()
        for j in range(NY // 2):
            cols = slice(2 * D + 128 * j, 2 * D + 128 * (j + 1))
            d_q = unpack_pair(rretq[2 * j].astype(F32), rretq[2 * j + 1].astype(F32))
            dpre[:, cols] = (d_q * slope(pre[:, cols])).astype(BF16)
        dout[...] += dot_nt(dpre[:, 2 * D : 3 * D], w_in_ref[:, 2 * D : 3 * D])


    @pl.when(x == 0)
    def _():
        finish_dq()

    g_chips()
    for d in near_first:
        yy = yo(d)
        copy(sret.at[yy], rret.at[yy], ret_s.at[yy], ret_r.at[yy], ctx=at(x, yy, c)).wait_recv()
    for j in range(NY // 2):
        even, odd = rret[2 * j].astype(F32), rret[2 * j + 1].astype(F32)
        cols = slice(3 * D + 128 * j, 3 * D + 128 * (j + 1))
        dpre[:, cols] = (jnp.where(lo, even, swap(odd)) * slope(pre[:, cols])).astype(BF16)
        cols = slice(D + 128 * j, D + 128 * (j + 1))
        dpre[:, cols] = (jnp.where(lo, swap(even), odd) * slope(pre[:, cols])).astype(BF16)
    dout[...] += dot_nt(dpre[:, D : 2 * D], w_in_ref[:, D : 2 * D]) + dot_nt(dpre[:, 3 * D :], w_in_ref[:, 3 * D :])

    @pl.when(x == 1)
    def _():
        finish_dq()

    dseq_ref[0] = dout[...].astype(BF16)

    copy(gfin.at[1 - c], gfin.at[1 - c], g4_s.at[0], g4_r.at[0], ctx=sib).wait_recv()
    d_total = jnp.concatenate([gfin[e // (H // 8), 8 * (e % (H // 8)) : 8 * (e % (H // 8)) + 8] for e in range(D // 128)], axis=1)
    nf = neg_ref[...].astype(F32)
    scale = lax.rsqrt(jnp.sum(nf * nf, axis=1, keepdims=True) + 1e-06)
    unit = nf * scale
    dneg_ref[...] = scale * (d_total - unit * jnp.sum(unit * d_total, axis=1, keepdims=True))

    for d in range(1, NY):
        kv_copy(d).wait_send()
        q_copy(d).wait_send()
        mix_copy(yo(d)).wait_send()
        dm_copy(d).wait_send()
        retq_copy(yo(d)).wait_send()
        ret_copy(yo(d)).wait_send()
    for i in range(NY):
        relay(i).wait_send()
        sib_own(i).wait_send()
    for d in range(1, NB):
        neg_copy(d).wait_send()
        gb_copy(d).wait_send()
    for d in range(1, NY):
        gc_copy(d).wait_send()
    gx_copy().wait_send()
    g1_copy().wait_send()
    g4_copy().wait_send()

    @pl.when(x == 0)
    def _():
        for i in range(NY):
            mix_cross(i).wait_send()
            dq_cross(i).wait_send()
        for i in range(E, NY):
            forward(i).wait_send()

    @pl.when(x == 1)
    def _():
        for i in range(NY):
            q_forward(i).wait_send()
            dm_forward(i).wait_send()
        for i in range(2 * HALF, NY):
            sib_cross(i).wait_send()
            cross(i).wait_send()
            cross_relay(i, c).wait_send()


def solution(mesh):
    NY = mesh.shape["ctx"] // 4
    NB = mesh.shape["batch"]
    D = HEAD * NY
    V, S = pltpu.VMEM, pltpu.SemaphoreType.DMA

    def body(*refs):
        kernel(NY, NB, *refs)

    def shards(seq_in, w_in, w_out, pos_emb, pos_ids, neg_emb, neg_ids, neg_counts):
        vm = pl.BlockSpec(memory_space=pltpu.VMEM)
        return pl.pallas_call(
            body,
            out_shape=(
                V((1, ROWS), F32),
                V((1, ROWS, D), BF16),
                V((8, D), F32),
            ),
            in_specs=[pl.BlockSpec(memory_space=pltpu.HBM)] * 8,
            out_specs=(vm, vm, vm),
            scratch_shapes=[
                V((1, ROWS, D), BF16),
                V((D, 4 * D), BF16),
                V((D, D), BF16),
                V((1, ROWS, D), BF16),
                V((1, ROWS), I32),
                V((8, D), BF16),
                pltpu.SMEM((8,), I32),
                pltpu.SMEM((8,), I32),
                S((12,)),
                V((ROWS, 4 * D), F32),
                V((NY, 128, 128), BF16),
                V((NY, 64, 128), BF16),
                V((4 * NY, 128, 128), BF16),
                V((2 * NY, 64, 128), BF16),
                V((NY * 256, 128), BF16),
                V((NY * 128, 128), F32),
                V((NY, 64, 128), BF16),
                V((NY, 64, 128), BF16),
                V((NY, 64, 128), BF16),
                V((2 * NY, 64, 128), BF16),
                V((NY * 256, 128), BF16),
                V((128, NY * 256), BF16),
                V((NY * 256, 128), F32),
                V((4 * NY, 128, 128), F32),
                V((NY, 128, 128), F32),
                V((NY, 128, 128), F32),
                V((NY, 128, 128), BF16),
                V((NY, 128, 128), BF16),
                V((NY, 64, 128), BF16),
                V((NY, 64, 128), BF16),
                V((NY, 64, 128), BF16),
                V((NY, 64, 128), BF16),
                V((NY, 128, 128), BF16),
                V((NY, 128, 128), BF16),
                V((NY, 64, 128), BF16),
                V((NY, 64, 128), BF16),
                V((ROWS, D), F32),
                V((ROWS, 4 * D), BF16),
                V((8, D + 128), F32),
                V((NB, 8, D + 128), F32),
                V((NB, D // 16, 128), BF16),
                V((NB, D // 16, 128), BF16),
                V((D // 16, 128), F32),
                V((D // 16, 128), F32),
                V((D // 32, 128), F32),
                V((D // 32, 128), F32),
                V((D // 32, 128), BF16),
                V((NY, D // 32, 128), BF16),
                V((2, D // 32, 128), F32),
            ]
            + [S((NY,))] * 32
            + [S((NB,))] * 4
            + [S((1,))] * 2
            + [S((NY,))] * 2
            + [S((1,))] * 4
            + [pltpu.SemaphoreType.REGULAR],
            compiler_params=pltpu.CompilerParams(
                collective_id=0, has_side_effects=True, vmem_limit_bytes=60 << 20
            ),
        )(seq_in, w_in, w_out, pos_emb, pos_ids, neg_emb, neg_ids, neg_counts)

    in_specs = (
        P("batch", "ctx", None), P(), P(), P("batch", "ctx", None), P("batch", "ctx"),
        P("batch", None), P("batch"), P("batch"),
    )
    out_specs = (P("batch", "ctx"), P("batch", "ctx", None), P("batch", None))
    return jax.shard_map(shards, mesh=mesh, in_specs=in_specs, out_specs=out_specs, check_vma=False)
```

```python
import jax
import jax.numpy as jnp
from jax import lax
from jax.experimental import pallas as pl
from jax.experimental.pallas import tpu as pltpu
from jax.sharding import PartitionSpec as P

MESH = pl.DeviceIdType.MESH
F32, BF16, I32 = jnp.float32, jnp.bfloat16, jnp.int32
HEAD = 64
ROWS = 128
TEMPER_INV = 20.0


def dot_nn(a, b):
    return lax.dot_general(a, b, (((1,), (0,)), ((), ())), preferred_element_type=F32)


def dot_nt(a, b):
    return lax.dot_general(a, b, (((1,), (1,)), ((), ())), preferred_element_type=F32)


def swap(v):
    return pltpu.roll(v, 64, 1)


def low(shape):
    return lax.broadcasted_iota(I32, shape, 1) < HEAD


def slope(v):
    g = jax.nn.sigmoid(v)
    return g * (1.0 + v * (1.0 - g))


def pack_rows(tile, which):
    top, bottom = tile[:64], tile[64:]
    if which == 0:
        return jnp.where(low(top.shape), top, swap(bottom))
    return jnp.where(low(top.shape), swap(top), bottom)


def unpack_pair(even, odd):
    top = jnp.where(low(even.shape), even, swap(odd))
    bottom = jnp.where(low(even.shape), swap(even), odd)
    return jnp.concatenate([top, bottom], axis=0)


def kernel(
    NY, NB,
    seq_hbm, w_in_hbm, w_out_hbm, pos_hbm, pid_hbm, neg_hbm, nid_hbm, ncnt_hbm,
    loss_ref, dseq_ref, dneg_ref,
    seq_ref, w_in_ref, w_out_ref, pos_ref, pid_ref, neg_ref, nid_ref, ncnt_ref, in_s,
    pre, skv, sq, kv, rq, qz, acc, smix, rmix, sdm, rdm, dmz, qdt, dq, dkv,
    sibo, sibx, sx, rx, sxq, rxq, smx, rmx, sret, rret, sretq, rretq, dout, dpre, negs, nega, gsend, grecv, g1, g2, g3, g3x, gsum, g4, gfin,
    kv_s, kv_r, q_s, q_r, rel_s, rel_r, xf_s, xf_r, xr_s, xr_r, mix_s, mix_r, dm_s, dm_r,
    qf_s, qf_r, mx_s, mx_r, df_s, df_r, xq_s, xq_r, so_s, so_r, sx_s, sx_r, xx_s, xx_r, ret_s, ret_r, retq_s, retq_r,
    neg_s, neg_r, gb_s, gb_r, g1_s, g1_r, gc_s, gc_r, g4_s, g4_r, gx_s, gx_r, hello,
):
    D = HEAD * NY
    T = NY // 2
    me = lax.axis_index("ctx")
    b = lax.axis_index("batch")
    c = lax.rem(me, 2)
    y = lax.rem(lax.div(me, 2), NY)
    x = lax.div(me, 2 * NY)

    def at(xx, yy, cc):
        return (xx * NY + yy) * 2 + cc

    def yo(d):
        return lax.rem(y + d, NY)

    def bo(d):
        return lax.rem(b + d, NB)

    sib = at(x, y, 1 - c)
    others = [at(x, yo(d), c) for d in range(1, NY)]
    across = at(1 - x, y, c)

    def copy(src, dst, ss, rs, ctx=None, batch=None):
        where = {"ctx": ctx} if batch is None else {"batch": batch}
        return pltpu.make_async_remote_copy(
            src_ref=src, dst_ref=dst, send_sem=ss, recv_sem=rs, device_id=where, device_id_type=MESH
        )


    loads = [
        pltpu.make_async_copy(src, dst, in_s.at[i])
        for i, (src, dst) in enumerate(
            [
                (seq_hbm, seq_ref),
                *[
                    (w_in_hbm.at[pl.ds(r * D // 4, D // 4), D:], w_in_ref.at[pl.ds(r * D // 4, D // 4), D:])
                    for r in range(4)
                ],
                (neg_hbm, neg_ref),
                (nid_hbm, nid_ref),
                (ncnt_hbm, ncnt_ref),
                (w_in_hbm.at[:, :D], w_in_ref.at[:, :D]),
                (pos_hbm, pos_ref),
                (pid_hbm, pid_ref),
                (w_out_hbm, w_out_ref),
            ]
        )
    ]
    for load in loads[:8]:
        load.start()
    barrier = pltpu.get_barrier_semaphore()
    for p in [sib, across] + others:
        pl.semaphore_signal(barrier, inc=1, device_id={"ctx": p}, device_id_type=MESH)
    for d in range(1, NB):

        @pl.when(bo(d) > b)
        def _():
            pl.semaphore_signal(barrier, inc=1, device_id={"batch": bo(d)}, device_id_type=MESH)


    for load in loads[:5]:
        load.wait()
    for load in loads[8:]:
        load.start()
    xin = seq_ref[0]
    lane = lax.broadcasted_iota(I32, (ROWS, 128), 1)
    lo = lane < HEAD

    for j in range(NY // 2):
        cols = [slice(p * D + 128 * j, p * D + 128 * (j + 1)) for p in range(4)]
        tiles = []
        for p in (1, 2, 3):
            v = dot_nn(xin, w_in_ref[:, cols[p]])
            pre[:, cols[p]] = v
            tiles.append(jax.nn.silu(v))
        vt, qt, kt = tiles
        skv[2 * j] = jnp.where(lo, kt, swap(vt)).astype(BF16)
        skv[2 * j + 1] = jnp.where(lo, swap(kt), vt).astype(BF16)
        qt = qt * 0.0625
        sq[2 * j] = pack_rows(qt, 0).astype(BF16)
        sq[2 * j + 1] = pack_rows(qt, 1).astype(BF16)

    for load in loads[5:8]:
        load.wait()
    negs[:, :D] = neg_ref[...].astype(F32)
    meta_lane = lax.broadcasted_iota(I32, (8, 128), 1)
    meta_row = lax.broadcasted_iota(I32, (8, 128), 0)
    meta = jnp.zeros((8, 128), F32)
    for i in range(8):
        here = meta_lane == b * 8 + i
        meta = meta + jnp.where(
            jnp.logical_and(here, meta_row == 0), nid_ref[i].astype(F32),
            jnp.where(jnp.logical_and(here, meta_row == 1), ncnt_ref[i].astype(F32), 0.0),
        )
    negs[:, D:] = meta

    pl.semaphore_wait(barrier, 2 + (NY - 1) + b)

    def kv_copy(d):
        h = yo(d)
        return copy(skv.at[h], kv.at[me], kv_s.at[h], kv_r.at[y], ctx=at(x, h, c))

    def q_copy(d):
        h = yo(d)
        return copy(sq.at[h], rq.at[y], q_s.at[h], q_r.at[y], ctx=at(x, h, c))

    far_first = sorted(range(1, NY), key=lambda d: -min(d, NY - d))
    @pl.when(x == 0)
    def _():
        for d in far_first:
            kv_copy(d).start()
        for d in far_first:
            q_copy(d).start()

    @pl.when(x == 1)
    def _():
        for d in far_first:
            q_copy(d).start()
        for d in far_first:
            kv_copy(d).start()

    kv[me] = skv[y]
    rq[y] = sq[y]

    def relay(yy):
        r = at(x, yy, c)
        return copy(kv.at[r], kv.at[r], rel_s.at[yy], rel_r.at[yy], ctx=sib)

    def own_relay():
        return copy(skv.at[y], kv.at[me], rel_s.at[y], rel_r.at[y], ctx=sib)

    E = NY // 2

    def forward(yy):
        r = at(0, yy, c)
        return copy(kv.at[r], kv.at[r], xf_s.at[yy], xf_r.at[yy], ctx=at(1 - x, y, c))

    def q_forward(i):
        return copy(rq.at[i], rq.at[NY + i], qf_s.at[i], qf_r.at[i], ctx=at(1 - x, y, c))

    own_relay().start()

    @pl.when(jnp.logical_and(x == 0, y >= E))
    def _():
        copy(skv.at[y], kv.at[me], xf_s.at[y], xf_r.at[y], ctx=at(1 - x, y, c)).start()

    @pl.when(x == 1)
    def _():
        copy(sq.at[y], rq.at[NY + y], qf_s.at[y], qf_r.at[y], ctx=at(1 - x, y, c)).start()

    def neg_copy(d):
        return copy(negs, nega.at[b], neg_s.at[d], neg_r.at[b], batch=bo(d))

    for d in range(1, NB):

        @pl.when(bo(d) < b)
        def _():
            pl.semaphore_signal(hello, inc=1, device_id={"batch": bo(d)}, device_id_type=MESH)
            neg_copy(d).start()

    nega[b] = negs[...]

    for load in loads[8:]:
        load.wait()
    g_pre = dot_nn(xin, w_in_ref[:, :D])
    pre[:, :D] = g_pre

    near_first = far_first[::-1]
    half = low((64, 128))

    def take_q(i):
        v = rq[i].astype(F32)
        qz[i * 128 : i * 128 + 64] = jnp.where(half, v, 0.0).astype(BF16)
        qz[i * 128 + 64 : i * 128 + 128] = jnp.where(half, swap(v), 0.0).astype(BF16)

    def take_own_q():
        for d in near_first:
            yy = yo(d)
            copy(sq.at[yy], rq.at[yy], q_s.at[yy], q_r.at[yy], ctx=at(x, yy, c)).wait_recv()

            @pl.when(x == 1)
            def _():
                q_forward(yy).start()

        for i in range(NY):
            take_q(i)

    def weighted(q, tile):
        h = dot_nt(q, tile)
        return h + h * jnp.tanh(h)

    def pack_mixed(rows, e):
        top, bottom = rows[e * 128 : e * 128 + 64], rows[e * 128 + 64 : e * 128 + 128]
        return jnp.where(half, swap(top), bottom)

    def mix_cross(i):
        return copy(smx.at[i], rmx.at[i], mx_s.at[i], mx_r.at[i], ctx=at(1 - x, y, c))

    W = 128 * T

    def meet_higher():
        @pl.when(b < NB - 1)
        def _():
            pl.semaphore_wait(hello, NB - 1 - b)

        for d in range(1, NB):

            @pl.when(bo(d) > b)
            def _():
                neg_copy(d).start()

    @pl.when(x == 1)
    def _():
        take_own_q()

    for d in near_first:
        yy = yo(d)
        copy(skv.at[yy], kv.at[at(x, yy, c)], kv_s.at[yy], kv_r.at[yy], ctx=at(x, yy, c)).wait_recv()
        relay(yy).start()

        @pl.when(jnp.logical_and(x == 0, yy >= E))
        def _():
            forward(yy).start()


    @pl.when(x == 1)
    def _():
        meet_higher()

    for d in range(NY):
        yy = yo(d)
        r = at(x, yy, 1 - c)
        copy(kv.at[r], kv.at[r], rel_s.at[yy], rel_r.at[yy], ctx=sib).wait_recv()


    @pl.when(x == 0)
    def _():
        for i in range(NY):
            q_forward(i).wait_recv()
            take_q(NY + i)
        tile = kv[:NY].reshape(128 * NY, 128)
        for n in range(2):
            w = weighted(qz[256 * T + W * n : 256 * T + W * (n + 1)], tile)
            rows = dot_nn(w.astype(BF16), tile)
            for e in range(T):
                smx[n * T + e] = pack_mixed(rows, e).astype(BF16)
                mix_cross(n * T + e).start()
        meet_higher()
        take_own_q()

    def keys_of(t):
        return kv[pl.ds(t * 4, 4)].reshape(512, 128)

    def allowed(rows, keys):
        i = lax.broadcasted_iota(I32, (rows, keys), 0)
        j = lax.broadcasted_iota(I32, (rows, keys), 1)
        return j <= i + lax.shift_right_logical(i, 7) * 128 + c * 128

    def rows_of(q, tile, diagonal):
        w = weighted(q, tile)
        if diagonal:
            last = jnp.where(allowed(256, 512), w[:, -512:], 0.0)
            w = last if w.shape[1] == 512 else jnp.concatenate([w[:, :-512], last], axis=1)
        return dot_nn(w.astype(BF16), tile)

    def mix_copy(i):
        return copy(smix.at[i], rmix.at[y], mix_s.at[i], mix_r.at[y], ctx=at(x, i, c))

    def send_mixed(i, packed):
        smix[i] = packed.astype(BF16)

        @pl.when(y == i)
        def _():
            rmix[y] = smix[i]

        @pl.when(y != i)
        def _():
            mix_copy(i).start()

    def cross_in(yy):
        r = at(0, yy, c)
        return copy(kv.at[r], kv.at[r], xf_s.at[yy], xf_r.at[yy], ctx=at(1 - x, y, c))

    def cross_relay(yy, cc):
        r = at(0, yy, cc)
        return copy(kv.at[r], kv.at[r], xr_s.at[yy], xr_r.at[yy], ctx=sib)

    for k in range(T):
        if k == T - 1:

            @pl.when(x == 1)
            def _():
                for i in range(E, NY):
                    cross_in(i).wait_recv()
                    cross_relay(i, c).start()

        tile = kv[pl.ds(x * 2 * NY, 4 * (k + 1))].reshape(512 * (k + 1), 128)
        rows = rows_of(qz[256 * k : 256 * (k + 1)], tile, True)

        @pl.when(x == 0)
        def _():
            for e in range(2):
                send_mixed(2 * k + e, pack_mixed(rows, e))

        @pl.when(x == 1)
        def _():
            acc[256 * k : 256 * (k + 1)] = rows

    @pl.when(x == 1)
    def _():
        for i in range(E, NY):
            cross_relay(i, 1 - c).wait_recv()
        tile = kv[NY : 2 * NY].reshape(128 * NY, 128)
        for n in range(2):
            piece = slice(W * n, W * (n + 1))
            acc[piece] += rows_of(qz[piece], tile, False)
        for d in far_first + [0]:
            i = yo(d)
            mix_cross(i).wait_recv()
            rows = acc[pl.ds(pl.multiple_of(i * 128, 128), 128), :]
            send_mixed(i, pack_mixed(rows, 0) + rmx[i].astype(F32))

    for d in range(1, NB):
        bb = bo(d)
        copy(negs, nega.at[bb], neg_s.at[d], neg_r.at[bb], batch=bb).wait_recv()
    NEG = 8 * NB
    neg_f = nega[:, :, :D].reshape(NEG, D)
    neg_b = (neg_f * lax.rsqrt(jnp.sum(neg_f * neg_f, axis=1, keepdims=True) + 1e-06)).astype(BF16)
    metas = nega[0, :, D:]
    for i in range(1, NB):
        metas = metas + nega[i, :, D:]
    ids = metas[0:1, :NEG]
    counts = metas[1:2, :NEG]
    log_share = jnp.log(NEG * counts / jnp.sum(counts, axis=1, keepdims=True))
    pid = jnp.transpose(jnp.broadcast_to(pid_ref[...].astype(F32), (NEG, ROWS)))
    same = pid == ids
    posf = pos_ref[0].astype(F32)
    pos_unit = posf * lax.rsqrt(jnp.sum(posf * posf, axis=1, keepdims=True) + 1e-06)
    gate_u = jax.nn.silu(pre[:, :D]).astype(BF16).astype(F32)

    for d in near_first:
        yy = yo(d)
        copy(smix.at[yy], rmix.at[yy], mix_s.at[yy], mix_r.at[yy], ctx=at(x, yy, c)).wait_recv()
    mixed = jnp.concatenate(
        [unpack_pair(rmix[2 * j].astype(F32), rmix[2 * j + 1].astype(F32)) for j in range(NY // 2)], axis=1
    )
    centred = mixed - jnp.mean(mixed, axis=1, keepdims=True)
    inv_std = lax.rsqrt(jnp.mean(centred * centred, axis=1, keepdims=True) + 1e-05)
    normed = centred * inv_std
    gated = (normed * gate_u).astype(BF16)
    outputs = xin.astype(F32) + dot_nn(gated, w_out_ref[...])
    out_scale = lax.rsqrt(jnp.sum(outputs * outputs, axis=1, keepdims=True) + 1e-06)
    user = outputs * out_scale
    user_b = user.astype(BF16)
    positive = jnp.sum(user * pos_unit, axis=1, keepdims=True) * TEMPER_INV
    logits = dot_nt(user_b, neg_b) * TEMPER_INV - log_share
    terms = jnp.where(same, 0.0, jnp.exp(logits))
    pos_exp = jnp.exp(positive)
    denom = pos_exp + jnp.sum(terms, axis=1, keepdims=True)
    loss = jnp.log(denom) - positive
    d_pos = pos_exp / denom - 1.0
    probs = terms / denom
    probs_b = probs.astype(BF16)
    d_user = (d_pos * TEMPER_INV) * pos_unit + dot_nn(probs_b, neg_b) * TEMPER_INV
    d_out = out_scale * (d_user - user * jnp.sum(user * d_user, axis=1, keepdims=True))
    d_gated = dot_nt(d_out.astype(BF16), w_out_ref[...])
    d_normed = d_gated * gate_u
    d_gate = d_gated * normed
    d_mixed = inv_std * (
        d_normed
        - jnp.mean(d_normed, axis=1, keepdims=True)
        - normed * jnp.mean(d_normed * normed, axis=1, keepdims=True)
    )
    for j in range(NY // 2):
        tile = d_mixed[:, 128 * j : 128 * (j + 1)]
        sdm[2 * j] = pack_rows(tile, 0).astype(BF16)
        sdm[2 * j + 1] = pack_rows(tile, 1).astype(BF16)

    def dm_copy(d):
        yy = yo(d)
        return copy(sdm.at[yy], rdm.at[y], dm_s.at[yy], dm_r.at[y], ctx=at(x, yy, c))

    for d in far_first:
        dm_copy(d).start()
    rdm[y] = sdm[y]

    d_pre = (d_gate * slope(pre[:, :D])).astype(BF16)
    dout[...] = d_out + dot_nt(d_pre, w_in_ref[:, :D])
    loss_ref[...] = jnp.transpose(jnp.broadcast_to(loss, (ROWS, 128)))[0:1, :]
    grad = dot_nn(jnp.transpose(probs).astype(BF16), user_b) * TEMPER_INV
    for j in range(D // 256):
        pair = [grad[:, 256 * j + 128 * e : 256 * j + 128 * (e + 1)].reshape(NB, 8, 128) for e in range(2)]
        gsend[:, 16 * j : 16 * (j + 1), :] = jnp.concatenate(pair, axis=1).astype(BF16)

    def gb_copy(d):
        bb = bo(d)
        return copy(gsend.at[bb], grecv.at[b], gb_s.at[d], gb_r.at[b], batch=bb)

    for d in range(1, NB):
        gb_copy(d).start()
    grecv[b] = gsend[b]
    dq[...] = jnp.zeros_like(dq)

    def dm_forward(i):
        return copy(rdm.at[i], rdm.at[NY + i], df_s.at[i], df_r.at[i], ctx=at(1 - x, y, c))

    def pass_dm(i):
        @pl.when(x == 1)
        def _():
            dm_forward(i).start()

    pass_dm(y)
    for d in near_first:
        yy = yo(d)
        copy(sdm.at[yy], rdm.at[yy], dm_s.at[yy], dm_r.at[yy], ctx=at(x, yy, c)).wait_recv()
        pass_dm(yy)

    def take_dm(i):
        v = rdm[i].astype(F32)
        up = jnp.concatenate([jnp.where(half, 0.0, swap(v)), jnp.where(half, 0.0, v)], axis=0)
        dmz[i * 128 : i * 128 + 128] = up.astype(BF16)
        both = up + qz[i * 128 : i * 128 + 128].astype(F32)
        qdt[:, i * 128 : i * 128 + 128] = jnp.transpose(both).astype(BF16)

    for i in range(NY):
        take_dm(i)

    def g1_copy():
        return copy(g1, g2, g1_s.at[0], g1_r.at[0], ctx=sib)

    def gx_copy():
        return copy(g3, g3x, gx_s.at[0], gx_r.at[0], ctx=across)

    def gc_copy(d):
        return copy(gsum, g4.at[y], gc_s.at[d], gc_r.at[y], ctx=at(x, yo(d), c))

    def g4_copy():
        return copy(gfin.at[c], gfin.at[c], g4_s.at[0], g4_r.at[0], ctx=sib)

    H = D // 32

    def g_histories():
        for d in range(1, NB):
            bb = bo(d)
            copy(gsend.at[bb], grecv.at[bb], gb_s.at[d], gb_r.at[bb], batch=bb).wait_recv()
        g1[...] = jnp.sum(grecv[...].astype(F32), axis=0)
        g1_copy().start()

    def g_pair():
        g1_copy().wait_recv()
        total = g1[...] + g2[...]
        g3[...] = jnp.where(c == 0, total[:H], total[H:])
        gx_copy().start()

    def g_across():
        gx_copy().wait_recv()
        gsum[...] = (g3[...] + g3x[...]).astype(BF16)
        for d in range(1, NY):
            gc_copy(d).start()
        g4[y] = gsum[...]

    def g_chips():
        for d in range(1, NY):
            copy(gsum, g4.at[yo(d)], gc_s.at[d], gc_r.at[yo(d)], ctx=sib).wait_recv()
        gfin[c] = jnp.sum(g4[...].astype(F32), axis=0)
        g4_copy().start()

    def bwd(rows, block, blocks, diagonal, more):
        tile = kv[pl.ds(block, blocks)].reshape(128 * blocks, 128)
        h = dot_nt(qz[rows], tile)
        dw = dot_nt(dmz[rows], tile)
        th = jnp.tanh(h)
        u = 1.0 + th
        w = h * u
        ds = dw * (u + w * (1.0 - th))
        if diagonal:
            lead = 64 * blocks
            ok = allowed(lead, 128 * blocks)

            def masked(v):
                first = jnp.where(ok, v[:lead], 0.0)
                return first if v.shape[0] == lead else jnp.concatenate([first, v[lead:]], axis=0)

            w, ds = masked(w), masked(ds)
        w = w.astype(BF16)
        ds = ds.astype(BF16)
        dq[rows] += dot_nn(ds, tile)
        dk = dot_nn(qdt[:64, rows], ds)
        dv = dot_nn(qdt[64:, rows], w)
        for j in range(blocks):
            one = slice(128 * j, 128 * (j + 1))
            if more:
                dkv[block + j, :64, :] += dk[:, one]
                dkv[block + j, 64:, :] += dv[:, one]
            else:
                dkv[block + j, :64, :] = dk[:, one]
                dkv[block + j, 64:, :] = dv[:, one]

    def sib_own(yy):
        return copy(dkv.at[at(x, yy, 1 - c)], sibo.at[yy], so_s.at[yy], so_r.at[yy], ctx=sib)

    def sib_cross(yy):
        return copy(dkv.at[at(0, yy, 1 - c)], sibx.at[yy], sx_s.at[yy], sx_r.at[yy], ctx=sib)

    def cross(yy):
        return copy(sx.at[yy], rx.at[yy], xx_s.at[yy], xx_r.at[yy], ctx=at(1 - x, y, c))

    def cross_sums(t):
        for e in range(2):
            i = 2 * t + e
            sib_cross(i).wait_recv()
            sx[i] = (dkv[at(0, i, c)] + sibx[i]).astype(BF16)
            cross(i).start()

    def retq_copy(i):
        return copy(sretq.at[i], rretq.at[y], retq_s.at[i], retq_r.at[y], ctx=at(x, i, c))

    def ret_copy(i):
        return copy(sret.at[i], rret.at[y], ret_s.at[i], ret_r.at[y], ctx=at(x, i, c))

    def pack_dq(i):
        top = dq[pl.ds(pl.multiple_of(i * 128, 128), 64), :] * 0.0625
        bottom = dq[pl.ds(pl.multiple_of(i * 128 + 64, 64), 64), :] * 0.0625
        return jnp.where(half, top, swap(bottom))

    def send_dq(blocks, crossed):
        for i in blocks:
            mine = pack_dq(i)
            if crossed:
                dq_cross(i).wait_recv()
                mine = mine + rxq[i].astype(F32)
            sretq[i] = mine.astype(BF16)

            @pl.when(y == i)
            def _():
                rretq[y] = sretq[i]

            @pl.when(y != i)
            def _():
                retq_copy(i).start()

    def dq_cross(i):
        return copy(sxq.at[i], rxq.at[i], xq_s.at[i], xq_r.at[i], ctx=at(1 - x, y, c))

    def send_dkv(t, crossed):
        for i in (2 * t, 2 * t + 1):
            sib_own(i).wait_recv()
            total = dkv[at(x, i, c)] + sibo[i]
            if crossed:
                cross(i).wait_recv()
                total = total + rx[i].astype(F32)
            sret[i] = jnp.transpose(total).astype(BF16)

            @pl.when(y == i)
            def _():
                rret[y] = sret[i]

            @pl.when(y != i)
            def _():
                ret_copy(i).start()


    HALF = T // 2
    every = slice(0, 256 * T)

    def own_step(t, tiles):
        bwd(slice(256 * t, 256 * T), (x * T + t) * 4, 4 * tiles, True, False)

        @pl.when(jnp.logical_or(x == 1, t >= HALF))
        def _():
            for i in range(2 * t, 2 * (t + tiles)):
                sib_own(i).start()

        @pl.when(x == 0)
        def _():
            send_dq(range(2 * t, 2 * (t + tiles)), False)

    if T == 2:
        steps = [(0, 1), (1, 1)]
    else:
        steps = [(t, 1) for t in range(T - 2)] + [(T - 2, 2)]
    own_step(*steps[0])

    def cross_step(t):
        bwd(every, 4 * t, 4, False, False)
        for e in range(2):
            sib_cross(2 * t + e).start()


    @pl.when(x == 1)
    def _():
        cross_step(HALF)

    own_step(*steps[1])


    @pl.when(x == 1)
    def _():
        cross_sums(HALF)
        send_dkv(0, False)

    if T > 2:
        own_step(*steps[2])

    g_histories()

    @pl.when(x == 1)
    def _():
        send_dkv(1, False)
        if T > 2:
            cross_step(T - 1)
        g_pair()
        for k in range(2, T):
            send_dkv(k, False)
        if T > 2:
            cross_sums(T - 1)
        g_across()
        send_dq([yo(d) for d in far_first + [0]], True)


    @pl.when(x == 0)
    def _():
        for i in range(NY):
            dm_forward(i).wait_recv()
            take_dm(NY + i)
        for n in range(2):
            bwd(slice(256 * T + 128 * T * n, 256 * T + 128 * T * (n + 1)), 0, 4 * HALF, False, True)
            for e in range(T):
                i = n * T + e
                sxq[i] = pack_dq(NY + i).astype(BF16)
                dq_cross(i).start()
            if n == 0:
                g_pair()
        for i in range(2 * HALF):
            sib_own(i).start()


    @pl.when(x == 0)
    def _():
        send_dkv(HALF, True)
        g_across()
        send_dkv(0, False)
        for t in range(1, HALF):
            send_dkv(t, False)
        for t in range(HALF + 1, T):
            send_dkv(t, True)

    def finish_dq():
        for d in near_first:
            yy = yo(d)
            copy(sretq.at[yy], rretq.at[yy], retq_s.at[yy], retq_r.at[yy], ctx=at(x, yy, c)).wait_recv()
        for j in range(NY // 2):
            cols = slice(2 * D + 128 * j, 2 * D + 128 * (j + 1))
            d_q = unpack_pair(rretq[2 * j].astype(F32), rretq[2 * j + 1].astype(F32))
            dpre[:, cols] = (d_q * slope(pre[:, cols])).astype(BF16)
        dout[...] += dot_nt(dpre[:, 2 * D : 3 * D], w_in_ref[:, 2 * D : 3 * D])


    @pl.when(x == 0)
    def _():
        finish_dq()

    g_chips()
    for d in near_first:
        yy = yo(d)
        copy(sret.at[yy], rret.at[yy], ret_s.at[yy], ret_r.at[yy], ctx=at(x, yy, c)).wait_recv()
    for j in range(NY // 2):
        even, odd = rret[2 * j].astype(F32), rret[2 * j + 1].astype(F32)
        cols = slice(3 * D + 128 * j, 3 * D + 128 * (j + 1))
        dpre[:, cols] = (jnp.where(lo, even, swap(odd)) * slope(pre[:, cols])).astype(BF16)
        cols = slice(D + 128 * j, D + 128 * (j + 1))
        dpre[:, cols] = (jnp.where(lo, swap(even), odd) * slope(pre[:, cols])).astype(BF16)
    dout[...] += dot_nt(dpre[:, D : 2 * D], w_in_ref[:, D : 2 * D]) + dot_nt(dpre[:, 3 * D :], w_in_ref[:, 3 * D :])

    @pl.when(x == 1)
    def _():
        finish_dq()

    dseq_ref[0] = dout[...].astype(BF16)

    copy(gfin.at[1 - c], gfin.at[1 - c], g4_s.at[0], g4_r.at[0], ctx=sib).wait_recv()
    d_total = jnp.concatenate([gfin[e // (H // 8), 8 * (e % (H // 8)) : 8 * (e % (H // 8)) + 8] for e in range(D // 128)], axis=1)
    nf = neg_ref[...].astype(F32)
    scale = lax.rsqrt(jnp.sum(nf * nf, axis=1, keepdims=True) + 1e-06)
    unit = nf * scale
    dneg_ref[...] = scale * (d_total - unit * jnp.sum(unit * d_total, axis=1, keepdims=True))

    for d in range(1, NY):
        kv_copy(d).wait_send()
        q_copy(d).wait_send()
        mix_copy(yo(d)).wait_send()
        dm_copy(d).wait_send()
        retq_copy(yo(d)).wait_send()
        ret_copy(yo(d)).wait_send()
    for i in range(NY):
        relay(i).wait_send()
        sib_own(i).wait_send()
    for d in range(1, NB):
        neg_copy(d).wait_send()
        gb_copy(d).wait_send()
    for d in range(1, NY):
        gc_copy(d).wait_send()
    gx_copy().wait_send()
    g1_copy().wait_send()
    g4_copy().wait_send()

    @pl.when(x == 0)
    def _():
        for i in range(NY):
            mix_cross(i).wait_send()
            dq_cross(i).wait_send()
        for i in range(E, NY):
            forward(i).wait_send()

    @pl.when(x == 1)
    def _():
        for i in range(NY):
            q_forward(i).wait_send()
            dm_forward(i).wait_send()
        for i in range(2 * HALF, NY):
            sib_cross(i).wait_send()
            cross(i).wait_send()
            cross_relay(i, c).wait_send()


def solution(mesh):
    NY = mesh.shape["ctx"] // 4
    NB = mesh.shape["batch"]
    D = HEAD * NY
    V, S = pltpu.VMEM, pltpu.SemaphoreType.DMA

    def body(*refs):
        kernel(NY, NB, *refs)

    def shards(seq_in, w_in, w_out, pos_emb, pos_ids, neg_emb, neg_ids, neg_counts):
        vm = pl.BlockSpec(memory_space=pltpu.VMEM)
        return pl.pallas_call(
            body,
            out_shape=(
                V((1, ROWS), F32),
                V((1, ROWS, D), BF16),
                V((8, D), F32),
            ),
            in_specs=[pl.BlockSpec(memory_space=pltpu.HBM)] * 8,
            out_specs=(vm, vm, vm),
            scratch_shapes=[
                V((1, ROWS, D), BF16),
                V((D, 4 * D), BF16),
                V((D, D), BF16),
                V((1, ROWS, D), BF16),
                V((1, ROWS), I32),
                V((8, D), BF16),
                pltpu.SMEM((8,), I32),
                pltpu.SMEM((8,), I32),
                S((12,)),
                V((ROWS, 4 * D), F32),
                V((NY, 128, 128), BF16),
                V((NY, 64, 128), BF16),
                V((4 * NY, 128, 128), BF16),
                V((2 * NY, 64, 128), BF16),
                V((NY * 256, 128), BF16),
                V((NY * 128, 128), F32),
                V((NY, 64, 128), BF16),
                V((NY, 64, 128), BF16),
                V((NY, 64, 128), BF16),
                V((2 * NY, 64, 128), BF16),
                V((NY * 256, 128), BF16),
                V((128, NY * 256), BF16),
                V((NY * 256, 128), F32),
                V((4 * NY, 128, 128), F32),
                V((NY, 128, 128), F32),
                V((NY, 128, 128), F32),
                V((NY, 128, 128), BF16),
                V((NY, 128, 128), BF16),
                V((NY, 64, 128), BF16),
                V((NY, 64, 128), BF16),
                V((NY, 64, 128), BF16),
                V((NY, 64, 128), BF16),
                V((NY, 128, 128), BF16),
                V((NY, 128, 128), BF16),
                V((NY, 64, 128), BF16),
                V((NY, 64, 128), BF16),
                V((ROWS, D), F32),
                V((ROWS, 4 * D), BF16),
                V((8, D + 128), F32),
                V((NB, 8, D + 128), F32),
                V((NB, D // 16, 128), BF16),
                V((NB, D // 16, 128), BF16),
                V((D // 16, 128), F32),
                V((D // 16, 128), F32),
                V((D // 32, 128), F32),
                V((D // 32, 128), F32),
                V((D // 32, 128), BF16),
                V((NY, D // 32, 128), BF16),
                V((2, D // 32, 128), F32),
            ]
            + [S((NY,))] * 32
            + [S((NB,))] * 4
            + [S((1,))] * 2
            + [S((NY,))] * 2
            + [S((1,))] * 4
            + [pltpu.SemaphoreType.REGULAR],
            compiler_params=pltpu.CompilerParams(
                collective_id=0, has_side_effects=True, vmem_limit_bytes=60 << 20
            ),
        )(seq_in, w_in, w_out, pos_emb, pos_ids, neg_emb, neg_ids, neg_counts)

    in_specs = (
        P("batch", "ctx", None), P(), P(), P("batch", "ctx", None), P("batch", "ctx"),
        P("batch", None), P("batch"), P("batch"),
    )
    out_specs = (P("batch", "ctx"), P("batch", "ctx", None), P("batch", None))
    return jax.shard_map(shards, mesh=mesh, in_specs=in_specs, out_specs=out_specs, check_vma=False)
```

```python
import jax
import jax.numpy as jnp
from jax import lax
from jax.experimental import pallas as pl
from jax.experimental.pallas import tpu as pltpu
from jax.sharding import PartitionSpec as P

MESH = pl.DeviceIdType.MESH
F32, BF16, I32 = jnp.float32, jnp.bfloat16, jnp.int32
HEAD = 64
ROWS = 128
TEMPER_INV = 20.0


def dot_nn(a, b):
    return lax.dot_general(a, b, (((1,), (0,)), ((), ())), preferred_element_type=F32)


def dot_nt(a, b):
    return lax.dot_general(a, b, (((1,), (1,)), ((), ())), preferred_element_type=F32)


def swap(v):
    return pltpu.roll(v, 64, 1)


def low(shape):
    return lax.broadcasted_iota(I32, shape, 1) < HEAD


def slope(v):
    g = jax.nn.sigmoid(v)
    return g * (1.0 + v * (1.0 - g))


def pack_rows(tile, which):
    top, bottom = tile[:64], tile[64:]
    if which == 0:
        return jnp.where(low(top.shape), top, swap(bottom))
    return jnp.where(low(top.shape), swap(top), bottom)


def unpack_pair(even, odd):
    top = jnp.where(low(even.shape), even, swap(odd))
    bottom = jnp.where(low(even.shape), swap(even), odd)
    return jnp.concatenate([top, bottom], axis=0)


def kernel(
    NY, NB,
    seq_hbm, w_in_hbm, w_out_hbm, pos_hbm, pid_hbm, neg_hbm, nid_hbm, ncnt_hbm,
    loss_ref, dseq_ref, dneg_ref,
    seq_ref, w_in_ref, w_out_ref, pos_ref, pid_ref, neg_ref, nid_ref, ncnt_ref, in_s,
    pre, skv, sq, kv, rq, qz, acc, smix, rmix, sdm, rdm, dmz, qdt, dq, dkv,
    sibo, sibx, sx, rx, sxq, rxq, smx, rmx, sret, rret, sretq, rretq, dout, dpre, negs, nega, gsend, grecv, g1, g2, g3, g3x, gsum, g4, gfin,
    kv_s, kv_r, q_s, q_r, rel_s, rel_r, xf_s, xf_r, xr_s, xr_r, mix_s, mix_r, dm_s, dm_r,
    qf_s, qf_r, mx_s, mx_r, df_s, df_r, xq_s, xq_r, so_s, so_r, sx_s, sx_r, xx_s, xx_r, ret_s, ret_r, retq_s, retq_r,
    neg_s, neg_r, gb_s, gb_r, g1_s, g1_r, gc_s, gc_r, g4_s, g4_r, gx_s, gx_r, hello,
):
    D = HEAD * NY
    T = NY // 2
    me = lax.axis_index("ctx")
    b = lax.axis_index("batch")
    c = lax.rem(me, 2)
    y = lax.rem(lax.div(me, 2), NY)
    x = lax.div(me, 2 * NY)

    def at(xx, yy, cc):
        return (xx * NY + yy) * 2 + cc

    def yo(d):
        return lax.rem(y + d, NY)

    def bo(d):
        return lax.rem(b + d, NB)

    sib = at(x, y, 1 - c)
    others = [at(x, yo(d), c) for d in range(1, NY)]
    across = at(1 - x, y, c)

    def copy(src, dst, ss, rs, ctx=None, batch=None):
        where = {"ctx": ctx} if batch is None else {"batch": batch}
        return pltpu.make_async_remote_copy(
            src_ref=src, dst_ref=dst, send_sem=ss, recv_sem=rs, device_id=where, device_id_type=MESH
        )


    loads = [
        pltpu.make_async_copy(src, dst, in_s.at[i])
        for i, (src, dst) in enumerate(
            [
                (seq_hbm, seq_ref),
                *[
                    (w_in_hbm.at[pl.ds(r * D // 4, D // 4), D:], w_in_ref.at[pl.ds(r * D // 4, D // 4), D:])
                    for r in range(4)
                ],
                (neg_hbm, neg_ref),
                (nid_hbm, nid_ref),
                (ncnt_hbm, ncnt_ref),
                (w_in_hbm.at[:, :D], w_in_ref.at[:, :D]),
                (pos_hbm, pos_ref),
                (pid_hbm, pid_ref),
                (w_out_hbm, w_out_ref),
            ]
        )
    ]
    for load in loads[:8]:
        load.start()
    barrier = pltpu.get_barrier_semaphore()
    for p in [sib, across] + others:
        pl.semaphore_signal(barrier, inc=1, device_id={"ctx": p}, device_id_type=MESH)
    for d in range(1, NB):

        @pl.when(bo(d) > b)
        def _():
            pl.semaphore_signal(barrier, inc=1, device_id={"batch": bo(d)}, device_id_type=MESH)


    for load in loads[:5]:
        load.wait()
    for load in loads[8:]:
        load.start()
    xin = seq_ref[0]
    lane = lax.broadcasted_iota(I32, (ROWS, 128), 1)
    lo = lane < HEAD

    for j in range(NY // 2):
        cols = [slice(p * D + 128 * j, p * D + 128 * (j + 1)) for p in range(4)]
        tiles = []
        for p in (1, 2, 3):
            v = dot_nn(xin, w_in_ref[:, cols[p]])
            pre[:, cols[p]] = v
            tiles.append(jax.nn.silu(v))
        vt, qt, kt = tiles
        skv[2 * j] = jnp.where(lo, kt, swap(vt)).astype(BF16)
        skv[2 * j + 1] = jnp.where(lo, swap(kt), vt).astype(BF16)
        qt = qt * 0.0625
        sq[2 * j] = pack_rows(qt, 0).astype(BF16)
        sq[2 * j + 1] = pack_rows(qt, 1).astype(BF16)

    for load in loads[5:8]:
        load.wait()
    negs[:, :D] = neg_ref[...].astype(F32)
    meta_lane = lax.broadcasted_iota(I32, (8, 128), 1)
    meta_row = lax.broadcasted_iota(I32, (8, 128), 0)
    meta = jnp.zeros((8, 128), F32)
    for i in range(8):
        here = meta_lane == b * 8 + i
        meta = meta + jnp.where(
            jnp.logical_and(here, meta_row == 0), nid_ref[i].astype(F32),
            jnp.where(jnp.logical_and(here, meta_row == 1), ncnt_ref[i].astype(F32), 0.0),
        )
    negs[:, D:] = meta

    pl.semaphore_wait(barrier, 2 + (NY - 1) + b)

    def kv_copy(d):
        h = yo(d)
        return copy(skv.at[h], kv.at[me], kv_s.at[h], kv_r.at[y], ctx=at(x, h, c))

    def q_copy(d):
        h = yo(d)
        return copy(sq.at[h], rq.at[y], q_s.at[h], q_r.at[y], ctx=at(x, h, c))

    far_first = sorted(range(1, NY), key=lambda d: -min(d, NY - d))
    @pl.when(x == 0)
    def _():
        for d in far_first:
            kv_copy(d).start()
        for d in far_first:
            q_copy(d).start()

    @pl.when(x == 1)
    def _():
        for d in far_first:
            q_copy(d).start()
        for d in far_first:
            kv_copy(d).start()

    kv[me] = skv[y]
    rq[y] = sq[y]

    def relay(yy):
        r = at(x, yy, c)
        return copy(kv.at[r], kv.at[r], rel_s.at[yy], rel_r.at[yy], ctx=sib)

    def own_relay():
        return copy(skv.at[y], kv.at[me], rel_s.at[y], rel_r.at[y], ctx=sib)

    E = NY // 2

    def forward(yy):
        r = at(0, yy, c)
        return copy(kv.at[r], kv.at[r], xf_s.at[yy], xf_r.at[yy], ctx=at(1 - x, y, c))

    def q_forward(i):
        return copy(rq.at[i], rq.at[NY + i], qf_s.at[i], qf_r.at[i], ctx=at(1 - x, y, c))

    own_relay().start()

    @pl.when(jnp.logical_and(x == 0, y >= E))
    def _():
        copy(skv.at[y], kv.at[me], xf_s.at[y], xf_r.at[y], ctx=at(1 - x, y, c)).start()

    @pl.when(x == 1)
    def _():
        copy(sq.at[y], rq.at[NY + y], qf_s.at[y], qf_r.at[y], ctx=at(1 - x, y, c)).start()

    def neg_copy(d):
        return copy(negs, nega.at[b], neg_s.at[d], neg_r.at[b], batch=bo(d))

    for d in range(1, NB):

        @pl.when(bo(d) < b)
        def _():
            pl.semaphore_signal(hello, inc=1, device_id={"batch": bo(d)}, device_id_type=MESH)
            neg_copy(d).start()

    nega[b] = negs[...]

    for load in loads[8:]:
        load.wait()
    g_pre = dot_nn(xin, w_in_ref[:, :D])
    pre[:, :D] = g_pre

    near_first = far_first[::-1]
    half = low((64, 128))

    def take_q(i):
        v = rq[i].astype(F32)
        qz[i * 128 : i * 128 + 64] = jnp.where(half, v, 0.0).astype(BF16)
        qz[i * 128 + 64 : i * 128 + 128] = jnp.where(half, swap(v), 0.0).astype(BF16)

    def take_own_q():
        for d in near_first:
            yy = yo(d)
            copy(sq.at[yy], rq.at[yy], q_s.at[yy], q_r.at[yy], ctx=at(x, yy, c)).wait_recv()

            @pl.when(x == 1)
            def _():
                q_forward(yy).start()

        for i in range(NY):
            take_q(i)

    def weighted(q, tile):
        h = dot_nt(q, tile)
        return h + h * jnp.tanh(h)

    def pack_mixed(rows, e):
        top, bottom = rows[e * 128 : e * 128 + 64], rows[e * 128 + 64 : e * 128 + 128]
        return jnp.where(half, swap(top), bottom)

    def mix_cross(i):
        return copy(smx.at[i], rmx.at[i], mx_s.at[i], mx_r.at[i], ctx=at(1 - x, y, c))

    W = 128 * T

    def meet_higher():
        @pl.when(b < NB - 1)
        def _():
            pl.semaphore_wait(hello, NB - 1 - b)

        for d in range(1, NB):

            @pl.when(bo(d) > b)
            def _():
                neg_copy(d).start()

    @pl.when(x == 1)
    def _():
        take_own_q()

    for d in near_first:
        yy = yo(d)
        copy(skv.at[yy], kv.at[at(x, yy, c)], kv_s.at[yy], kv_r.at[yy], ctx=at(x, yy, c)).wait_recv()
        relay(yy).start()

        @pl.when(jnp.logical_and(x == 0, yy >= E))
        def _():
            forward(yy).start()


    @pl.when(x == 1)
    def _():
        meet_higher()

    def relay_in(i):
        r = at(x, i, 1 - c)
        return copy(kv.at[r], kv.at[r], rel_s.at[i], rel_r.at[i], ctx=sib)

    for i in range(E):
        relay_in(i).wait_recv()


    @pl.when(x == 0)
    def _():
        tile = kv[:NY].reshape(128 * NY, 128)
        for n in range(2):
            for i in range(n * T, (n + 1) * T):
                q_forward(i).wait_recv()
                take_q(NY + i)
            w = weighted(qz[256 * T + W * n : 256 * T + W * (n + 1)], tile)
            rows = dot_nn(w.astype(BF16), tile)
            for e in range(T):
                smx[n * T + e] = pack_mixed(rows, e).astype(BF16)
                mix_cross(n * T + e).start()
        meet_higher()
        take_own_q()

    for i in range(E, NY):
        relay_in(i).wait_recv()

    def keys_of(t):
        return kv[pl.ds(t * 4, 4)].reshape(512, 128)

    def allowed(rows, keys):
        i = lax.broadcasted_iota(I32, (rows, keys), 0)
        j = lax.broadcasted_iota(I32, (rows, keys), 1)
        return j <= i + lax.shift_right_logical(i, 7) * 128 + c * 128

    def rows_of(q, tile, diagonal):
        w = weighted(q, tile)
        if diagonal:
            last = jnp.where(allowed(256, 512), w[:, -512:], 0.0)
            w = last if w.shape[1] == 512 else jnp.concatenate([w[:, :-512], last], axis=1)
        return dot_nn(w.astype(BF16), tile)

    def mix_copy(i):
        return copy(smix.at[i], rmix.at[y], mix_s.at[i], mix_r.at[y], ctx=at(x, i, c))

    def send_mixed(i, packed):
        smix[i] = packed.astype(BF16)

        @pl.when(y == i)
        def _():
            rmix[y] = smix[i]

        @pl.when(y != i)
        def _():
            mix_copy(i).start()

    def cross_in(yy):
        r = at(0, yy, c)
        return copy(kv.at[r], kv.at[r], xf_s.at[yy], xf_r.at[yy], ctx=at(1 - x, y, c))

    def cross_relay(yy, cc):
        r = at(0, yy, cc)
        return copy(kv.at[r], kv.at[r], xr_s.at[yy], xr_r.at[yy], ctx=sib)

    for k in range(T):
        if k == T - 1:

            @pl.when(x == 1)
            def _():
                for i in range(E, NY):
                    cross_in(i).wait_recv()
                    cross_relay(i, c).start()

        tile = kv[pl.ds(x * 2 * NY, 4 * (k + 1))].reshape(512 * (k + 1), 128)
        rows = rows_of(qz[256 * k : 256 * (k + 1)], tile, True)

        @pl.when(x == 0)
        def _():
            for e in range(2):
                send_mixed(2 * k + e, pack_mixed(rows, e))

        @pl.when(x == 1)
        def _():
            acc[256 * k : 256 * (k + 1)] = rows

    @pl.when(x == 1)
    def _():
        for i in range(E, NY):
            cross_relay(i, 1 - c).wait_recv()
        tile = kv[NY : 2 * NY].reshape(128 * NY, 128)
        for n in range(2):
            piece = slice(W * n, W * (n + 1))
            acc[piece] += rows_of(qz[piece], tile, False)
        for d in far_first + [0]:
            i = yo(d)
            mix_cross(i).wait_recv()
            rows = acc[pl.ds(pl.multiple_of(i * 128, 128), 128), :]
            send_mixed(i, pack_mixed(rows, 0) + rmx[i].astype(F32))

    for d in range(1, NB):
        bb = bo(d)
        copy(negs, nega.at[bb], neg_s.at[d], neg_r.at[bb], batch=bb).wait_recv()
    NEG = 8 * NB
    neg_f = nega[:, :, :D].reshape(NEG, D)
    neg_b = (neg_f * lax.rsqrt(jnp.sum(neg_f * neg_f, axis=1, keepdims=True) + 1e-06)).astype(BF16)
    metas = nega[0, :, D:]
    for i in range(1, NB):
        metas = metas + nega[i, :, D:]
    ids = metas[0:1, :NEG]
    counts = metas[1:2, :NEG]
    log_share = jnp.log(NEG * counts / jnp.sum(counts, axis=1, keepdims=True))
    pid = jnp.transpose(jnp.broadcast_to(pid_ref[...].astype(F32), (NEG, ROWS)))
    same = pid == ids
    posf = pos_ref[0].astype(F32)
    pos_unit = posf * lax.rsqrt(jnp.sum(posf * posf, axis=1, keepdims=True) + 1e-06)
    gate_u = jax.nn.silu(pre[:, :D]).astype(BF16).astype(F32)

    for d in near_first:
        yy = yo(d)
        copy(smix.at[yy], rmix.at[yy], mix_s.at[yy], mix_r.at[yy], ctx=at(x, yy, c)).wait_recv()
    mixed = jnp.concatenate(
        [unpack_pair(rmix[2 * j].astype(F32), rmix[2 * j + 1].astype(F32)) for j in range(NY // 2)], axis=1
    )
    centred = mixed - jnp.mean(mixed, axis=1, keepdims=True)
    inv_std = lax.rsqrt(jnp.mean(centred * centred, axis=1, keepdims=True) + 1e-05)
    normed = centred * inv_std
    gated = (normed * gate_u).astype(BF16)
    outputs = xin.astype(F32) + dot_nn(gated, w_out_ref[...])
    out_scale = lax.rsqrt(jnp.sum(outputs * outputs, axis=1, keepdims=True) + 1e-06)
    user = outputs * out_scale
    user_b = user.astype(BF16)
    positive = jnp.sum(user * pos_unit, axis=1, keepdims=True) * TEMPER_INV
    logits = dot_nt(user_b, neg_b) * TEMPER_INV - log_share
    terms = jnp.where(same, 0.0, jnp.exp(logits))
    pos_exp = jnp.exp(positive)
    denom = pos_exp + jnp.sum(terms, axis=1, keepdims=True)
    loss = jnp.log(denom) - positive
    d_pos = pos_exp / denom - 1.0
    probs = terms / denom
    probs_b = probs.astype(BF16)
    d_user = (d_pos * TEMPER_INV) * pos_unit + dot_nn(probs_b, neg_b) * TEMPER_INV
    d_out = out_scale * (d_user - user * jnp.sum(user * d_user, axis=1, keepdims=True))
    d_gated = dot_nt(d_out.astype(BF16), w_out_ref[...])
    d_normed = d_gated * gate_u
    d_gate = d_gated * normed
    d_mixed = inv_std * (
        d_normed
        - jnp.mean(d_normed, axis=1, keepdims=True)
        - normed * jnp.mean(d_normed * normed, axis=1, keepdims=True)
    )
    for j in range(NY // 2):
        tile = d_mixed[:, 128 * j : 128 * (j + 1)]
        sdm[2 * j] = pack_rows(tile, 0).astype(BF16)
        sdm[2 * j + 1] = pack_rows(tile, 1).astype(BF16)

    def dm_copy(d):
        yy = yo(d)
        return copy(sdm.at[yy], rdm.at[y], dm_s.at[yy], dm_r.at[y], ctx=at(x, yy, c))

    for d in far_first:
        dm_copy(d).start()
    rdm[y] = sdm[y]

    d_pre = (d_gate * slope(pre[:, :D])).astype(BF16)
    dout[...] = d_out + dot_nt(d_pre, w_in_ref[:, :D])
    loss_ref[...] = jnp.transpose(jnp.broadcast_to(loss, (ROWS, 128)))[0:1, :]
    grad = dot_nn(jnp.transpose(probs).astype(BF16), user_b) * TEMPER_INV
    for j in range(D // 256):
        pair = [grad[:, 256 * j + 128 * e : 256 * j + 128 * (e + 1)].reshape(NB, 8, 128) for e in range(2)]
        gsend[:, 16 * j : 16 * (j + 1), :] = jnp.concatenate(pair, axis=1).astype(BF16)

    def gb_copy(d):
        bb = bo(d)
        return copy(gsend.at[bb], grecv.at[b], gb_s.at[d], gb_r.at[b], batch=bb)

    for d in range(1, NB):
        gb_copy(d).start()
    grecv[b] = gsend[b]
    dq[...] = jnp.zeros_like(dq)

    def dm_forward(i):
        return copy(rdm.at[i], rdm.at[NY + i], df_s.at[i], df_r.at[i], ctx=at(1 - x, y, c))

    def pass_dm(i):
        @pl.when(x == 1)
        def _():
            dm_forward(i).start()

    pass_dm(y)
    for d in near_first:
        yy = yo(d)
        copy(sdm.at[yy], rdm.at[yy], dm_s.at[yy], dm_r.at[yy], ctx=at(x, yy, c)).wait_recv()
        pass_dm(yy)

    def take_dm(i):
        v = rdm[i].astype(F32)
        up = jnp.concatenate([jnp.where(half, 0.0, swap(v)), jnp.where(half, 0.0, v)], axis=0)
        dmz[i * 128 : i * 128 + 128] = up.astype(BF16)
        both = up + qz[i * 128 : i * 128 + 128].astype(F32)
        qdt[:, i * 128 : i * 128 + 128] = jnp.transpose(both).astype(BF16)

    for i in range(NY):
        take_dm(i)

    def g1_copy():
        return copy(g1, g2, g1_s.at[0], g1_r.at[0], ctx=sib)

    def gx_copy():
        return copy(g3, g3x, gx_s.at[0], gx_r.at[0], ctx=across)

    def gc_copy(d):
        return copy(gsum, g4.at[y], gc_s.at[d], gc_r.at[y], ctx=at(x, yo(d), c))

    def g4_copy():
        return copy(gfin.at[c], gfin.at[c], g4_s.at[0], g4_r.at[0], ctx=sib)

    H = D // 32

    def g_histories():
        for d in range(1, NB):
            bb = bo(d)
            copy(gsend.at[bb], grecv.at[bb], gb_s.at[d], gb_r.at[bb], batch=bb).wait_recv()
        g1[...] = jnp.sum(grecv[...].astype(F32), axis=0)
        g1_copy().start()

    def g_pair():
        g1_copy().wait_recv()
        total = g1[...] + g2[...]
        g3[...] = jnp.where(c == 0, total[:H], total[H:])
        gx_copy().start()

    def g_across():
        gx_copy().wait_recv()
        gsum[...] = (g3[...] + g3x[...]).astype(BF16)
        for d in range(1, NY):
            gc_copy(d).start()
        g4[y] = gsum[...]

    def g_chips():
        for d in range(1, NY):
            copy(gsum, g4.at[yo(d)], gc_s.at[d], gc_r.at[yo(d)], ctx=sib).wait_recv()
        gfin[c] = jnp.sum(g4[...].astype(F32), axis=0)
        g4_copy().start()

    def bwd(rows, block, blocks, diagonal, more):
        tile = kv[pl.ds(block, blocks)].reshape(128 * blocks, 128)
        h = dot_nt(qz[rows], tile)
        dw = dot_nt(dmz[rows], tile)
        th = jnp.tanh(h)
        u = 1.0 + th
        w = h * u
        ds = dw * (u + w * (1.0 - th))
        if diagonal:
            lead = 64 * blocks
            ok = allowed(lead, 128 * blocks)

            def masked(v):
                first = jnp.where(ok, v[:lead], 0.0)
                return first if v.shape[0] == lead else jnp.concatenate([first, v[lead:]], axis=0)

            w, ds = masked(w), masked(ds)
        w = w.astype(BF16)
        ds = ds.astype(BF16)
        dq[rows] += dot_nn(ds, tile)
        dk = dot_nn(qdt[:64, rows], ds)
        dv = dot_nn(qdt[64:, rows], w)
        for j in range(blocks):
            one = slice(128 * j, 128 * (j + 1))
            if more:
                dkv[block + j, :64, :] += dk[:, one]
                dkv[block + j, 64:, :] += dv[:, one]
            else:
                dkv[block + j, :64, :] = dk[:, one]
                dkv[block + j, 64:, :] = dv[:, one]

    def sib_own(yy):
        return copy(dkv.at[at(x, yy, 1 - c)], sibo.at[yy], so_s.at[yy], so_r.at[yy], ctx=sib)

    def sib_cross(yy):
        return copy(dkv.at[at(0, yy, 1 - c)], sibx.at[yy], sx_s.at[yy], sx_r.at[yy], ctx=sib)

    def cross(yy):
        return copy(sx.at[yy], rx.at[yy], xx_s.at[yy], xx_r.at[yy], ctx=at(1 - x, y, c))

    def cross_sums(t):
        for e in range(2):
            i = 2 * t + e
            sib_cross(i).wait_recv()
            sx[i] = (dkv[at(0, i, c)] + sibx[i]).astype(BF16)
            cross(i).start()

    def retq_copy(i):
        return copy(sretq.at[i], rretq.at[y], retq_s.at[i], retq_r.at[y], ctx=at(x, i, c))

    def ret_copy(i):
        return copy(sret.at[i], rret.at[y], ret_s.at[i], ret_r.at[y], ctx=at(x, i, c))

    def pack_dq(i):
        top = dq[pl.ds(pl.multiple_of(i * 128, 128), 64), :] * 0.0625
        bottom = dq[pl.ds(pl.multiple_of(i * 128 + 64, 64), 64), :] * 0.0625
        return jnp.where(half, top, swap(bottom))

    def send_dq(blocks, crossed):
        for i in blocks:
            mine = pack_dq(i)
            if crossed:
                dq_cross(i).wait_recv()
                mine = mine + rxq[i].astype(F32)
            sretq[i] = mine.astype(BF16)

            @pl.when(y == i)
            def _():
                rretq[y] = sretq[i]

            @pl.when(y != i)
            def _():
                retq_copy(i).start()

    def dq_cross(i):
        return copy(sxq.at[i], rxq.at[i], xq_s.at[i], xq_r.at[i], ctx=at(1 - x, y, c))

    def send_dkv(t, crossed):
        for i in (2 * t, 2 * t + 1):
            sib_own(i).wait_recv()
            total = dkv[at(x, i, c)] + sibo[i]
            if crossed:
                cross(i).wait_recv()
                total = total + rx[i].astype(F32)
            sret[i] = jnp.transpose(total).astype(BF16)

            @pl.when(y == i)
            def _():
                rret[y] = sret[i]

            @pl.when(y != i)
            def _():
                ret_copy(i).start()


    HALF = T // 2
    every = slice(0, 256 * T)

    def own_step(t, tiles):
        bwd(slice(256 * t, 256 * T), (x * T + t) * 4, 4 * tiles, True, False)

        @pl.when(jnp.logical_or(x == 1, t >= HALF))
        def _():
            for i in range(2 * t, 2 * (t + tiles)):
                sib_own(i).start()

        @pl.when(x == 0)
        def _():
            send_dq(range(2 * t, 2 * (t + tiles)), False)

    if T == 2:
        steps = [(0, 1), (1, 1)]
    else:
        steps = [(t, 1) for t in range(T - 2)] + [(T - 2, 2)]
    own_step(*steps[0])

    def cross_step(t):
        bwd(every, 4 * t, 4, False, False)
        for e in range(2):
            sib_cross(2 * t + e).start()


    @pl.when(x == 1)
    def _():
        cross_step(HALF)

    own_step(*steps[1])


    @pl.when(x == 1)
    def _():
        cross_sums(HALF)
        send_dkv(0, False)

    if T > 2:
        own_step(*steps[2])

    g_histories()

    @pl.when(x == 1)
    def _():
        send_dkv(1, False)
        if T > 2:
            cross_step(T - 1)
        g_pair()
        for k in range(2, T):
            send_dkv(k, False)
        if T > 2:
            cross_sums(T - 1)
        g_across()
        send_dq([yo(d) for d in far_first + [0]], True)


    @pl.when(x == 0)
    def _():
        for i in range(NY):
            dm_forward(i).wait_recv()
            take_dm(NY + i)
        for n in range(2):
            bwd(slice(256 * T + 128 * T * n, 256 * T + 128 * T * (n + 1)), 0, 4 * HALF, False, True)
            for e in range(T):
                i = n * T + e
                sxq[i] = pack_dq(NY + i).astype(BF16)
                dq_cross(i).start()
            if n == 0:
                g_pair()
        for i in range(2 * HALF):
            sib_own(i).start()


    @pl.when(x == 0)
    def _():
        send_dkv(HALF, True)
        g_across()
        send_dkv(0, False)
        for t in range(1, HALF):
            send_dkv(t, False)
        for t in range(HALF + 1, T):
            send_dkv(t, True)

    def finish_dq():
        for d in near_first:
            yy = yo(d)
            copy(sretq.at[yy], rretq.at[yy], retq_s.at[yy], retq_r.at[yy], ctx=at(x, yy, c)).wait_recv()
        for j in range(NY // 2):
            cols = slice(2 * D + 128 * j, 2 * D + 128 * (j + 1))
            d_q = unpack_pair(rretq[2 * j].astype(F32), rretq[2 * j + 1].astype(F32))
            dpre[:, cols] = (d_q * slope(pre[:, cols])).astype(BF16)
        dout[...] += dot_nt(dpre[:, 2 * D : 3 * D], w_in_ref[:, 2 * D : 3 * D])


    @pl.when(x == 0)
    def _():
        finish_dq()

    g_chips()
    for d in near_first:
        yy = yo(d)
        copy(sret.at[yy], rret.at[yy], ret_s.at[yy], ret_r.at[yy], ctx=at(x, yy, c)).wait_recv()
    for j in range(NY // 2):
        even, odd = rret[2 * j].astype(F32), rret[2 * j + 1].astype(F32)
        cols = slice(3 * D + 128 * j, 3 * D + 128 * (j + 1))
        dpre[:, cols] = (jnp.where(lo, even, swap(odd)) * slope(pre[:, cols])).astype(BF16)
        cols = slice(D + 128 * j, D + 128 * (j + 1))
        dpre[:, cols] = (jnp.where(lo, swap(even), odd) * slope(pre[:, cols])).astype(BF16)
    dout[...] += dot_nt(dpre[:, D : 2 * D], w_in_ref[:, D : 2 * D]) + dot_nt(dpre[:, 3 * D :], w_in_ref[:, 3 * D :])

    @pl.when(x == 1)
    def _():
        finish_dq()

    dseq_ref[0] = dout[...].astype(BF16)

    copy(gfin.at[1 - c], gfin.at[1 - c], g4_s.at[0], g4_r.at[0], ctx=sib).wait_recv()
    d_total = jnp.concatenate([gfin[e // (H // 8), 8 * (e % (H // 8)) : 8 * (e % (H // 8)) + 8] for e in range(D // 128)], axis=1)
    nf = neg_ref[...].astype(F32)
    scale = lax.rsqrt(jnp.sum(nf * nf, axis=1, keepdims=True) + 1e-06)
    unit = nf * scale
    dneg_ref[...] = scale * (d_total - unit * jnp.sum(unit * d_total, axis=1, keepdims=True))

    for d in range(1, NY):
        kv_copy(d).wait_send()
        q_copy(d).wait_send()
        mix_copy(yo(d)).wait_send()
        dm_copy(d).wait_send()
        retq_copy(yo(d)).wait_send()
        ret_copy(yo(d)).wait_send()
    for i in range(NY):
        relay(i).wait_send()
        sib_own(i).wait_send()
    for d in range(1, NB):
        neg_copy(d).wait_send()
        gb_copy(d).wait_send()
    for d in range(1, NY):
        gc_copy(d).wait_send()
    gx_copy().wait_send()
    g1_copy().wait_send()
    g4_copy().wait_send()

    @pl.when(x == 0)
    def _():
        for i in range(NY):
            mix_cross(i).wait_send()
            dq_cross(i).wait_send()
        for i in range(E, NY):
            forward(i).wait_send()

    @pl.when(x == 1)
    def _():
        for i in range(NY):
            q_forward(i).wait_send()
            dm_forward(i).wait_send()
        for i in range(2 * HALF, NY):
            sib_cross(i).wait_send()
            cross(i).wait_send()
            cross_relay(i, c).wait_send()


def solution(mesh):
    NY = mesh.shape["ctx"] // 4
    NB = mesh.shape["batch"]
    D = HEAD * NY
    V, S = pltpu.VMEM, pltpu.SemaphoreType.DMA

    def body(*refs):
        kernel(NY, NB, *refs)

    def shards(seq_in, w_in, w_out, pos_emb, pos_ids, neg_emb, neg_ids, neg_counts):
        vm = pl.BlockSpec(memory_space=pltpu.VMEM)
        return pl.pallas_call(
            body,
            out_shape=(
                V((1, ROWS), F32),
                V((1, ROWS, D), BF16),
                V((8, D), F32),
            ),
            in_specs=[pl.BlockSpec(memory_space=pltpu.HBM)] * 8,
            out_specs=(vm, vm, vm),
            scratch_shapes=[
                V((1, ROWS, D), BF16),
                V((D, 4 * D), BF16),
                V((D, D), BF16),
                V((1, ROWS, D), BF16),
                V((1, ROWS), I32),
                V((8, D), BF16),
                pltpu.SMEM((8,), I32),
                pltpu.SMEM((8,), I32),
                S((12,)),
                V((ROWS, 4 * D), F32),
                V((NY, 128, 128), BF16),
                V((NY, 64, 128), BF16),
                V((4 * NY, 128, 128), BF16),
                V((2 * NY, 64, 128), BF16),
                V((NY * 256, 128), BF16),
                V((NY * 128, 128), F32),
                V((NY, 64, 128), BF16),
                V((NY, 64, 128), BF16),
                V((NY, 64, 128), BF16),
                V((2 * NY, 64, 128), BF16),
                V((NY * 256, 128), BF16),
                V((128, NY * 256), BF16),
                V((NY * 256, 128), F32),
                V((4 * NY, 128, 128), F32),
                V((NY, 128, 128), F32),
                V((NY, 128, 128), F32),
                V((NY, 128, 128), BF16),
                V((NY, 128, 128), BF16),
                V((NY, 64, 128), BF16),
                V((NY, 64, 128), BF16),
                V((NY, 64, 128), BF16),
                V((NY, 64, 128), BF16),
                V((NY, 128, 128), BF16),
                V((NY, 128, 128), BF16),
                V((NY, 64, 128), BF16),
                V((NY, 64, 128), BF16),
                V((ROWS, D), F32),
                V((ROWS, 4 * D), BF16),
                V((8, D + 128), F32),
                V((NB, 8, D + 128), F32),
                V((NB, D // 16, 128), BF16),
                V((NB, D // 16, 128), BF16),
                V((D // 16, 128), F32),
                V((D // 16, 128), F32),
                V((D // 32, 128), F32),
                V((D // 32, 128), F32),
                V((D // 32, 128), BF16),
                V((NY, D // 32, 128), BF16),
                V((2, D // 32, 128), F32),
            ]
            + [S((NY,))] * 32
            + [S((NB,))] * 4
            + [S((1,))] * 2
            + [S((NY,))] * 2
            + [S((1,))] * 4
            + [pltpu.SemaphoreType.REGULAR],
            compiler_params=pltpu.CompilerParams(
                collective_id=0, has_side_effects=True, vmem_limit_bytes=60 << 20
            ),
        )(seq_in, w_in, w_out, pos_emb, pos_ids, neg_emb, neg_ids, neg_counts)

    in_specs = (
        P("batch", "ctx", None), P(), P(), P("batch", "ctx", None), P("batch", "ctx"),
        P("batch", None), P("batch"), P("batch"),
    )
    out_specs = (P("batch", "ctx"), P("batch", "ctx", None), P("batch", None))
    return jax.shard_map(shards, mesh=mesh, in_specs=in_specs, out_specs=out_specs, check_vma=False)
```
